128 devices in a mesh: node: 4 (over x), dev: 32 (over y, z, core).
Axes of the slice: x: 4, y: 4, z: 4, core: 2. Of those that a mesh axis runs over, the one named last changes fastest.
Arguments:
- state: float32 [72, 8, 32768], P(None, None, ('node', 'dev')), may hold values from -6 to 6
- span_owner: int32 [32768, 1], P(('node', 'dev')), may hold values from 0 to 127; in each aligned block of 256 rows (0 to 255, 256 to 511, ...) at most 4 rows name the same one
- regime: int32 [32768], P(('node', 'dev')), may hold values from 0 to 2
- moments: float32 [72, 8, 65536], P(None, None, ('node', 'dev')), may hold values from -6 to 6
- remap_weights: float32 [512, 128, 128], P(('node', 'dev')), may hold values from -0.5 to 0.5
- remap_rows: int32 [512], P(('node', 'dev')), may hold values from 0 to 511
- remap_cols: int32 [512], P(('node', 'dev')), may hold values from 0 to 1
Outputs:
- tendencies: float32 [72, 8, 32768], P(None, None, ('node', 'dev'))
- moments_out: float32 [72, 8, 65536], P(None, None, ('node', 'dev'))
- ocean_flux: float32 [512, 4, 128], P(('node', 'dev'))
The draws below stay inside these ranges and needn't reach their ends.
Inputs may be any that keep to these rules, and one draw needn't show every extreme that they name: `span_owner`: among the 256 columns of one device no owner is named more than 4 times; some device names some owner exactly 4 times.
All inputs are finite; a program needn't handle non-finite values.
Results may differ from the reference program's by a relative error of at most 0.00014.
Values sent between devices are 32-bit elements; how exact they have to be, the bound alone decides.
No kernel may reach another device: no remote copies, remote signals or barrier semaphores. Data moves between devices by JAX's collectives and lax.ppermute only.
A program may use at most 64 MiB of HBM per device.

```python
import math
import jax
import jax.numpy as jnp
import numpy as np
from jax import lax

LEV = 72
FLD = 8
MOM = 8
TILE = 128
MICRO_SUB = 2
TURB_ITERS = 3
COL_DEV = 256
PEERS = 128
COLS = 32768
CAP = 4
SLOTS = 65536
ABLK = 2
NBLK_DEV = 4
NBLK = 512
OCN_BLOCKS = 512


def draw_moments(key, part):
    key_base = jax.random.fold_in(key, 11)
    key_offset = jax.random.fold_in(key, 23)
    key_noise = jax.random.fold_in(key, 37)
    base = jnp.clip(jax.random.normal(key_base, (LEV, MOM, SLOTS), jnp.float32), -6.0, 6.0)
    offset = jax.random.uniform(key_offset, (SLOTS,), jnp.float32, -2.5, 2.5)
    noise = 0.7 * jnp.clip(jax.random.normal(key_noise, (LEV, SLOTS), jnp.float32), -2.5, 2.5)
    first = offset[None, :] + noise
    return jnp.concatenate([first[:, None, :], base[:, 1:, :]], axis=1).astype(jnp.float32)


def touch_ends(values, rng, least, largest):
    extent = values.shape
    index_at = [jax.random.randint(jax.random.fold_in(rng, axis), (), 0, extent[axis]) for axis in range(len(extent))]
    values = values.at[tuple(index_at)].set(least)
    longest = extent.index(max(extent))
    index_at[longest] = (index_at[longest] + 1) % extent[longest]
    return values.at[tuple(index_at)].set(largest)


def levels(rng, dims, shards, smallest, top_value):
    level = 1.0
    for axis_at, shards_of in shards:
        draws = jax.random.uniform(jax.random.fold_in(jax.random.fold_in(rng, 6), axis_at), (shards_of,), jnp.float32, smallest / len(shards), top_value / len(shards))
        level = level * jnp.repeat(jnp.exp(draws), dims[axis_at] // shards_of).reshape((-1,) + (1,) * (len(dims) - 1 - axis_at))
    return level


def deal_out(own_key, own, number, rows, number_of, top, most, skew):
    ranking = jax.random.permutation(own_key, number_of)
    crowded, usual = shares(number_of, rows * top, most, skew, True), shares(number_of, rows * top, most, skew, False)
    places = jnp.arange(number_of)

    def named(lengths, rotation):
        used = int((lengths > 0).sum())
        fixed = max(1, used // 4)
        passed = fixed + (places - fixed + rotation * (used - fixed)) % max(1, number_of - fixed)
        return jnp.zeros((number_of,), jnp.int32).at[ranking[jnp.where(places < fixed, places, passed)]].set(jnp.asarray(lengths, jnp.int32))

    lengths = jnp.where(number % 4 == 0, named(crowded, number // 4), named(usual, number - number // 4 - 1))
    mixed = jax.random.permutation(jax.random.fold_in(own, 3), number_of)
    giver, sink = mixed[0:number_of // 2 * 2:2], mixed[1:number_of // 2 * 2:2]
    room = jnp.minimum(lengths[giver] - 1, most - lengths[sink]) // 2
    room = jnp.where((giver == ranking[0]) | (sink == ranking[0]) | (lengths[sink] == 0), 0, jnp.maximum(room, 0))
    passed = jax.random.randint(jax.random.fold_in(own, 4), (number_of // 2,), 0, 1 << 20) % (room + 1)
    lengths = lengths.at[giver].add(-passed).at[sink].add(passed)
    items = jnp.searchsorted(jnp.cumsum(lengths), jnp.arange(rows * top), side="right").astype(jnp.int32)
    listing = items.reshape(top, rows).T
    listing = listing[jax.random.permutation(jax.random.fold_in(own, 1), rows)]
    rotation = jax.random.randint(jax.random.fold_in(own, 2), (rows, 1), 0, top)
    return jnp.take_along_axis(listing, (jnp.arange(top)[None, :] + rotation) % top, axis=1)


def shares(number_of, total, bound, skew, full):
    portions = [(1 << 20) // math.isqrt(standing ** skew) + 1 for standing in range(1, number_of + 1)]
    largest = bound if full else min(bound, max(-(-total // number_of), total * portions[0] // sum(portions)))
    least = 1 if total - largest >= number_of - 1 else 0
    counts, spare = [largest] + [least] * (number_of - 1), total - largest - least * (number_of - 1)
    while spare > 0:
        free = [i for i in range(1, number_of) if counts[i] < largest] or [i for i in range(1, number_of) if counts[i] < bound]
        pool, remaining = sum([portions[i] for i in free]), spare
        for i in free:
            more = min(bound - counts[i], max(1, remaining * portions[i] // pool), spare)
            counts[i] = counts[i] + more
            spare = spare - more
    return np.array(counts)


def gaussian(key, dims, spread, most, split=(), held_as=jnp.bfloat16):
    level = levels(key, dims, split, -0.22, 0.18) if split else 1.0
    drawn = jax.random.normal(key, dims, jnp.float32) * spread * level
    return jnp.minimum(jnp.maximum(drawn, -most), most).astype(held_as)


def setup_inputs(seed: int = 0) -> dict:
    arg_keys = jax.random.split(jax.random.key(seed), 8)
    state = gaussian(arg_keys[0], (LEV, FLD, COLS), 1.0, 6.0, ((2, 128),), jnp.float32)
    span_owner_keys = jax.random.split(jax.random.fold_in(arg_keys[1], 1), COLS // COL_DEV)
    span_owner_turns = jax.random.permutation(jax.random.fold_in(arg_keys[1], 3), COLS // COL_DEV)
    span_owner = jax.vmap(lambda own, number: deal_out(jax.random.fold_in(arg_keys[1], 2), own, number, COL_DEV, PEERS, 1, CAP, 1))(span_owner_keys, span_owner_turns).reshape((COLS, 1))
    regime = touch_ends(jax.random.randint(arg_keys[2], (COLS,), 0, 3), jax.random.fold_in(arg_keys[2], 1), 0, 2).astype(jnp.int32)
    moments = draw_moments(jax.random.fold_in(arg_keys[7], 71), 0)
    remap_weights = gaussian(arg_keys[4], (NBLK, TILE, TILE), TILE ** -0.5, 0.5, ((0, 128),), jnp.float32)
    remap_rows = touch_ends(jax.random.randint(arg_keys[5], (NBLK,), 0, OCN_BLOCKS), jax.random.fold_in(arg_keys[5], 1), 0, OCN_BLOCKS - 1).astype(jnp.int32)
    remap_cols = touch_ends(jax.random.randint(arg_keys[6], (NBLK,), 0, ABLK), jax.random.fold_in(arg_keys[6], 1), 0, ABLK - 1).astype(jnp.int32)
    return {"state": state, "span_owner": span_owner, "regime": regime, "moments": moments, "remap_weights": remap_weights, "remap_rows": remap_rows, "remap_cols": remap_cols}


def level_grad(field):
    padded = jnp.concatenate([field[:1], field, field[-1:]], axis=0)
    return padded[:-2] - padded[2:]

def microphysics(current, column_moments, regime_real):
    temper = current[:, 0]
    vapour = jax.nn.softplus(current[:, 1])
    liquid = jax.nn.softplus(current[:, 2])
    rain_q = jax.nn.softplus(current[:, 3])
    ice_q = jax.nn.softplus(current[:, 4])
    satur = 0.6 * jnp.exp(0.5 * jnp.tanh(0.5 * temper))
    cloudy = 0.5 + jax.nn.sigmoid(column_moments[:, 2] + vapour - satur)
    conden = 0.4 * jnp.tanh(vapour - satur) * cloudy
    autoconv = 0.3 * liquid * liquid / (1.0 + liquid)
    evapor = 0.1 * rain_q * jax.nn.sigmoid(satur - vapour)
    freeze = 0.3 * liquid * jax.nn.sigmoid(-temper)
    melting = 0.2 * ice_q * jax.nn.sigmoid(temper)
    deposit = 0.35 * jnp.tanh(vapour - 0.8 * satur) * cloudy
    aggreg = 0.25 * ice_q * ice_q / (1.0 + ice_q)
    is_warm = (regime_real == 0.0).astype(current.dtype)[None, :]
    is_mixed = (regime_real == 1.0).astype(current.dtype)[None, :]
    is_icy = (regime_real == 2.0).astype(current.dtype)[None, :]
    falling = 0.5 * rain_q
    from_above = jnp.concatenate([jnp.zeros_like(falling[:1]), falling[:-1]], axis=0)
    d_temp = is_warm * (0.8 * (conden - evapor)) + is_mixed * (0.8 * conden + 0.5 * (freeze - melting)) + is_icy * (deposit + 0.5 * freeze)
    d_vapour = is_warm * (evapor - conden) - is_mixed * conden - is_icy * deposit
    d_liquid = is_warm * (conden - autoconv) + is_mixed * (conden - freeze - autoconv) - is_icy * freeze
    d_rain = is_warm * (autoconv - evapor) + is_mixed * (autoconv + melting) + is_icy * aggreg + from_above - falling
    d_ice = is_mixed * (freeze - melting) + is_icy * (deposit + freeze - aggreg)
    return jnp.stack([temper + 0.5 * d_temp, current[:, 1] + 0.5 * d_vapour, current[:, 2] + 0.5 * d_liquid, current[:, 3] + 0.5 * d_rain, current[:, 4] + 0.5 * d_ice, current[:, 5], current[:, 6], current[:, 7]], axis=1)

def diffusivity(mixed_state, column_moments):
    diff_u = mixed_state[:-1, 5] - mixed_state[1:, 5]
    diff_v = mixed_state[:-1, 6] - mixed_state[1:, 6]
    diff_t = mixed_state[:-1, 0] - mixed_state[1:, 0]
    shear_sq = diff_u * diff_u + diff_v * diff_v
    energy = 0.5 + 60.0 * jax.nn.sigmoid(2.0 * (column_moments[:-1, 0] + column_moments[1:, 0]))
    return (0.3 + 1.5 * shear_sq / (1.0 + shear_sq) * jax.nn.sigmoid(-2.0 * diff_t)) * energy

def implicit(kappa_int, right_side):
    zero_row = jnp.zeros_like(kappa_int[:1])
    below_k = jnp.concatenate([zero_row, kappa_int], axis=0)
    above_k = jnp.concatenate([kappa_int, zero_row], axis=0)

    def forward(carry, inputs):
        c_prev, d_prev = carry
        k_low, k_high, rhs_row = inputs
        denominator = 1.0 + k_low + k_high + k_low * c_prev
        c_now = -k_high / denominator
        d_now = (rhs_row + k_low[None, :] * d_prev) / denominator[None, :]
        return ((c_now, d_now), (c_now, d_now))
    start_carry = (jnp.zeros_like(kappa_int[0]), jnp.zeros_like(right_side[0]))
    _, (c_rows, d_rows) = lax.scan(forward, start_carry, (below_k, above_k, right_side))

    def backward(y_next, inputs):
        c_now, d_now = inputs
        y_now = d_now - c_now[None, :] * y_next
        return (y_now, y_now)
    _, solved = lax.scan(backward, jnp.zeros_like(right_side[0]), (c_rows, d_rows), reverse=True)
    return solved

def turbulence(after_micro, column_moments):
    right_side = jnp.concatenate([after_micro[:, 0:2], after_micro[:, 5:8]], axis=1)
    mixed_state = after_micro
    for iteration in range(TURB_ITERS):
        kappa_int = diffusivity(mixed_state, column_moments)
        solved = implicit(kappa_int, right_side)
        mixed_state = jnp.concatenate([solved[:, 0:2], after_micro[:, 2:5], solved[:, 2:5]], axis=1)
    return mixed_state

def update_moments(mixed_state, column_moments):
    grad_u = level_grad(mixed_state[:, 5])
    grad_v = level_grad(mixed_state[:, 6])
    grad_t = level_grad(mixed_state[:, 0])
    grad_q = level_grad(mixed_state[:, 1])
    production = [grad_u * grad_u + grad_v * grad_v, grad_t * grad_t, grad_q * grad_q, grad_t * grad_q, grad_u * grad_t, grad_v * grad_t, grad_u * grad_q, grad_u * grad_v]
    updated = [column_moments[:, index] + 0.5 * (jnp.tanh(production[index]) - (0.3 + 0.1 * index) * column_moments[:, index]) for index in range(8)]
    return jnp.stack(updated, axis=1)

def physics(columns, column_moments, regime_real):
    after_micro = columns
    for substep in range(MICRO_SUB):
        after_micro = microphysics(after_micro, column_moments, regime_real)
    mixed_state = turbulence(after_micro, column_moments)
    return (mixed_state - columns, update_moments(mixed_state, column_moments))

def surface(state, tendencies):
    bottom = state[-1] + tendencies[-1]
    wind_speed = jnp.sqrt(1.0 + bottom[5] * bottom[5] + bottom[6] * bottom[6])
    return jnp.stack([-0.5 * wind_speed * bottom[5], -0.5 * wind_speed * bottom[6], 0.5 * jax.nn.softplus(bottom[3]), -0.3 * wind_speed * bottom[0]], axis=0)

def reference(state, span_owner, regime, moments, remap_weights, remap_rows, remap_cols):
    owners_all = span_owner[:, 0]
    regime_all = regime.astype(jnp.float32)

    def device_block(index, carry):
        tend_all, moments_new = carry
        device = jnp.asarray(index).astype(jnp.int32)
        begin = device * COL_DEV
        columns = lax.dynamic_slice_in_dim(state, begin, COL_DEV, 2)
        owner_ids = lax.dynamic_slice_in_dim(owners_all, begin, COL_DEV, 0).astype(jnp.int32)
        kinds = lax.dynamic_slice_in_dim(regime_all, begin, COL_DEV, 0)
        one_hot = (owner_ids[:, None] == jnp.arange(PEERS, dtype=jnp.int32)[None, :]).astype(jnp.int32)
        rank_in = lax.optimization_barrier(jnp.sum((jnp.cumsum(one_hot, axis=0) - one_hot) * one_hot, axis=1)).astype(jnp.int32)
        global_slot = owner_ids * (CAP * PEERS) + rank_in * PEERS + device
        column_moments = jnp.take(moments, global_slot, axis=2)
        tend_block, new_block = physics(columns, column_moments, kinds)
        tend_all = lax.dynamic_update_slice_in_dim(tend_all, tend_block, begin, 2)
        moments_new = moments_new.at[:, :, global_slot].set(new_block)
        return (tend_all, moments_new)
    tendencies, moments_out = lax.fori_loop(0, PEERS, device_block, (jnp.zeros_like(state), moments))
    fluxes = surface(state, tendencies)
    flux_blocks = fluxes.reshape(4, COLS // TILE, TILE)
    block_ids = jnp.arange(NBLK, dtype=jnp.int32) // NBLK_DEV * ABLK + remap_cols.astype(jnp.int32)
    gathered = flux_blocks[:, block_ids]
    products = jnp.einsum('fbt,bts->bfs', gathered, remap_weights, precision=lax.Precision.HIGHEST)
    ocean_flux = jnp.zeros((OCN_BLOCKS, 4, TILE), dtype=remap_weights.dtype).at[remap_rows].add(products)
    return (tendencies, moments_out, ocean_flux)
```

```python
import jax
import jax.numpy as jnp
from jax import lax
from jax.experimental import pallas as pl
from jax.experimental.pallas import tpu as pltpu
from jax.sharding import PartitionSpec as P

LEV = 72
FLD = 8
PEERS = 128
LANES = 128
CAP = 4
COL = 256
SLOTS = CAP * PEERS
DOWN = 2
UP = 4
ROWS1 = 5
META = CAP * DOWN * LEV
ROWS_UP = CAP * UP * LEV // LANES
OCN_ROWS = 8
ROWS2 = ROWS_UP + OCN_ROWS
HALF = LEV // 2
PAD_ROWS = LEV * FLD + FLD
f32 = jnp.float32
bf16 = jnp.bfloat16


def iota(shape, axis):
    return lax.broadcasted_iota(jnp.int32, shape, axis)


def split3(x):
    hi = x.astype(bf16)
    rest = x - hi.astype(f32)
    mid = rest.astype(bf16)
    low = (rest - mid.astype(f32)).astype(bf16)
    return hi, mid, low


def columns_down(owner_row):
    real = owner_row.astype(f32)
    parts = [
        jnp.broadcast_to(real[:, h * LANES : (h + 1) * LANES], (LANES, LANES)).T
        for h in range(COL // LANES)
    ]
    return jnp.concatenate(parts, axis=0)


def pack_kernel(rows_ref, owner_ref, *refs):
    mom_refs, out_ref, block_ref = refs[:CAP], refs[CAP], refs[CAP + 1]
    owner_down = columns_down(owner_ref[...])
    peer = iota((COL, LANES), 1).astype(f32)
    count = jnp.sum((owner_down == peer).astype(f32), axis=0, keepdims=True)
    for slot in range(CAP):
        for at, moment in enumerate((0, 2)):
            first = (slot * DOWN + at) * LEV
            block_ref[first : first + LEV, :] = mom_refs[slot][pl.ds(moment, LEV, stride=FLD), :]
    tail = ROWS1 * LANES - META
    which = iota((tail, LANES), 0)
    meta = jnp.where(which == 4, jnp.broadcast_to(count, (tail, LANES)), 0.0)
    for n in range(4):
        meta = jnp.where(which == n, rows_ref[n].astype(f32), meta)
    block_ref[META:, :] = meta
    for t in range(ROWS1):
        out_ref[pl.ds(t, PEERS, stride=ROWS1), :] = block_ref[t * LANES : (t + 1) * LANES, :].T


def softplus(x):
    return jnp.maximum(x, 0.0) + jnp.log(1.0 + jnp.exp(-jnp.abs(x)))


def micro_step(x, m2, warm, mixed, above, top):
    temper, vap, liq, rain, ice = x
    vapour = softplus(vap)
    liquid = softplus(liq)
    rain_q = softplus(rain)
    ice_q = softplus(ice)
    half_t = jnp.tanh(0.5 * temper)
    satur = 0.6 * jnp.exp(0.5 * half_t)
    excess = vapour - satur
    cloudy = 1.0 + 0.5 * jnp.tanh(0.5 * (m2 + excess))
    conden = 0.4 * jnp.tanh(excess) * cloudy
    autoconv = 0.3 * liquid * liquid / (1.0 + liquid)
    evapor = 0.1 * rain_q * (0.5 - 0.5 * jnp.tanh(0.5 * excess))
    freeze = 0.3 * liquid * (0.5 - 0.5 * half_t)
    melting = 0.2 * ice_q * (0.5 + 0.5 * half_t)
    deposit = 0.35 * jnp.tanh(vapour - 0.8 * satur) * cloudy
    aggreg = 0.25 * ice_q * ice_q / (1.0 + ice_q)
    falling = 0.5 * rain_q
    rolled = pltpu.roll(falling, 1, 0)
    from_above = jnp.where(top, above, rolled)

    def pick(a, b, c):
        return jnp.where(warm, a, jnp.where(mixed, b, c))

    swap = freeze - melting
    d_temp = pick(0.8 * (conden - evapor), 0.8 * conden + 0.5 * swap, deposit + 0.5 * freeze)
    d_vap = pick(evapor - conden, -conden, -deposit)
    d_liq = pick(conden - autoconv, conden - freeze - autoconv, -freeze)
    d_rain = pick(autoconv - evapor, autoconv + melting, aggreg) + from_above - falling
    d_ice = pick(jnp.zeros_like(swap), swap, deposit + freeze - aggreg)
    new = (
        temper + 0.5 * d_temp,
        vap + 0.5 * d_vap,
        liq + 0.5 * d_liq,
        rain + 0.5 * d_rain,
        ice + 0.5 * d_ice,
    )
    return new, rolled


def solve(a_ref, k_ref, y_ref, g_ref):
    halves = range(COL // LANES)

    def kap(h, level):
        row = k_ref[level : level + 1, h * LANES : (h + 1) * LANES]
        return jnp.broadcast_to(row, (FLD, LANES))

    def rows(h, level):
        first = h * PAD_ROWS + level * FLD
        return slice(first, first + FLD)

    state = {}
    for step in range(HALF):
        for h in halves:
            for chain in range(2):
                k = LEV - 1 - step if chain else step
                k_new = kap(h, k - 1 if chain else k)
                a = a_ref[rows(h, k), :]
                if step == 0:
                    r = 1.0 / (1.0 + k_new)
                    d = a * r
                else:
                    k_old, g, d = state[h, chain]
                    r = 1.0 / (1.0 + k_new + k_old * (1.0 - g))
                    d = (a + k_old * d) * r
                g = k_new * r
                g_ref[rows(h, k), :] = g
                y_ref[rows(h, k), :] = d
                state[h, chain] = (k_new, g, d)
    z = {}
    for h in halves:
        (_, g_up, d_up), (_, g_dn, d_dn) = state[h, 0], state[h, 1]
        z[h, 0] = (d_up + g_up * d_dn) / (1.0 - g_up * g_dn)
        z[h, 1] = d_dn + g_dn * z[h, 0]
        y_ref[rows(h, HALF - 1), :] = z[h, 0]
        y_ref[rows(h, HALF), :] = z[h, 1]
    for step in range(1, HALF):
        for h in halves:
            for chain in range(2):
                k = HALF + step if chain else HALF - 1 - step
                z[h, chain] = y_ref[rows(h, k), :] + g_ref[rows(h, k), :] * z[h, chain]
                y_ref[rows(h, k), :] = z[h, chain]


def physics_kernel(
    cols_ref,
    owner_ref,
    regime_ref,
    got_ref,
    state_0,
    state_1,
    weight_ref,
    tend_out,
    out_ref,
    meta_ref,
    block_ref,
    hot_ref,
    mom_ref,
    a_ref,
    y_ref,
    g_ref,
    k_ref,
    e_ref,
    tend_ref,
    tend_sem,
):
    states = (state_0, state_1)
    owner_row = owner_ref[...]
    owner_down = columns_down(owner_row)
    owner_real = owner_row.astype(f32)
    before = jnp.zeros((1, COL), f32)
    for h in range(COL // LANES):
        same = (
            jnp.concatenate([owner_down[h * LANES : (h + 1) * LANES, :]] * 2, axis=1) == owner_real
        )
        earlier = iota((LANES, COL), 0) + h * LANES < iota((LANES, COL), 1)
        before = before + jnp.sum((same & earlier).astype(f32), axis=0, keepdims=True)
    slot = owner_row + PEERS * before.astype(jnp.int32)
    for p in range(CAP):
        hot_ref[p * PEERS : (p + 1) * PEERS, :] = (
            iota((PEERS, COL), 0) + p * PEERS == slot
        ).astype(bf16)

    for t in range(ROWS1):
        block_ref[t * LANES : (t + 1) * LANES, :] = got_ref[pl.ds(t, PEERS, stride=ROWS1), :].T
    meta_ref[...] = block_ref[META : META + 8, :]
    slotted = jnp.concatenate(
        [block_ref[p * DOWN * LEV : (p + 1) * DOWN * LEV, :] for p in range(CAP)], axis=1
    )
    total = None
    for part in split3(slotted):
        got = jnp.dot(part, hot_ref[...], preferred_element_type=f32)
        total = got if total is None else total + got
    mom_ref[0 : DOWN * LEV, :] = total

    top = iota((8, LANES), 0) == 0
    for h in range(COL // LANES):
        lanes = slice(h * LANES, (h + 1) * LANES)
        kind = regime_ref[:, lanes]
        warm = jnp.broadcast_to(kind, (8, LANES)) == 0
        mixed = jnp.broadcast_to(kind, (8, LANES)) == 1
        above = [jnp.zeros((8, LANES), f32)] * 2
        base = h * PAD_ROWS
        for i in range(LEV // 8):
            x = tuple(states[h][pl.ds(i * 64 + f, 8, stride=FLD), :] for f in range(FLD))
            x, rest = x[:5], x[5:]
            m2 = mom_ref[LEV + i * 8 : LEV + i * 8 + 8, lanes]
            for sub in range(2):
                x, above[sub] = micro_step(x, m2, warm, mixed, above[sub], top)
            for f, value in enumerate(x + rest):
                a_ref[pl.ds(base + i * 64 + f, 8, stride=FLD), :] = value
        for ref in (a_ref, y_ref):
            ref[base + LEV * FLD : base + PAD_ROWS, :] = jnp.zeros((FLD, LANES), f32)
    last = iota((8, COL), 0) == 7
    for i in range(LEV // 8):
        m0 = mom_ref[i * 8 : i * 8 + 8, :]
        m0_next = mom_ref[i * 8 + 1 : i * 8 + 9, :]
        energy = 30.5 + 30.0 * jnp.tanh(m0 + m0_next)
        if i == LEV // 8 - 1:
            energy = jnp.where(last, 0.0, energy)
        e_ref[i * 8 : i * 8 + 8, :] = energy
    for turn in range(3):
        src = a_ref if turn == 0 else y_ref
        for h in range(COL // LANES):
            lanes = slice(h * LANES, (h + 1) * LANES)
            for i in range(LEV // 8):

                def drop(f):
                    first = h * PAD_ROWS + i * 64 + f
                    return (
                        src[pl.ds(first, 8, stride=FLD), :]
                        - src[pl.ds(first + FLD, 8, stride=FLD), :]
                    )

                du, dv, dt = drop(5), drop(6), drop(0)
                shear = du * du + dv * dv
                mixing = 0.3 + 1.5 * shear / (1.0 + shear) * (0.5 - 0.5 * jnp.tanh(dt))
                k_ref[i * 8 : i * 8 + 8, lanes] = mixing * e_ref[i * 8 : i * 8 + 8, lanes]
        solve(a_ref, k_ref, y_ref, g_ref)

    field = iota((FLD, LANES), 0)
    kept = (field >= 2) & (field <= 4)
    copies = []
    for h in range(COL // LANES):
        for k in range(LEV):
            rows = slice(k * FLD, (k + 1) * FLD)
            at = slice(h * PAD_ROWS + k * FLD, h * PAD_ROWS + (k + 1) * FLD)
            mixed_state = jnp.where(kept, a_ref[at, :], y_ref[at, :])
            tend_ref[h, rows, :] = mixed_state - states[h][rows, :]
        copies.append(
            pltpu.make_async_copy(
                tend_ref.at[h], tend_out.at[:, pl.ds(h * LANES, LANES)], tend_sem.at[h]
            )
        )
        copies[-1].start()

    fields = jnp.concatenate(
        [
            jnp.concatenate(
                [y_ref[pl.ds(h * PAD_ROWS + f, LEV, stride=FLD), :] for f in (0, 1, 5, 6)], axis=0
            )
            for h in range(COL // LANES)
        ],
        axis=1,
    )
    total = None
    for part in split3(fields):
        got = lax.dot_general(
            part, hot_ref[...], (((1,), (1,)), ((), ())), preferred_element_type=f32
        )
        total = got if total is None else total + got
    for p in range(CAP):
        block_ref[p * UP * LEV : (p + 1) * UP * LEV, :] = total[:, p * PEERS : (p + 1) * PEERS]
    for t in range(ROWS_UP):
        out_ref[pl.ds(t, PEERS, stride=ROWS2), :] = block_ref[t * LANES : (t + 1) * LANES, :].T

    bottom = slice((LEV - 1) * FLD, LEV * FLD)
    b = jnp.concatenate(
        [states[h][bottom, :] + tend_ref[h, bottom, :] for h in range(COL // LANES)], axis=1
    )
    b0, b3, b5, b6 = (b[f : f + 1, :] for f in (0, 3, 5, 6))
    wind = jnp.sqrt(1.0 + b5 * b5 + b6 * b6)
    flux = jnp.concatenate(
        [
            -0.5 * wind * b5,
            -0.5 * wind * b6,
            0.5 * softplus(b3),
            -0.3 * wind * b0,
            jnp.zeros((4, COL), f32),
        ],
        axis=0,
    )
    odd = iota((PEERS, LANES), 0) % 2 == 1
    for n in range(4):
        used = jnp.where(cols_ref[n] == 0, flux[:, :LANES], flux[:, LANES:])
        product = jnp.dot(
            used, weight_ref[n], precision=lax.Precision.HIGHEST, preferred_element_type=f32
        )
        for e in range(2):
            out_ref[pl.ds(ROWS_UP + 2 * n + e, PEERS, stride=ROWS2), :] = jnp.where(
                odd, product[2 + e : 3 + e, :], product[e : e + 1, :]
            )
    for copy in copies:
        copy.wait()


def ocean_kernel(base_ref, meta_ref, got_ref, keep_ref, send_ref):
    row = iota((8, PEERS), 0)
    wanted = jnp.where(row < 4, base_ref[0] + row, base_ref[1] + row - 4).astype(f32)
    chosen = jnp.concatenate(
        [(meta_ref[n : n + 1, :] == wanted).astype(bf16) for n in range(4)], axis=1
    )
    values = jnp.concatenate(
        [
            jnp.concatenate(
                [
                    got_ref[pl.ds(ROWS_UP + 2 * n + e, PEERS, stride=ROWS2), :]
                    for e in range(2)
                ],
                axis=1,
            )
            for n in range(4)
        ],
        axis=0,
    )
    total = None
    for part in split3(values):
        got = jnp.dot(chosen, part, preferred_element_type=f32)
        total = got if total is None else total + got
    keep_ref[...] = total[0:4, :]
    send_ref[...] = total[4:8, :]


def update_kernel(meta_ref, got_ref, mom_ref, out_ref, block_ref):
    p = pl.program_id(0)

    @pl.when(p == 0)
    def unpack():
        for t in range(ROWS_UP):
            block_ref[8 + t * LANES : 8 + (t + 1) * LANES, :] = got_ref[
                pl.ds(t, PEERS, stride=ROWS2), :
            ].T

    count = meta_ref[4:5, :]
    top = iota((8, LANES), 0) == 0
    last = iota((8, LANES), 0) == 7
    live = jnp.broadcast_to(count, (8, LANES)) > p.astype(f32) + 0.5
    for i in range(LEV // 8):

        def grad(which):
            first = pl.multiple_of(8 + (p * UP + which) * LEV + i * 8, 8)
            prev = block_ref[pl.ds(first - 1, 8), :]
            after = block_ref[pl.ds(first + 1, 8), :]
            if i == 0:
                prev = jnp.where(top, block_ref[pl.ds(first, 8), :], prev)
            if i == LEV // 8 - 1:
                after = jnp.where(last, block_ref[pl.ds(first, 8), :], after)
            return prev - after

        gt, gq, gu, gv = (grad(which) for which in range(UP))
        production = (
            gu * gu + gv * gv, gt * gt, gq * gq, gt * gq, gu * gt, gv * gt, gu * gq, gu * gv,
        )
        for j in range(FLD):
            at = pl.ds(i * 64 + j, 8, stride=FLD)
            m = mom_ref[at, :]
            new = m + 0.5 * (jnp.tanh(production[j]) - (0.3 + 0.1 * j) * m)
            out_ref[at, :] = jnp.where(live, new, m)


SMEM = pl.BlockSpec(memory_space=pltpu.SMEM)
VMEM = pl.BlockSpec(memory_space=pltpu.VMEM)


def lane_tile(rows, tile):
    return pl.BlockSpec((rows, LANES), lambda *_: (0, tile))


def call(kernel, grid, ins, outs, out_specs, scratch, name):
    return pl.pallas_call(
        kernel,
        grid=grid,
        in_specs=ins,
        out_specs=out_specs,
        out_shape=[jax.ShapeDtypeStruct(shape, f32) for shape in outs],
        scratch_shapes=scratch,
        name=name,
    )


def pack(rows, owner_row, mom):
    return call(
        pack_kernel,
        (1,),
        [SMEM, VMEM] + [lane_tile(LEV * FLD, p) for p in range(CAP)],
        [(ROWS1 * PEERS, LANES)],
        [VMEM],
        [pltpu.VMEM((ROWS1 * LANES, LANES), f32)],
        "pack",
    )(rows, owner_row, *[mom] * CAP)[0]


def physics(cols, owner_row, regime_row, got, state, weights):
    rows = LEV * FLD
    return call(
        physics_kernel,
        (1,),
        [SMEM] + [VMEM] * 3 + [lane_tile(rows, h) for h in range(COL // LANES)] + [VMEM],
        [(rows, COL), (ROWS2 * PEERS, LANES), (8, PEERS)],
        [pl.BlockSpec(memory_space=pl.ANY), VMEM, VMEM],
        [
            pltpu.VMEM((ROWS_UP * LANES, LANES), f32),
            pltpu.VMEM((SLOTS, COL), bf16),
            pltpu.VMEM((DOWN * LEV + 8, COL), f32),
            pltpu.VMEM((2 * PAD_ROWS, LANES), f32),
            pltpu.VMEM((2 * PAD_ROWS, LANES), f32),
            pltpu.VMEM((2 * PAD_ROWS, LANES), f32),
            pltpu.VMEM((LEV, COL), f32),
            pltpu.VMEM((LEV, COL), f32),
            pltpu.VMEM((2, rows, LANES), f32),
            pltpu.SemaphoreType.DMA((2,)),
        ],
        "physics",
    )(cols, owner_row, regime_row, got, state, state, weights)


def ocean(*args):
    return call(
        ocean_kernel, (1,), [SMEM, VMEM, VMEM], [(4, 2 * LANES)] * 2, [VMEM] * 2, [], "ocean"
    )(*args)


def update(meta, back, mom):
    block = pl.BlockSpec((LEV * FLD, LANES), lambda p: (0, p))
    return call(
        update_kernel,
        (CAP,),
        [VMEM, VMEM, block],
        [(LEV * FLD, SLOTS)],
        [block],
        [pltpu.VMEM((ROWS_UP * LANES + 16, LANES), f32)],
        "update",
    )(meta, back, mom)[0]


def exchange(sent, rows):
    got = lax.all_to_all(
        sent.reshape(PEERS, 1, rows * LANES), ("node", "dev"), 0, 0, tiled=True
    )
    return got.reshape(PEERS * rows, LANES)


def local(state, span_owner, regime, moments, remap_weights, remap_rows, remap_cols):
    dev_count = lax.axis_size("dev")
    core = lax.axis_index("dev") % 2
    device = lax.axis_index(("node", "dev"))
    owner_row = span_owner.reshape(1, COL)
    mom = moments.reshape(LEV * FLD, SLOTS)
    got = exchange(pack(remap_rows, owner_row, mom), ROWS1)
    tend, sent, meta = physics(
        remap_cols, owner_row, regime.reshape(1, COL), got, state.reshape(LEV * FLD, COL), remap_weights
    )
    back = exchange(sent, ROWS2)
    base = jnp.stack([device * 4, (device + 1 - 2 * core) * 4]).astype(jnp.int32)
    keep, send = ocean(base, meta, back)
    other = lax.ppermute(send, "dev", [(i, i ^ 1) for i in range(dev_count)])
    new_mom = update(meta, back, mom)
    low = jnp.where(core == 0, keep, other).reshape(4, 2, LANES)
    high = jnp.where(core == 0, other, keep).reshape(4, 2, LANES)
    return (
        tend.reshape(LEV, FLD, COL),
        new_mom.reshape(LEV, FLD, SLOTS),
        jnp.concatenate([low, high], axis=1),
    )


def solution(mesh):
    return jax.shard_map(
        local,
        mesh=mesh,
        in_specs=(
            P(None, None, ("node", "dev")),
            P(("node", "dev"), None),
            P(("node", "dev")),
            P(None, None, ("node", "dev")),
            P(("node", "dev"), None, None),
            P(("node", "dev")),
            P(("node", "dev")),
        ),
        out_specs=(
            P(None, None, ("node", "dev")),
            P(None, None, ("node", "dev")),
            P(("node", "dev"), None, None),
        ),
        check_vma=False,
    )
```

```python
import jax
import jax.numpy as jnp
from jax import lax
from jax.experimental import pallas as pl
from jax.experimental.pallas import tpu as pltpu
from jax.sharding import PartitionSpec as P

LEV = 72
FLD = 8
PEERS = 128
LANES = 128
CAP = 4
COL = 256
SLOTS = CAP * PEERS
DOWN = 2
UP = 4
ROWS1 = 5
META = CAP * DOWN * LEV
ROWS_UP = CAP * UP * LEV // LANES
OCN_ROWS = 8
ROWS2 = ROWS_UP + OCN_ROWS
HALF = LEV // 2
PAD_ROWS = LEV * FLD + FLD
f32 = jnp.float32
bf16 = jnp.bfloat16


def iota(shape, axis):
    return lax.broadcasted_iota(jnp.int32, shape, axis)


def split3(x):
    hi = x.astype(bf16)
    rest = x - hi.astype(f32)
    mid = rest.astype(bf16)
    low = (rest - mid.astype(f32)).astype(bf16)
    return hi, mid, low


def columns_down(owner_row):
    real = owner_row.astype(f32)
    parts = [
        jnp.broadcast_to(real[:, h * LANES : (h + 1) * LANES], (LANES, LANES)).T
        for h in range(COL // LANES)
    ]
    return jnp.concatenate(parts, axis=0)


def pack_kernel(
    rows_hbm, owner_hbm, mom_ref, out_ref, tile_ref, rows_ref, owner_ref, block_ref, sem, small_sem
):
    small = [
        pltpu.make_async_copy(owner_hbm, owner_ref, small_sem.at[0]),
        pltpu.make_async_copy(rows_hbm, rows_ref, small_sem.at[1]),
    ]
    for copy in small:
        copy.start()
    copies = [
        pltpu.make_async_copy(
            mom_ref.at[:, pl.ds(p * LANES, LANES)], tile_ref.at[p], sem.at[p]
        )
        for p in range(CAP)
    ]
    for copy in copies:
        copy.start()
    for copy in small:
        copy.wait()
    owner_down = columns_down(owner_ref[...])
    peer = iota((COL, LANES), 1).astype(f32)
    count = jnp.sum((owner_down == peer).astype(f32), axis=0, keepdims=True)
    tail = ROWS1 * LANES - META
    which = iota((tail, LANES), 0)
    meta = jnp.where(which == 4, jnp.broadcast_to(count, (tail, LANES)), 0.0)
    for n in range(4):
        meta = jnp.where(which == n, rows_ref[n].astype(f32), meta)
    block_ref[META:, :] = meta
    for p in range(CAP):
        copies[p].wait()
        for at, moment in enumerate((0, 2)):
            first = (p * DOWN + at) * LEV
            block_ref[first : first + LEV, :] = tile_ref[p, pl.ds(moment, LEV, stride=FLD), :]
    for t in range(ROWS1):
        out_ref[pl.ds(t, PEERS, stride=ROWS1), :] = block_ref[t * LANES : (t + 1) * LANES, :].T


def softplus(x):
    return jnp.maximum(x, 0.0) + jnp.log(1.0 + jnp.exp(-jnp.abs(x)))


def micro_free(x, warm, mixed, icy, above, top):
    temper, vap, liq, rain, ice = x
    vapour = softplus(vap)
    liquid = softplus(liq)
    rain_q = softplus(rain)
    ice_q = softplus(ice)
    half_t = jnp.tanh(0.5 * temper)
    satur = 0.6 * jnp.exp(0.5 * half_t)
    excess = vapour - satur
    autoconv = 0.3 * liquid * liquid / (1.0 + liquid)
    evapor = 0.1 * rain_q * (0.5 - 0.5 * jnp.tanh(0.5 * excess))
    freeze = 0.3 * liquid * (0.5 - 0.5 * half_t)
    melting = 0.2 * ice_q * (0.5 + 0.5 * half_t)
    aggreg = 0.25 * ice_q * ice_q / (1.0 + ice_q)
    falling = 0.5 * rain_q
    rolled = pltpu.roll(falling, 1, 0)
    from_above = jnp.where(top, above, rolled)
    source = jnp.where(
        icy, 0.175 * jnp.tanh(vapour - 0.8 * satur), 0.2 * jnp.tanh(excess)
    )

    def pick(a, b, c):
        return jnp.where(warm, a, jnp.where(mixed, b, c))

    swap = freeze - melting
    kept = (
        temper + pick(-0.4 * evapor, 0.25 * swap, 0.25 * freeze),
        jnp.where(warm, vap + 0.5 * evapor, vap),
        liq - 0.5 * pick(autoconv, freeze + autoconv, freeze),
        rain
        + 0.5 * (pick(autoconv - evapor, autoconv + melting, aggreg) + from_above - falling),
        jnp.where(warm, ice, ice + 0.5 * jnp.where(mixed, swap, freeze - aggreg)),
    )
    return kept, source, excess, rolled


def micro_bound(kept, source, excess, m2, icy):
    temper, vap, liq, rain, ice = kept
    gain = source * (1.0 + 0.5 * jnp.tanh(0.5 * (m2 + excess)))
    return (
        temper + jnp.where(icy, gain, 0.8 * gain),
        vap - gain,
        jnp.where(icy, liq, liq + gain),
        rain,
        jnp.where(icy, ice + gain, ice),
    )


def solve(a_ref, k_ref, y_ref, g_ref):
    halves = range(COL // LANES)

    def kap(h, level):
        row = k_ref[level : level + 1, h * LANES : (h + 1) * LANES]
        return jnp.broadcast_to(row, (FLD, LANES))

    def rows(h, level):
        first = h * PAD_ROWS + level * FLD
        return slice(first, first + FLD)

    state = {}
    for step in range(HALF):
        for h in halves:
            for chain in range(2):
                k = LEV - 1 - step if chain else step
                k_new = kap(h, k - 1 if chain else k)
                a = a_ref[rows(h, k), :]
                if step == 0:
                    r = 1.0 / (1.0 + k_new)
                    d = a * r
                else:
                    k_old, g, d = state[h, chain]
                    r = 1.0 / (1.0 + k_new + k_old * (1.0 - g))
                    d = (a + k_old * d) * r
                g = k_new * r
                g_ref[rows(h, k), :] = g
                y_ref[rows(h, k), :] = d
                state[h, chain] = (k_new, g, d)
    z = {}
    for h in halves:
        (_, g_up, d_up), (_, g_dn, d_dn) = state[h, 0], state[h, 1]
        z[h, 0] = (d_up + g_up * d_dn) / (1.0 - g_up * g_dn)
        z[h, 1] = d_dn + g_dn * z[h, 0]
        y_ref[rows(h, HALF - 1), :] = z[h, 0]
        y_ref[rows(h, HALF), :] = z[h, 1]
    for step in range(1, HALF):
        for h in halves:
            for chain in range(2):
                k = HALF + step if chain else HALF - 1 - step
                z[h, chain] = y_ref[rows(h, k), :] + g_ref[rows(h, k), :] * z[h, chain]
                y_ref[rows(h, k), :] = z[h, chain]


def regimes(regime_ref, h):
    kind = jnp.broadcast_to(regime_ref[:, h * LANES : (h + 1) * LANES], (8, LANES))
    return kind == 0, kind == 1, kind == 2


def prepare_kernel(
    owner_ref, regime_ref, state_ref, tile_ref, hot_ref, part_ref, sem
):
    copies = [
        pltpu.make_async_copy(
            state_ref.at[:, pl.ds(h * LANES, LANES)], tile_ref.at[h], sem.at[h]
        )
        for h in range(COL // LANES)
    ]
    for copy in copies:
        copy.start()
    owner_row = owner_ref[...]
    owner_down = columns_down(owner_row)
    owner_real = owner_row.astype(f32)
    before = jnp.zeros((1, COL), f32)
    for h in range(COL // LANES):
        same = (
            jnp.concatenate([owner_down[h * LANES : (h + 1) * LANES, :]] * 2, axis=1) == owner_real
        )
        earlier = iota((LANES, COL), 0) + h * LANES < iota((LANES, COL), 1)
        before = before + jnp.sum((same & earlier).astype(f32), axis=0, keepdims=True)
    slot = owner_row + PEERS * before.astype(jnp.int32)
    for p in range(CAP):
        hot_ref[p * PEERS : (p + 1) * PEERS, :] = (
            iota((PEERS, COL), 0) + p * PEERS == slot
        ).astype(bf16)
    top = iota((8, LANES), 0) == 0
    for h in range(COL // LANES):
        copies[h].wait()
        warm, mixed, icy = regimes(regime_ref, h)
        above = jnp.zeros((8, LANES), f32)
        for i in range(LEV // 8):
            x = tuple(tile_ref[h, pl.ds(i * 64 + f, 8, stride=FLD), :] for f in range(5))
            kept, source, excess, above = micro_free(x, warm, mixed, icy, above, top)
            for f, value in enumerate(kept + (source, excess)):
                part_ref[h, f, i * 8 : i * 8 + 8, :] = value


def physics_kernel(
    cols_ref,
    regime_ref,
    got_ref,
    tile_ref,
    hot_ref,
    part_ref,
    weight_hbm,
    tend_out,
    out_ref,
    meta_ref,
    weight_ref,
    tend_ref,
    block_ref,
    mom_ref,
    a_ref,
    y_ref,
    g_ref,
    k_ref,
    e_ref,
    weight_sem,
    tend_sem,
):
    weights = pltpu.make_async_copy(weight_hbm, weight_ref, weight_sem)
    weights.start()
    for t in range(ROWS1):
        block_ref[t * LANES : (t + 1) * LANES, :] = got_ref[pl.ds(t, PEERS, stride=ROWS1), :].T
    meta_ref[...] = block_ref[META : META + 8, :]
    slotted = jnp.concatenate(
        [block_ref[p * DOWN * LEV : (p + 1) * DOWN * LEV, :] for p in range(CAP)], axis=1
    )
    total = None
    for part in split3(slotted):
        got = jnp.dot(part, hot_ref[...], preferred_element_type=f32)
        total = got if total is None else total + got
    mom_ref[0 : DOWN * LEV, :] = total

    top = iota((8, LANES), 0) == 0
    for h in range(COL // LANES):
        lanes = slice(h * LANES, (h + 1) * LANES)
        warm, mixed, icy = regimes(regime_ref, h)
        above = jnp.zeros((8, LANES), f32)
        base = h * PAD_ROWS
        for i in range(LEV // 8):
            m2 = mom_ref[LEV + i * 8 : LEV + i * 8 + 8, lanes]
            first = tuple(part_ref[h, f, i * 8 : i * 8 + 8, :] for f in range(7))
            x = micro_bound(first[:5], first[5], first[6], m2, icy)
            kept, source, excess, above = micro_free(x, warm, mixed, icy, above, top)
            x = micro_bound(kept, source, excess, m2, icy)
            for f, value in enumerate(x):
                a_ref[pl.ds(base + i * 64 + f, 8, stride=FLD), :] = value
            for f in range(5, FLD):
                a_ref[pl.ds(base + i * 64 + f, 8, stride=FLD), :] = tile_ref[
                    h, pl.ds(i * 64 + f, 8, stride=FLD), :
                ]
        for ref in (a_ref, y_ref):
            ref[base + LEV * FLD : base + PAD_ROWS, :] = jnp.zeros((FLD, LANES), f32)
    last = iota((8, COL), 0) == 7
    for i in range(LEV // 8):
        m0 = mom_ref[i * 8 : i * 8 + 8, :]
        m0_next = mom_ref[i * 8 + 1 : i * 8 + 9, :]
        energy = 30.5 + 30.0 * jnp.tanh(m0 + m0_next)
        if i == LEV // 8 - 1:
            energy = jnp.where(last, 0.0, energy)
        e_ref[i * 8 : i * 8 + 8, :] = energy
    for turn in range(3):
        src = a_ref if turn == 0 else y_ref
        for h in range(COL // LANES):
            lanes = slice(h * LANES, (h + 1) * LANES)
            for i in range(LEV // 8):

                def drop(f):
                    first = h * PAD_ROWS + i * 64 + f
                    return (
                        src[pl.ds(first, 8, stride=FLD), :]
                        - src[pl.ds(first + FLD, 8, stride=FLD), :]
                    )

                du, dv, dt = drop(5), drop(6), drop(0)
                shear = du * du + dv * dv
                mixing = 0.3 + 1.5 * shear / (1.0 + shear) * (0.5 - 0.5 * jnp.tanh(dt))
                k_ref[i * 8 : i * 8 + 8, lanes] = mixing * e_ref[i * 8 : i * 8 + 8, lanes]
        solve(a_ref, k_ref, y_ref, g_ref)

    field = iota((FLD, LANES), 0)
    kept = (field >= 2) & (field <= 4)
    copies = []
    for h in range(COL // LANES):
        for k in range(LEV):
            rows = slice(k * FLD, (k + 1) * FLD)
            at = slice(h * PAD_ROWS + k * FLD, h * PAD_ROWS + (k + 1) * FLD)
            mixed_state = jnp.where(kept, a_ref[at, :], y_ref[at, :])
            tend_ref[h, rows, :] = mixed_state - tile_ref[h, rows, :]
        copies.append(
            pltpu.make_async_copy(
                tend_ref.at[h], tend_out.at[:, pl.ds(h * LANES, LANES)], tend_sem.at[h]
            )
        )
        copies[-1].start()

    fields = jnp.concatenate(
        [
            jnp.concatenate(
                [y_ref[pl.ds(h * PAD_ROWS + f, LEV, stride=FLD), :] for f in (0, 1, 5, 6)], axis=0
            )
            for h in range(COL // LANES)
        ],
        axis=1,
    )
    total = None
    for part in split3(fields):
        got = lax.dot_general(
            part, hot_ref[...], (((1,), (1,)), ((), ())), preferred_element_type=f32
        )
        total = got if total is None else total + got
    for p in range(CAP):
        block_ref[p * UP * LEV : (p + 1) * UP * LEV, :] = total[:, p * PEERS : (p + 1) * PEERS]
    for t in range(ROWS_UP):
        out_ref[pl.ds(t, PEERS, stride=ROWS2), :] = block_ref[t * LANES : (t + 1) * LANES, :].T

    bottom = slice((LEV - 1) * FLD, LEV * FLD)
    b = jnp.concatenate(
        [tile_ref[h, bottom, :] + tend_ref[h, bottom, :] for h in range(COL // LANES)], axis=1
    )
    b0, b3, b5, b6 = (b[f : f + 1, :] for f in (0, 3, 5, 6))
    wind = jnp.sqrt(1.0 + b5 * b5 + b6 * b6)
    flux = jnp.concatenate(
        [
            -0.5 * wind * b5,
            -0.5 * wind * b6,
            0.5 * softplus(b3),
            -0.3 * wind * b0,
            jnp.zeros((4, COL), f32),
        ],
        axis=0,
    )
    odd = iota((PEERS, LANES), 0) % 2 == 1
    weights.wait()
    for n in range(4):
        used = jnp.where(cols_ref[n] == 0, flux[:, :LANES], flux[:, LANES:])
        product = jnp.dot(
            used, weight_ref[n], precision=lax.Precision.HIGHEST, preferred_element_type=f32
        )
        for e in range(2):
            out_ref[pl.ds(ROWS_UP + 2 * n + e, PEERS, stride=ROWS2), :] = jnp.where(
                odd, product[2 + e : 3 + e, :], product[e : e + 1, :]
            )
    for copy in copies:
        copy.wait()


def ocean_kernel(base_ref, meta_ref, got_ref, keep_ref, send_ref):
    row = iota((8, PEERS), 0)
    wanted = jnp.where(row < 4, base_ref[0] + row, base_ref[1] + row - 4).astype(f32)
    chosen = jnp.concatenate(
        [(meta_ref[n : n + 1, :] == wanted).astype(bf16) for n in range(4)], axis=1
    )
    values = jnp.concatenate(
        [
            jnp.concatenate(
                [
                    got_ref[pl.ds(ROWS_UP + 2 * n + e, PEERS, stride=ROWS2), :]
                    for e in range(2)
                ],
                axis=1,
            )
            for n in range(4)
        ],
        axis=0,
    )
    total = None
    for part in split3(values):
        got = jnp.dot(chosen, part, preferred_element_type=f32)
        total = got if total is None else total + got
    keep_ref[...] = total[0:4, :]
    send_ref[...] = total[4:8, :]


def update_kernel(meta_ref, got_ref, tile_ref, out_ref, block_ref, new_ref, sem):
    for t in range(ROWS_UP):
        block_ref[8 + t * LANES : 8 + (t + 1) * LANES, :] = got_ref[
            pl.ds(t, PEERS, stride=ROWS2), :
        ].T
    count = meta_ref[4:5, :]
    top = iota((8, LANES), 0) == 0
    last = iota((8, LANES), 0) == 7
    copies = []
    for p in range(CAP):
        live = jnp.broadcast_to(count, (8, LANES)) > p + 0.5
        for i in range(LEV // 8):

            def grad(which):
                first = 8 + (p * UP + which) * LEV + i * 8
                prev = block_ref[first - 1 : first + 7, :]
                after = block_ref[first + 1 : first + 9, :]
                if i == 0:
                    prev = jnp.where(top, block_ref[first : first + 8, :], prev)
                if i == LEV // 8 - 1:
                    after = jnp.where(last, block_ref[first : first + 8, :], after)
                return prev - after

            gt, gq, gu, gv = (grad(which) for which in range(UP))
            production = (
                gu * gu + gv * gv, gt * gt, gq * gq, gt * gq, gu * gt, gv * gt, gu * gq, gu * gv,
            )
            for j in range(FLD):
                at = pl.ds(i * 64 + j, 8, stride=FLD)
                m = tile_ref[p, at, :]
                new = m + 0.5 * (jnp.tanh(production[j]) - (0.3 + 0.1 * j) * m)
                new_ref[p, at, :] = jnp.where(live, new, m)
        copies.append(
            pltpu.make_async_copy(
                new_ref.at[p], out_ref.at[:, pl.ds(p * LANES, LANES)], sem.at[p]
            )
        )
        copies[-1].start()
    for copy in copies:
        copy.wait()


SMEM = pl.BlockSpec(memory_space=pltpu.SMEM)
VMEM = pl.BlockSpec(memory_space=pltpu.VMEM)
ANY = pl.BlockSpec(memory_space=pl.ANY)
HBM = pl.BlockSpec(memory_space=pltpu.HBM)
PLANE = LEV * FLD
VMEM_LIMIT = 16 << 20


def here(shape, dtype=f32):
    return pltpu.VMEM(shape, dtype)


def far(shape):
    return jax.ShapeDtypeStruct(shape, f32)


def hold(x):
    return pltpu.with_memory_space_constraint(x, pltpu.VMEM)


def outside(x):
    return pltpu.with_memory_space_constraint(x, pltpu.HBM)


def call(kernel, ins, outs, out_specs, scratch, name):
    return pl.pallas_call(
        kernel,
        in_specs=ins,
        out_specs=out_specs,
        out_shape=outs,
        scratch_shapes=scratch,
        name=name,
        compiler_params=pltpu.CompilerParams(vmem_limit_bytes=VMEM_LIMIT),
    )


def pack(rows, owner_row, mom):
    return call(
        pack_kernel,
        [HBM] * 3,
        [here((ROWS1 * PEERS, LANES)), here((CAP, PLANE, LANES))],
        [VMEM] * 2,
        [
            pltpu.SMEM((4,), jnp.int32),
            pltpu.VMEM((1, COL), jnp.int32),
            pltpu.VMEM((ROWS1 * LANES, LANES), f32),
            pltpu.SemaphoreType.DMA((CAP,)),
            pltpu.SemaphoreType.DMA((2,)),
        ],
        "pack",
    )(outside(rows), outside(owner_row), outside(mom))


def prepare(owner_row, regime_row, state):
    return call(
        prepare_kernel,
        [VMEM, VMEM, HBM],
        [
            here((2, PLANE, LANES)),
            here((SLOTS, COL), bf16),
            here((2, 7, LEV, LANES)),
        ],
        [VMEM] * 3,
        [pltpu.SemaphoreType.DMA((2,))],
        "prepare",
    )(owner_row, regime_row, outside(state))


def physics(cols, regime_row, got, tiles, hot, parts, weights):
    return call(
        physics_kernel,
        [SMEM] + [VMEM] * 5 + [HBM],
        [far((PLANE, COL)), here((ROWS2 * PEERS, LANES)), here((8, PEERS))],
        [ANY, VMEM, VMEM],
        [
            pltpu.VMEM((4, LANES, LANES), f32),
            pltpu.VMEM((2, PLANE, LANES), f32),
            pltpu.VMEM((ROWS_UP * LANES, LANES), f32),
            pltpu.VMEM((DOWN * LEV + 8, COL), f32),
            pltpu.VMEM((2 * PAD_ROWS, LANES), f32),
            pltpu.VMEM((2 * PAD_ROWS, LANES), f32),
            pltpu.VMEM((2 * PAD_ROWS, LANES), f32),
            pltpu.VMEM((LEV, COL), f32),
            pltpu.VMEM((LEV, COL), f32),
            pltpu.SemaphoreType.DMA,
            pltpu.SemaphoreType.DMA((2,)),
        ],
        "physics",
    )(cols, regime_row, *(hold(x) for x in (got, tiles, hot, parts)), outside(weights))


def ocean(base, meta, back):
    return call(
        ocean_kernel, [SMEM, VMEM, VMEM], [here((4, 2 * LANES))] * 2, [VMEM] * 2, [], "ocean"
    )(base, hold(meta), hold(back))


def update(meta, back, tiles):
    return call(
        update_kernel,
        [VMEM] * 3,
        [far((PLANE, SLOTS))],
        [ANY],
        [
            pltpu.VMEM((ROWS_UP * LANES + 16, LANES), f32),
            pltpu.VMEM((CAP, PLANE, LANES), f32),
            pltpu.SemaphoreType.DMA((CAP,)),
        ],
        "update",
    )(hold(meta), hold(back), hold(tiles))[0]


def exchange(sent, rows):
    got = lax.all_to_all(
        sent.reshape(PEERS, 1, rows * LANES), ("node", "dev"), 0, 0, tiled=True
    )
    return got.reshape(PEERS * rows, LANES)


def local(state, span_owner, regime, moments, remap_weights, remap_rows, remap_cols):
    dev_count = lax.axis_size("dev")
    core = lax.axis_index("dev") % 2
    device = lax.axis_index(("node", "dev"))
    owner_row = span_owner.reshape(1, COL)
    regime_row = regime.reshape(1, COL)
    sent, mom_tiles = pack(remap_rows, owner_row, moments.reshape(PLANE, SLOTS))
    tiles, hot, parts = prepare(owner_row, regime_row, state.reshape(PLANE, COL))
    got = exchange(sent, ROWS1)
    tend, sent, meta = physics(remap_cols, regime_row, got, tiles, hot, parts, remap_weights)
    back = exchange(sent, ROWS2)
    base = jnp.stack([device * 4, (device + 1 - 2 * core) * 4]).astype(jnp.int32)
    keep, send = ocean(base, meta, back)
    other = lax.ppermute(send, "dev", [(i, i ^ 1) for i in range(dev_count)])
    new_mom = update(meta, back, mom_tiles)
    low = jnp.where(core == 0, keep, other).reshape(4, 2, LANES)
    high = jnp.where(core == 0, other, keep).reshape(4, 2, LANES)
    return (
        tend.reshape(LEV, FLD, COL),
        new_mom.reshape(LEV, FLD, SLOTS),
        jnp.concatenate([low, high], axis=1),
    )


def solution(mesh):
    return jax.shard_map(
        local,
        mesh=mesh,
        in_specs=(
            P(None, None, ("node", "dev")),
            P(("node", "dev"), None),
            P(("node", "dev")),
            P(None, None, ("node", "dev")),
            P(("node", "dev"), None, None),
            P(("node", "dev")),
            P(("node", "dev")),
        ),
        out_specs=(
            P(None, None, ("node", "dev")),
            P(None, None, ("node", "dev")),
            P(("node", "dev"), None, None),
        ),
        check_vma=False,
    )
```

```python
import jax
import jax.numpy as jnp
from jax import lax
from jax.experimental import pallas as pl
from jax.experimental.pallas import tpu as pltpu
from jax.sharding import PartitionSpec as P

LEV = 72
FLD = 8
PEERS = 128
LANES = 128
CAP = 4
COL = 256
SLOTS = CAP * PEERS
DOWN = 2
UP = 4
ROWS1 = 5
META = CAP * DOWN * LEV
ROWS_UP = CAP * UP * LEV // LANES
OCN_ROWS = 8
ROWS2 = ROWS_UP + OCN_ROWS
HALF = LEV // 2
PAD_ROWS = LEV * FLD + FLD
f32 = jnp.float32
bf16 = jnp.bfloat16


def iota(shape, axis):
    return lax.broadcasted_iota(jnp.int32, shape, axis)


def split3(x):
    hi = x.astype(bf16)
    rest = x - hi.astype(f32)
    mid = rest.astype(bf16)
    low = (rest - mid.astype(f32)).astype(bf16)
    return hi, mid, low


def columns_down(owner_row):
    real = owner_row.astype(f32)
    parts = [
        jnp.broadcast_to(real[:, h * LANES : (h + 1) * LANES], (LANES, LANES)).T
        for h in range(COL // LANES)
    ]
    return jnp.concatenate(parts, axis=0)


def pack_kernel(
    rows_hbm, owner_hbm, mom_ref, out_ref, rows_ref, owner_ref, block_ref, sem, small_sem
):
    small = [
        pltpu.make_async_copy(owner_hbm, owner_ref, small_sem.at[0]),
        pltpu.make_async_copy(rows_hbm, rows_ref, small_sem.at[1]),
    ]
    copies = []
    for p in range(CAP):
        for at, moment in enumerate((0, 2)):
            copies.append(
                pltpu.make_async_copy(
                    mom_ref.at[:, moment, pl.ds(p * LANES, LANES)],
                    block_ref.at[pl.ds((p * DOWN + at) * LEV, LEV), :],
                    sem.at[p, at],
                )
            )
    for copy in small + copies:
        copy.start()
    for copy in small:
        copy.wait()
    owner_down = columns_down(owner_ref[...])
    peer = iota((COL, LANES), 1).astype(f32)
    count = jnp.sum((owner_down == peer).astype(f32), axis=0, keepdims=True)
    tail = ROWS1 * LANES - META
    which = iota((tail, LANES), 0)
    meta = jnp.where(which == 4, jnp.broadcast_to(count, (tail, LANES)), 0.0)
    for n in range(4):
        meta = jnp.where(which == n, rows_ref[n].astype(f32), meta)
    block_ref[META:, :] = meta
    for copy in copies:
        copy.wait()
    for t in range(ROWS1):
        out_ref[pl.ds(t, PEERS, stride=ROWS1), :] = block_ref[t * LANES : (t + 1) * LANES, :].T


def softplus(x):
    return jnp.maximum(x, 0.0) + jnp.log(1.0 + jnp.exp(-jnp.abs(x)))


def micro_free(x, warm, mixed, icy, above, top):
    temper, vap, liq, rain, ice = x
    vapour = softplus(vap)
    liquid = softplus(liq)
    rain_q = softplus(rain)
    ice_q = softplus(ice)
    half_t = jnp.tanh(0.5 * temper)
    satur = 0.6 * jnp.exp(0.5 * half_t)
    excess = vapour - satur
    autoconv = 0.3 * liquid * liquid / (1.0 + liquid)
    evapor = 0.1 * rain_q * (0.5 - 0.5 * jnp.tanh(0.5 * excess))
    freeze = 0.3 * liquid * (0.5 - 0.5 * half_t)
    melting = 0.2 * ice_q * (0.5 + 0.5 * half_t)
    aggreg = 0.25 * ice_q * ice_q / (1.0 + ice_q)
    falling = 0.5 * rain_q
    rolled = pltpu.roll(falling, 1, 0)
    from_above = jnp.where(top, above, rolled)
    source = jnp.where(
        icy, 0.175 * jnp.tanh(vapour - 0.8 * satur), 0.2 * jnp.tanh(excess)
    )

    def pick(a, b, c):
        return jnp.where(warm, a, jnp.where(mixed, b, c))

    swap = freeze - melting
    kept = (
        temper + pick(-0.4 * evapor, 0.25 * swap, 0.25 * freeze),
        jnp.where(warm, vap + 0.5 * evapor, vap),
        liq - 0.5 * pick(autoconv, freeze + autoconv, freeze),
        rain
        + 0.5 * (pick(autoconv - evapor, autoconv + melting, aggreg) + from_above - falling),
        jnp.where(warm, ice, ice + 0.5 * jnp.where(mixed, swap, freeze - aggreg)),
    )
    return kept, source, excess, rolled


def micro_bound(kept, source, excess, m2, icy):
    temper, vap, liq, rain, ice = kept
    gain = source * (1.0 + 0.5 * jnp.tanh(0.5 * (m2 + excess)))
    return (
        temper + jnp.where(icy, gain, 0.8 * gain),
        vap - gain,
        jnp.where(icy, liq, liq + gain),
        rain,
        jnp.where(icy, ice + gain, ice),
    )


def solve(a_ref, k_ref, c_ref, y_ref, g_ref):
    halves = range(COL // LANES)

    def row(ref, h, level):
        one = ref[level : level + 1, h * LANES : (h + 1) * LANES]
        return jnp.broadcast_to(one, (FLD, LANES))

    def rows(h, level):
        first = h * PAD_ROWS + level * FLD
        return slice(first, first + FLD)

    state = {}
    ends = {}
    for step in range(HALF):
        for h in halves:
            for chain in range(2):
                k = LEV - 1 - step if chain else step
                k_new = row(k_ref, h, k - 1 if chain else k)
                a = a_ref[rows(h, k), :]
                if step == 0:
                    r = 1.0 / row(c_ref, h, k)
                    d = a * r
                else:
                    k_old, r, d = state[h, chain]
                    r = 1.0 / (row(c_ref, h, k) - (k_old * k_old) * r)
                    d = a * r + (k_old * r) * d
                g = k_new * r
                g_ref[rows(h, k), :] = g
                y_ref[rows(h, k), :] = d
                state[h, chain] = (k_new, r, d)
                ends[h, chain] = g
    z = {}
    for h in halves:
        d_up, d_dn = state[h, 0][2], state[h, 1][2]
        g_up, g_dn = ends[h, 0], ends[h, 1]
        z[h, 0] = (d_up + g_up * d_dn) / (1.0 - g_up * g_dn)
        z[h, 1] = d_dn + g_dn * z[h, 0]
        y_ref[rows(h, HALF - 1), :] = z[h, 0]
        y_ref[rows(h, HALF), :] = z[h, 1]
    for step in range(1, HALF):
        for h in halves:
            for chain in range(2):
                k = HALF + step if chain else HALF - 1 - step
                z[h, chain] = y_ref[rows(h, k), :] + g_ref[rows(h, k), :] * z[h, chain]
                y_ref[rows(h, k), :] = z[h, chain]


def regimes(regime_ref, h):
    kind = jnp.broadcast_to(regime_ref[:, h * LANES : (h + 1) * LANES], (8, LANES))
    return kind == 0, kind == 1, kind == 2


def prepare_kernel(
    owner_ref, regime_ref, state_ref, mom_ref, weight_ref,
    tile_ref, hot_ref, part_ref, mom_tile_ref, weight_part_ref,
    weight_own, sem, mom_sem, weight_sem,
):
    copies = [
        pltpu.make_async_copy(
            state_ref.at[:, pl.ds(h * LANES, LANES)], tile_ref.at[h], sem.at[h]
        )
        for h in range(COL // LANES)
    ]
    weights = pltpu.make_async_copy(weight_ref, weight_own, weight_sem)
    moments = [
        pltpu.make_async_copy(
            mom_ref.at[:, pl.ds(p * LANES, LANES)], mom_tile_ref.at[p], mom_sem.at[p]
        )
        for p in range(CAP)
    ]
    for copy in copies + [weights] + moments:
        copy.start()
    owner_row = owner_ref[...]
    owner_down = columns_down(owner_row)
    owner_real = owner_row.astype(f32)
    before = jnp.zeros((1, COL), f32)
    for h in range(COL // LANES):
        same = (
            jnp.concatenate([owner_down[h * LANES : (h + 1) * LANES, :]] * 2, axis=1) == owner_real
        )
        earlier = iota((LANES, COL), 0) + h * LANES < iota((LANES, COL), 1)
        before = before + jnp.sum((same & earlier).astype(f32), axis=0, keepdims=True)
    slot = owner_row + PEERS * before.astype(jnp.int32)
    for p in range(CAP):
        hot_ref[p * PEERS : (p + 1) * PEERS, :] = (
            iota((PEERS, COL), 0) + p * PEERS == slot
        ).astype(bf16)
    top = iota((8, LANES), 0) == 0
    for h in range(COL // LANES):
        copies[h].wait()
        warm, mixed, icy = regimes(regime_ref, h)
        above = jnp.zeros((8, LANES), f32)
        for i in range(LEV // 8):
            x = tuple(tile_ref[h, pl.ds(i * 64 + f, 8, stride=FLD), :] for f in range(5))
            kept, source, excess, above = micro_free(x, warm, mixed, icy, above, top)
            for f, value in enumerate(kept + (source, excess)):
                part_ref[h, f, i * 8 : i * 8 + 8, :] = value
    weights.wait()
    for n in range(4):
        down, across = (n % 2) * LANES, (n // 2) * LANES
        for at, part in enumerate(split3(weight_own[n])):
            weight_part_ref[at, down : down + LANES, across : across + LANES] = part
    for copy in moments:
        copy.wait()


def physics_kernel(
    device_ref,
    cols_ref,
    regime_ref,
    got_ref,
    tile_ref,
    hot_ref,
    part_ref,
    weight_ref,
    tend_out,
    out_ref,
    meta_ref,
    tend_ref,
    block_ref,
    mom_ref,
    a_ref,
    y_ref,
    g_ref,
    k_ref,
    c_ref,
    e_ref,
    tend_sem,
):
    for t in range(ROWS1):
        block_ref[t * LANES : (t + 1) * LANES, :] = got_ref[pl.ds(t, PEERS, stride=ROWS1), :].T
    device = device_ref[0]
    core = device % 2
    meta_ref[0:2, :] = jnp.where(
        core == 1, block_ref[META + 2 : META + 4, :], block_ref[META : META + 2, :]
    )
    meta_ref[2:3, :] = jnp.full((1, PEERS), (device * 4).astype(f32))
    meta_ref[3:4, :] = jnp.full((1, PEERS), ((device + 1 - 2 * core) * 4).astype(f32))
    meta_ref[4:8, :] = block_ref[META + 4 : META + 8, :]
    slotted = jnp.concatenate(
        [block_ref[p * DOWN * LEV : (p + 1) * DOWN * LEV, :] for p in range(CAP)], axis=1
    )
    total = None
    for part in split3(slotted):
        got = jnp.dot(part, hot_ref[...], preferred_element_type=f32)
        total = got if total is None else total + got
    mom_ref[0 : DOWN * LEV, :] = total

    top = iota((8, LANES), 0) == 0
    for h in range(COL // LANES):
        lanes = slice(h * LANES, (h + 1) * LANES)
        warm, mixed, icy = regimes(regime_ref, h)
        above = jnp.zeros((8, LANES), f32)
        base = h * PAD_ROWS
        for i in range(LEV // 8):
            m2 = mom_ref[LEV + i * 8 : LEV + i * 8 + 8, lanes]
            first = tuple(part_ref[h, f, i * 8 : i * 8 + 8, :] for f in range(7))
            x = micro_bound(first[:5], first[5], first[6], m2, icy)
            kept, source, excess, above = micro_free(x, warm, mixed, icy, above, top)
            x = micro_bound(kept, source, excess, m2, icy)
            for f, value in enumerate(x):
                a_ref[pl.ds(base + i * 64 + f, 8, stride=FLD), :] = value
            for f in range(5, FLD):
                a_ref[pl.ds(base + i * 64 + f, 8, stride=FLD), :] = tile_ref[
                    h, pl.ds(i * 64 + f, 8, stride=FLD), :
                ]
        for ref in (a_ref, y_ref):
            ref[base + LEV * FLD : base + PAD_ROWS, :] = jnp.zeros((FLD, LANES), f32)
    last = iota((8, COL), 0) == 7
    for i in range(LEV // 8):
        m0 = mom_ref[i * 8 : i * 8 + 8, :]
        m0_next = mom_ref[i * 8 + 1 : i * 8 + 9, :]
        energy = 30.5 + 30.0 * jnp.tanh(m0 + m0_next)
        if i == LEV // 8 - 1:
            energy = jnp.where(last, 0.0, energy)
        e_ref[i * 8 : i * 8 + 8, :] = energy
    for turn in range(3):
        src = a_ref if turn == 0 else y_ref
        for h in range(COL // LANES):
            lanes = slice(h * LANES, (h + 1) * LANES)
            above = jnp.zeros((8, LANES), f32)
            for i in range(LEV // 8):

                def drop(f):
                    first = h * PAD_ROWS + i * 64 + f
                    return (
                        src[pl.ds(first, 8, stride=FLD), :]
                        - src[pl.ds(first + FLD, 8, stride=FLD), :]
                    )

                du, dv, dt = drop(5), drop(6), drop(0)
                shear = du * du + dv * dv
                mixing = 0.3 + 1.5 * shear / (1.0 + shear) * (0.5 - 0.5 * jnp.tanh(dt))
                kappa = mixing * e_ref[i * 8 : i * 8 + 8, lanes]
                rolled = pltpu.roll(kappa, 1, 0)
                k_ref[i * 8 : i * 8 + 8, lanes] = kappa
                c_ref[i * 8 : i * 8 + 8, lanes] = 1.0 + kappa + jnp.where(top, above, rolled)
                above = rolled
        solve(a_ref, k_ref, c_ref, y_ref, g_ref)

    field = iota((FLD, LANES), 0)
    kept = (field >= 2) & (field <= 4)
    bottom = []
    for h in range(COL // LANES):
        level = slice((LEV - 1) * FLD, LEV * FLD)
        at = slice(h * PAD_ROWS + (LEV - 1) * FLD, h * PAD_ROWS + LEV * FLD)
        old = tile_ref[h, level, :]
        bottom.append(old + (jnp.where(kept, a_ref[at, :], y_ref[at, :]) - old))
    b = jnp.concatenate(bottom, axis=1)
    b0, b3, b5, b6 = (b[f : f + 1, :] for f in (0, 3, 5, 6))
    wind = jnp.sqrt(1.0 + b5 * b5 + b6 * b6)
    flux = jnp.concatenate(
        [
            -0.5 * wind * b5,
            -0.5 * wind * b6,
            0.5 * softplus(b3),
            -0.3 * wind * b0,
            jnp.zeros((4, COL), f32),
        ],
        axis=0,
    )
    none = jnp.zeros((FLD, LANES), f32)
    used = []
    for n in range(4):
        mine = jnp.where(cols_ref[n] == 0, flux[:, :LANES], flux[:, LANES:])
        used.append(jnp.concatenate([none, mine] if n % 2 else [mine, none], axis=1))
    hi, mid, low = split3(jnp.concatenate(used, axis=0))

    def weighted(parts, at):
        got = jnp.dot(
            jnp.concatenate(parts, axis=0), weight_ref[at], preferred_element_type=f32
        )
        total = got[0:32, :]
        for i in range(1, len(parts)):
            total = total + got[i * 32 : i * 32 + 32, :]
        return total

    products = weighted([hi], 2) + weighted([hi, mid], 1) + weighted([hi, mid, low], 0)
    odd = iota((PEERS, LANES), 0) % 2 == 1
    for n in range(2):
        for e in range(4):
            even_row = products[n * 8 + e : n * 8 + e + 1, 0:LANES]
            odd_row = products[n * 8 + 16 + e : n * 8 + 17 + e, LANES:]
            out_ref[pl.ds(ROWS_UP + 4 * n + e, PEERS, stride=ROWS2), :] = jnp.where(
                odd, odd_row, even_row
            )

    copies = []
    for h in range(COL // LANES):
        for k in range(LEV):
            rows = slice(k * FLD, (k + 1) * FLD)
            at = slice(h * PAD_ROWS + k * FLD, h * PAD_ROWS + (k + 1) * FLD)
            mixed_state = jnp.where(kept, a_ref[at, :], y_ref[at, :])
            tend_ref[h, rows, :] = mixed_state - tile_ref[h, rows, :]
        copies.append(
            pltpu.make_async_copy(
                tend_ref.at[h], tend_out.at[:, pl.ds(h * LANES, LANES)], tend_sem.at[h]
            )
        )
        copies[-1].start()

    fields = jnp.concatenate(
        [
            jnp.concatenate(
                [y_ref[pl.ds(h * PAD_ROWS + f, LEV, stride=FLD), :] for f in (0, 1, 5, 6)], axis=0
            )
            for h in range(COL // LANES)
        ],
        axis=1,
    )
    parts = split3(fields)
    sent = 0
    for pair in range(CAP // 2):
        hot = hot_ref[pair * 2 * PEERS : (pair + 1) * 2 * PEERS, :]
        total = None
        for part in parts:
            got = lax.dot_general(
                part, hot, (((1,), (1,)), ((), ())), preferred_element_type=f32
            )
            total = got if total is None else total + got
        for q in range(2):
            first = (pair * 2 + q) * UP * LEV
            block_ref[first : first + UP * LEV, :] = total[:, q * PEERS : (q + 1) * PEERS]
        ready = (pair + 1) * 2 * UP * LEV // LANES
        for t in range(sent, ready):
            out_ref[pl.ds(t, PEERS, stride=ROWS2), :] = block_ref[
                t * LANES : (t + 1) * LANES, :
            ].T
        sent = ready
    for copy in copies:
        copy.wait()


def ocean_kernel(meta_ref, got_ref, keep_ref, send_ref):
    row = iota((8, PEERS), 0).astype(f32)
    wanted = jnp.where(row < 3.5, meta_ref[2:3, :] + row, meta_ref[3:4, :] + (row - 4.0))
    chosen = jnp.concatenate(
        [(meta_ref[n : n + 1, :] == wanted).astype(bf16) for n in range(2)], axis=1
    )
    values = jnp.concatenate(
        [
            jnp.concatenate(
                [
                    got_ref[pl.ds(ROWS_UP + 4 * n + e, PEERS, stride=ROWS2), :]
                    for e in range(4)
                ],
                axis=1,
            )
            for n in range(2)
        ],
        axis=0,
    )
    total = None
    for part in split3(values):
        got = jnp.dot(chosen, part, preferred_element_type=f32)
        total = got if total is None else total + got
    for e in range(4):
        part = total[:, e * LANES : (e + 1) * LANES]
        keep_ref[:, e, :] = part[0:4, :]
        send_ref[:, e, :] = part[4:8, :]


def update_kernel(meta_ref, got_ref, tile_ref, out_ref, block_ref, new_ref, sem):
    for t in range(ROWS_UP):
        block_ref[8 + t * LANES : 8 + (t + 1) * LANES, :] = got_ref[
            pl.ds(t, PEERS, stride=ROWS2), :
        ].T
    count = meta_ref[4:5, :]
    top = iota((8, LANES), 0) == 0
    last = iota((8, LANES), 0) == 7
    copies = []
    for p in range(CAP):
        live = jnp.broadcast_to(count, (8, LANES)) > p + 0.5
        for i in range(LEV // 8):

            def grad(which):
                first = 8 + (p * UP + which) * LEV + i * 8
                prev = block_ref[first - 1 : first + 7, :]
                after = block_ref[first + 1 : first + 9, :]
                if i == 0:
                    prev = jnp.where(top, block_ref[first : first + 8, :], prev)
                if i == LEV // 8 - 1:
                    after = jnp.where(last, block_ref[first : first + 8, :], after)
                return prev - after

            gt, gq, gu, gv = (grad(which) for which in range(UP))
            production = (
                gu * gu + gv * gv, gt * gt, gq * gq, gt * gq, gu * gt, gv * gt, gu * gq, gu * gv,
            )
            for j in range(FLD):
                at = pl.ds(i * 64 + j, 8, stride=FLD)
                m = tile_ref[p, at, :]
                new = m + 0.5 * (jnp.tanh(production[j]) - (0.3 + 0.1 * j) * m)
                new_ref[p, at, :] = jnp.where(live, new, m)
        copies.append(
            pltpu.make_async_copy(
                new_ref.at[p], out_ref.at[:, pl.ds(p * LANES, LANES)], sem.at[p]
            )
        )
        copies[-1].start()
    for copy in copies:
        copy.wait()


SMEM = pl.BlockSpec(memory_space=pltpu.SMEM)
VMEM = pl.BlockSpec(memory_space=pltpu.VMEM)
ANY = pl.BlockSpec(memory_space=pl.ANY)
HBM = pl.BlockSpec(memory_space=pltpu.HBM)
PLANE = LEV * FLD
VMEM_LIMIT = 16 << 20


def here(shape, dtype=f32):
    return pltpu.VMEM(shape, dtype)


def far(shape):
    return jax.ShapeDtypeStruct(shape, f32)


def hold(x):
    return pltpu.with_memory_space_constraint(x, pltpu.VMEM)


def outside(x):
    return pltpu.with_memory_space_constraint(x, pltpu.HBM)


def call(kernel, ins, outs, out_specs, scratch, name):
    return pl.pallas_call(
        kernel,
        in_specs=ins,
        out_specs=out_specs,
        out_shape=outs,
        scratch_shapes=scratch,
        name=name,
        compiler_params=pltpu.CompilerParams(vmem_limit_bytes=VMEM_LIMIT),
    )


def pack(rows, owner_row, mom):
    return call(
        pack_kernel,
        [HBM] * 3,
        [here((ROWS1 * PEERS, LANES))],
        [VMEM],
        [
            pltpu.SMEM((4,), jnp.int32),
            pltpu.VMEM((1, COL), jnp.int32),
            pltpu.VMEM((ROWS1 * LANES, LANES), f32),
            pltpu.SemaphoreType.DMA((CAP, DOWN)),
            pltpu.SemaphoreType.DMA((2,)),
        ],
        "pack",
    )(outside(rows), outside(owner_row), outside(mom))[0]


def prepare(owner_row, regime_row, state, mom, weights):
    return call(
        prepare_kernel,
        [VMEM] * 2 + [HBM] * 3,
        [
            here((2, PLANE, LANES)),
            here((SLOTS, COL), bf16),
            here((2, 7, LEV, LANES)),
            here((CAP, PLANE, LANES)),
            here((3, 2 * LANES, 2 * LANES), bf16),
        ],
        [VMEM] * 5,
        [
            pltpu.VMEM((4, LANES, LANES), f32),
            pltpu.SemaphoreType.DMA((2,)),
            pltpu.SemaphoreType.DMA((CAP,)),
            pltpu.SemaphoreType.DMA,
        ],
        "prepare",
    )(owner_row, regime_row, outside(state), outside(mom), outside(weights))


def physics(device, cols, regime_row, got, tiles, hot, parts, weights):
    return call(
        physics_kernel,
        [SMEM] * 2 + [VMEM] * 6,
        [far((PLANE, COL)), here((ROWS2 * PEERS, LANES)), here((8, PEERS))],
        [ANY, VMEM, VMEM],
        [
            pltpu.VMEM((2, PLANE, LANES), f32),
            pltpu.VMEM((ROWS_UP * LANES, LANES), f32),
            pltpu.VMEM((DOWN * LEV + 8, COL), f32),
            pltpu.VMEM((2 * PAD_ROWS, LANES), f32),
            pltpu.VMEM((2 * PAD_ROWS, LANES), f32),
            pltpu.VMEM((2 * PAD_ROWS, LANES), f32),
            pltpu.VMEM((LEV, COL), f32),
            pltpu.VMEM((LEV, COL), f32),
            pltpu.VMEM((LEV, COL), f32),
            pltpu.SemaphoreType.DMA((2,)),
        ],
        "physics",
    )(device, cols, regime_row, *(hold(x) for x in (got, tiles, hot, parts, weights)))


def ocean(meta, back):
    return call(
        ocean_kernel, [VMEM, VMEM], [here((4, 4, LANES))] * 2, [VMEM] * 2, [], "ocean"
    )(hold(meta), hold(back))


def update(meta, back, tiles):
    return call(
        update_kernel,
        [VMEM] * 3,
        [far((PLANE, SLOTS))],
        [ANY],
        [
            pltpu.VMEM((ROWS_UP * LANES + 16, LANES), f32),
            pltpu.VMEM((CAP, PLANE, LANES), f32),
            pltpu.SemaphoreType.DMA((CAP,)),
        ],
        "update",
    )(hold(meta), hold(back), hold(tiles))[0]


def exchange(sent, rows):
    got = lax.all_to_all(
        sent.reshape(PEERS, 1, rows * LANES), ("node", "dev"), 0, 0, tiled=True
    )
    return got.reshape(PEERS * rows, LANES)


def local(state, span_owner, regime, moments, remap_weights, remap_rows, remap_cols):
    dev_count = lax.axis_size("dev")
    device = lax.axis_index(("node", "dev")).astype(jnp.int32).reshape(1)
    owner_row = span_owner.reshape(1, COL)
    regime_row = regime.reshape(1, COL)
    sent = pack(remap_rows, owner_row, moments)
    tiles, hot, parts, mom_tiles, weights = prepare(
        owner_row,
        regime_row,
        state.reshape(PLANE, COL),
        moments.reshape(PLANE, SLOTS),
        remap_weights,
    )
    got = exchange(sent, ROWS1)
    tend, sent, meta = physics(device, remap_cols, regime_row, got, tiles, hot, parts, weights)
    back = exchange(sent, ROWS2)
    keep, send = ocean(meta, back)
    other = lax.ppermute(send, "dev", [(i, i ^ 1) for i in range(dev_count)])
    new_mom = update(meta, back, mom_tiles)
    return tend.reshape(LEV, FLD, COL), new_mom.reshape(LEV, FLD, SLOTS), keep + other


def solution(mesh):
    return jax.shard_map(
        local,
        mesh=mesh,
        in_specs=(
            P(None, None, ("node", "dev")),
            P(("node", "dev"), None),
            P(("node", "dev")),
            P(None, None, ("node", "dev")),
            P(("node", "dev"), None, None),
            P(("node", "dev")),
            P(("node", "dev")),
        ),
        out_specs=(
            P(None, None, ("node", "dev")),
            P(None, None, ("node", "dev")),
            P(("node", "dev"), None, None),
        ),
        check_vma=False,
    )
```

```python
import jax
import jax.numpy as jnp
from jax import lax
from jax.experimental import pallas as pl
from jax.experimental.pallas import tpu as pltpu
from jax.sharding import PartitionSpec as P

LEV = 72
FLD = 8
PEERS = 128
LANES = 128
CAP = 4
COL = 256
SLOTS = CAP * PEERS
DOWN = 2
UP = 4
ROWS1 = 5
META = CAP * DOWN * LEV
ROWS_UP = CAP * UP * LEV // LANES
OCN_ROWS = 8
ROWS2 = ROWS_UP + OCN_ROWS
HALF = LEV // 2
PAD_ROWS = LEV * FLD + FLD
PARTS = 9
f32 = jnp.float32
bf16 = jnp.bfloat16


def iota(shape, axis):
    return lax.broadcasted_iota(jnp.int32, shape, axis)


def split2(x):
    hi = x.astype(bf16)
    return hi, (x - hi.astype(f32)).astype(bf16)


def columns_down(owner_row):
    real = owner_row.astype(f32)
    parts = [
        jnp.broadcast_to(real[:, h * LANES : (h + 1) * LANES], (LANES, LANES)).T
        for h in range(COL // LANES)
    ]
    return jnp.concatenate(parts, axis=0)


def pack_kernel(
    rows_hbm, owner_hbm, mom_ref, out_ref, rows_ref, owner_ref, block_ref, sem, small_sem
):
    small = [
        pltpu.make_async_copy(owner_hbm, owner_ref, small_sem.at[0]),
        pltpu.make_async_copy(rows_hbm, rows_ref, small_sem.at[1]),
    ]
    copies = []
    for p in range(CAP):
        for at, moment in enumerate((0, 2)):
            copies.append(
                pltpu.make_async_copy(
                    mom_ref.at[:, moment, pl.ds(p * LANES, LANES)],
                    block_ref.at[pl.ds((p * DOWN + at) * LEV, LEV), :],
                    sem.at[p, at],
                )
            )
    for copy in small + copies:
        copy.start()
    for copy in small:
        copy.wait()
    owner_down = columns_down(owner_ref[...])
    peer = iota((COL, LANES), 1).astype(f32)
    count = jnp.sum((owner_down == peer).astype(f32), axis=0, keepdims=True)
    tail = ROWS1 * LANES - META
    which = iota((tail, LANES), 0)
    meta = jnp.where(which == 4, jnp.broadcast_to(count, (tail, LANES)), 0.0)
    for n in range(4):
        meta = jnp.where(which == n, rows_ref[n].astype(f32), meta)
    block_ref[META:, :] = meta
    for copy in copies:
        copy.wait()
    for t in range(ROWS1):
        out_ref[pl.ds(t, PEERS, stride=ROWS1), :] = block_ref[t * LANES : (t + 1) * LANES, :].T


def softplus(x):
    return jnp.maximum(x, 0.0) + jnp.log(1.0 + jnp.exp(-jnp.abs(x)))


def rain_fall(rain, above, top):
    rain_q = softplus(rain)
    falling = 0.5 * rain_q
    rolled = pltpu.roll(falling, 1, 0)
    return rain_q, rain + 0.5 * (jnp.where(top, above, rolled) - falling), rolled


def micro_free(x, rain_q, warm, mixed, icy):
    temper, vap, liq, rain, ice = x
    vapour = softplus(vap)
    liquid = softplus(liq)
    ice_q = softplus(ice)
    half_t = jnp.tanh(0.5 * temper)
    satur = 0.6 * jnp.exp(0.5 * half_t)
    excess = vapour - satur
    autoconv = 0.3 * liquid * liquid / (1.0 + liquid)
    evapor = 0.1 * rain_q * (0.5 - 0.5 * jnp.tanh(0.5 * excess))
    freeze = 0.3 * liquid * (0.5 - 0.5 * half_t)
    melting = 0.2 * ice_q * (0.5 + 0.5 * half_t)
    aggreg = 0.25 * ice_q * ice_q / (1.0 + ice_q)
    source = jnp.where(
        icy, 0.175 * jnp.tanh(vapour - 0.8 * satur), 0.2 * jnp.tanh(excess)
    )

    def pick(a, b, c):
        return jnp.where(warm, a, jnp.where(mixed, b, c))

    swap = freeze - melting
    kept = (
        temper + pick(-0.4 * evapor, 0.25 * swap, 0.25 * freeze),
        jnp.where(warm, vap + 0.5 * evapor, vap),
        liq - 0.5 * pick(autoconv, freeze + autoconv, freeze),
        rain + 0.5 * pick(autoconv - evapor, autoconv + melting, aggreg),
        jnp.where(warm, ice, ice + 0.5 * jnp.where(mixed, swap, freeze - aggreg)),
    )
    return kept, source, excess


def micro_bound(kept, source, excess, m2, icy):
    temper, vap, liq, rain, ice = kept
    gain = source * (1.0 + 0.5 * jnp.tanh(0.5 * (m2 + excess)))
    return (
        temper + jnp.where(icy, gain, 0.8 * gain),
        vap - gain,
        jnp.where(icy, liq, liq + gain),
        rain,
        jnp.where(icy, ice + gain, ice),
    )


def solve(a_ref, k_ref, c_ref, y_ref, g_ref):
    halves = range(COL // LANES)

    def row(ref, h, level):
        one = ref[level : level + 1, h * LANES : (h + 1) * LANES]
        return jnp.broadcast_to(one, (FLD, LANES))

    def rows(h, level):
        first = h * PAD_ROWS + level * FLD
        return slice(first, first + FLD)

    def base(h, chain, step):
        return row(c_ref, h, LEV - 1 - step if chain else step)

    def link(h, chain, step):
        return row(k_ref, h, LEV - 1 - step if chain else step - 1)

    def finish(h, chain, step, r):
        k = LEV - 1 - step if chain else step
        d = a_ref[rows(h, k), :] * r
        if step > 0:
            d = d + (link(h, chain, step) * r) * last_d[h, chain]
        g = row(k_ref, h, k - 1 if chain else k) * r
        g_ref[rows(h, k), :] = g
        y_ref[rows(h, k), :] = d
        last_d[h, chain] = d
        last_g[h, chain] = g

    chains = [(h, chain) for h in halves for chain in range(2)]
    den, last_d, last_g = {}, {}, {}
    for at in chains:
        den[at] = base(*at, 0)
        finish(*at, 0, 1.0 / den[at])
    for step in range(1, HALF, 2):
        for at in chains:
            old = den[at]
            k = link(*at, step)
            r = 1.0 / (base(*at, step) * old - k * k)
            if step + 1 < HALF:
                k = link(*at, step + 1)
                den[at] = base(*at, step + 1) - (k * k * old) * r
            finish(*at, step, old * r)
            if step + 1 < HALF:
                finish(*at, step + 1, 1.0 / den[at])
    z = {}
    for h in halves:
        d_up, d_dn = last_d[h, 0], last_d[h, 1]
        g_up, g_dn = last_g[h, 0], last_g[h, 1]
        z[h, 0] = (d_up + g_up * d_dn) / (1.0 - g_up * g_dn)
        z[h, 1] = d_dn + g_dn * z[h, 0]
        y_ref[rows(h, HALF - 1), :] = z[h, 0]
        y_ref[rows(h, HALF), :] = z[h, 1]
    for step in range(1, HALF):
        for h in halves:
            for chain in range(2):
                k = HALF + step if chain else HALF - 1 - step
                z[h, chain] = y_ref[rows(h, k), :] + g_ref[rows(h, k), :] * z[h, chain]
                y_ref[rows(h, k), :] = z[h, chain]


def regimes(regime_ref, h):
    kind = jnp.broadcast_to(regime_ref[:, h * LANES : (h + 1) * LANES], (8, LANES))
    return kind == 0, kind == 1, kind == 2


def prepare_kernel(
    owner_ref, regime_ref, state_ref, mom_ref, weight_ref,
    tile_ref, hot_ref, part_ref, mom_tile_ref, weight_part_ref,
    weight_own, sem, mom_sem, weight_sem,
):
    copies = [
        pltpu.make_async_copy(
            state_ref.at[:, pl.ds(h * LANES, LANES)], tile_ref.at[h], sem.at[h]
        )
        for h in range(COL // LANES)
    ]
    weights = pltpu.make_async_copy(weight_ref, weight_own, weight_sem)
    moments = [
        pltpu.make_async_copy(
            mom_ref.at[:, pl.ds(p * LANES, LANES)], mom_tile_ref.at[p], mom_sem.at[p]
        )
        for p in range(CAP)
    ]
    for copy in copies + [weights] + moments:
        copy.start()
    owner_row = owner_ref[...]
    owner_down = columns_down(owner_row)
    owner_real = owner_row.astype(f32)
    before = jnp.zeros((1, COL), f32)
    for h in range(COL // LANES):
        same = (
            jnp.concatenate([owner_down[h * LANES : (h + 1) * LANES, :]] * 2, axis=1) == owner_real
        )
        earlier = iota((LANES, COL), 0) + h * LANES < iota((LANES, COL), 1)
        before = before + jnp.sum((same & earlier).astype(f32), axis=0, keepdims=True)
    slot = owner_row + PEERS * before.astype(jnp.int32)
    for p in range(CAP):
        hot_ref[p * PEERS : (p + 1) * PEERS, :] = (
            iota((PEERS, COL), 0) + p * PEERS == slot
        ).astype(bf16)
    top = iota((8, LANES), 0) == 0
    for h in range(COL // LANES):
        copies[h].wait()
        warm, mixed, icy = regimes(regime_ref, h)
        above = [jnp.zeros((8, LANES), f32)] * 2
        for i in range(LEV // 8):
            x = [tile_ref[h, pl.ds(i * 64 + f, 8, stride=FLD), :] for f in range(7)]
            rain_q, x[3], above[0] = rain_fall(x[3], above[0], top)
            kept, source, excess = micro_free(x[:5], rain_q, warm, mixed, icy)
            rain_q, rain, above[1] = rain_fall(kept[3], above[1], top)
            shear = None
            for f in (5, 6):
                if i < LEV // 8 - 1:
                    below = tile_ref[h, pl.ds(i * 64 + FLD + f, 8, stride=FLD), :]
                else:
                    below = pltpu.roll(x[f], 7, 0)
                square = (x[f] - below) * (x[f] - below)
                shear = square if shear is None else shear + square
            shear = 1.5 * shear / (1.0 + shear)
            values = kept[:3] + (rain, kept[4], source, excess, rain_q, shear)
            for f, value in enumerate(values):
                part_ref[h, f, i * 8 : i * 8 + 8, :] = value
    weights.wait()
    for n in range(4):
        down, across = (n % 2) * LANES, (n // 2) * LANES
        for at, part in enumerate(split2(weight_own[n])):
            weight_part_ref[at, down : down + LANES, across : across + LANES] = part
    for copy in moments:
        copy.wait()


def physics_kernel(
    device_ref,
    cols_ref,
    regime_ref,
    got_ref,
    tile_ref,
    hot_ref,
    part_ref,
    weight_ref,
    tend_out,
    out_ref,
    meta_ref,
    tend_ref,
    block_ref,
    mom_ref,
    a_ref,
    y_ref,
    g_ref,
    k_ref,
    c_ref,
    e_ref,
    tend_sem,
):
    for t in range(ROWS1):
        block_ref[t * LANES : (t + 1) * LANES, :] = got_ref[pl.ds(t, PEERS, stride=ROWS1), :].T
    device = device_ref[0]
    core = device % 2
    meta_ref[0:2, :] = jnp.where(
        core == 1, block_ref[META + 2 : META + 4, :], block_ref[META : META + 2, :]
    )
    meta_ref[2:3, :] = jnp.full((1, PEERS), (device * 4).astype(f32))
    meta_ref[3:4, :] = jnp.full((1, PEERS), ((device + 1 - 2 * core) * 4).astype(f32))
    meta_ref[4:8, :] = block_ref[META + 4 : META + 8, :]
    slotted = jnp.concatenate(
        [block_ref[p * DOWN * LEV : (p + 1) * DOWN * LEV, :] for p in range(CAP)], axis=1
    )
    total = None
    for part in split2(slotted):
        got = jnp.dot(part, hot_ref[...], preferred_element_type=f32)
        total = got if total is None else total + got
    mom_ref[0 : DOWN * LEV, :] = total

    top = iota((8, LANES), 0) == 0
    for h in range(COL // LANES):
        lanes = slice(h * LANES, (h + 1) * LANES)
        warm, mixed, icy = regimes(regime_ref, h)
        base = h * PAD_ROWS
        for i in range(LEV // 8):
            m2 = mom_ref[LEV + i * 8 : LEV + i * 8 + 8, lanes]
            first = tuple(part_ref[h, f, i * 8 : i * 8 + 8, :] for f in range(8))
            x = micro_bound(first[:5], first[5], first[6], m2, icy)
            kept, source, excess = micro_free(x, first[7], warm, mixed, icy)
            x = micro_bound(kept, source, excess, m2, icy)
            for f, value in enumerate(x):
                a_ref[pl.ds(base + i * 64 + f, 8, stride=FLD), :] = value
            for f in range(5, FLD):
                a_ref[pl.ds(base + i * 64 + f, 8, stride=FLD), :] = tile_ref[
                    h, pl.ds(i * 64 + f, 8, stride=FLD), :
                ]
        for ref in (a_ref, y_ref):
            ref[base + LEV * FLD : base + PAD_ROWS, :] = jnp.zeros((FLD, LANES), f32)
    last = iota((8, COL), 0) == 7
    for i in range(LEV // 8):
        m0 = mom_ref[i * 8 : i * 8 + 8, :]
        m0_next = mom_ref[i * 8 + 1 : i * 8 + 9, :]
        energy = 30.5 + 30.0 * jnp.tanh(m0 + m0_next)
        if i == LEV // 8 - 1:
            energy = jnp.where(last, 0.0, energy)
        e_ref[i * 8 : i * 8 + 8, :] = energy
    for turn in range(3):
        src = a_ref if turn == 0 else y_ref
        for h in range(COL // LANES):
            lanes = slice(h * LANES, (h + 1) * LANES)
            above = jnp.zeros((8, LANES), f32)
            for i in range(LEV // 8):

                def drop(f):
                    first = h * PAD_ROWS + i * 64 + f
                    return (
                        src[pl.ds(first, 8, stride=FLD), :]
                        - src[pl.ds(first + FLD, 8, stride=FLD), :]
                    )

                if turn == 0:
                    shear = part_ref[h, 8, i * 8 : i * 8 + 8, :]
                else:
                    du, dv = drop(5), drop(6)
                    shear = du * du + dv * dv
                    shear = 1.5 * shear / (1.0 + shear)
                mixing = 0.3 + shear * (0.5 - 0.5 * jnp.tanh(drop(0)))
                kappa = mixing * e_ref[i * 8 : i * 8 + 8, lanes]
                rolled = pltpu.roll(kappa, 1, 0)
                k_ref[i * 8 : i * 8 + 8, lanes] = kappa
                c_ref[i * 8 : i * 8 + 8, lanes] = 1.0 + kappa + jnp.where(top, above, rolled)
                above = rolled
        solve(a_ref, k_ref, c_ref, y_ref, g_ref)

    field = iota((FLD, LANES), 0)
    kept = (field >= 2) & (field <= 4)
    bottom = []
    for h in range(COL // LANES):
        level = slice((LEV - 1) * FLD, LEV * FLD)
        at = slice(h * PAD_ROWS + (LEV - 1) * FLD, h * PAD_ROWS + LEV * FLD)
        old = tile_ref[h, level, :]
        bottom.append(old + (jnp.where(kept, a_ref[at, :], y_ref[at, :]) - old))
    b = jnp.concatenate(bottom, axis=1)
    b0, b3, b5, b6 = (b[f : f + 1, :] for f in (0, 3, 5, 6))
    wind = jnp.sqrt(1.0 + b5 * b5 + b6 * b6)
    flux = jnp.concatenate(
        [
            -0.5 * wind * b5,
            -0.5 * wind * b6,
            0.5 * softplus(b3),
            -0.3 * wind * b0,
            jnp.zeros((4, COL), f32),
        ],
        axis=0,
    )
    none = jnp.zeros((FLD, LANES), f32)
    used = []
    for n in range(4):
        mine = jnp.where(cols_ref[n] == 0, flux[:, :LANES], flux[:, LANES:])
        used.append(jnp.concatenate([none, mine] if n % 2 else [mine, none], axis=1))
    hi, low = split2(jnp.concatenate(used, axis=0))

    def weighted(parts, at):
        got = jnp.dot(
            jnp.concatenate(parts, axis=0), weight_ref[at], preferred_element_type=f32
        )
        total = got[0:32, :]
        for i in range(1, len(parts)):
            total = total + got[i * 32 : i * 32 + 32, :]
        return total

    products = weighted([hi], 1) + weighted([hi, low], 0)
    odd = iota((PEERS, LANES), 0) % 2 == 1
    for n in range(2):
        for e in range(4):
            even_row = products[n * 8 + e : n * 8 + e + 1, 0:LANES]
            odd_row = products[n * 8 + 16 + e : n * 8 + 17 + e, LANES:]
            out_ref[pl.ds(ROWS_UP + 4 * n + e, PEERS, stride=ROWS2), :] = jnp.where(
                odd, odd_row, even_row
            )

    copies = []
    for h in range(COL // LANES):
        for k in range(LEV):
            rows = slice(k * FLD, (k + 1) * FLD)
            at = slice(h * PAD_ROWS + k * FLD, h * PAD_ROWS + (k + 1) * FLD)
            mixed_state = jnp.where(kept, a_ref[at, :], y_ref[at, :])
            tend_ref[h, rows, :] = mixed_state - tile_ref[h, rows, :]
        copies.append(
            pltpu.make_async_copy(
                tend_ref.at[h], tend_out.at[:, pl.ds(h * LANES, LANES)], tend_sem.at[h]
            )
        )
        copies[-1].start()

    fields = jnp.concatenate(
        [
            jnp.concatenate(
                [y_ref[pl.ds(h * PAD_ROWS + f, LEV, stride=FLD), :] for f in (0, 1, 5, 6)], axis=0
            )
            for h in range(COL // LANES)
        ],
        axis=1,
    )
    parts = split2(fields)
    sent = 0
    for pair in range(CAP // 2):
        hot = hot_ref[pair * 2 * PEERS : (pair + 1) * 2 * PEERS, :]
        total = None
        for part in parts:
            got = lax.dot_general(
                part, hot, (((1,), (1,)), ((), ())), preferred_element_type=f32
            )
            total = got if total is None else total + got
        for q in range(2):
            first = (pair * 2 + q) * UP * LEV
            block_ref[first : first + UP * LEV, :] = total[:, q * PEERS : (q + 1) * PEERS]
        ready = (pair + 1) * 2 * UP * LEV // LANES
        for t in range(sent, ready):
            out_ref[pl.ds(t, PEERS, stride=ROWS2), :] = block_ref[
                t * LANES : (t + 1) * LANES, :
            ].T
        sent = ready
    for copy in copies:
        copy.wait()


def ocean_kernel(meta_ref, got_ref, keep_ref, send_ref):
    row = iota((8, PEERS), 0).astype(f32)
    wanted = jnp.where(row < 3.5, meta_ref[2:3, :] + row, meta_ref[3:4, :] + (row - 4.0))
    chosen = jnp.concatenate(
        [(meta_ref[n : n + 1, :] == wanted).astype(bf16) for n in range(2)], axis=1
    )
    values = jnp.concatenate(
        [
            jnp.concatenate(
                [
                    got_ref[pl.ds(ROWS_UP + 4 * n + e, PEERS, stride=ROWS2), :]
                    for e in range(4)
                ],
                axis=1,
            )
            for n in range(2)
        ],
        axis=0,
    )
    total = None
    for part in split2(values):
        got = jnp.dot(chosen, part, preferred_element_type=f32)
        total = got if total is None else total + got
    for e in range(4):
        part = total[:, e * LANES : (e + 1) * LANES]
        keep_ref[:, e, :] = part[0:4, :]
        send_ref[:, e, :] = part[4:8, :]


def update_kernel(meta_ref, got_ref, tile_ref, out_ref, block_ref, new_ref, sem):
    count = meta_ref[4:5, :]
    unpacked = 0
    top = iota((8, LANES), 0) == 0
    last = iota((8, LANES), 0) == 7
    copies = []
    for p in range(CAP):
        needed = -(-(p + 1) * UP * LEV // LANES)
        for t in range(unpacked, needed):
            block_ref[8 + t * LANES : 8 + (t + 1) * LANES, :] = got_ref[
                pl.ds(t, PEERS, stride=ROWS2), :
            ].T
        unpacked = needed
        live = jnp.broadcast_to(count, (8, LANES)) > p + 0.5
        for i in range(LEV // 8):

            def grad(which):
                first = 8 + (p * UP + which) * LEV + i * 8
                prev = block_ref[first - 1 : first + 7, :]
                after = block_ref[first + 1 : first + 9, :]
                if i == 0:
                    prev = jnp.where(top, block_ref[first : first + 8, :], prev)
                if i == LEV // 8 - 1:
                    after = jnp.where(last, block_ref[first : first + 8, :], after)
                return prev - after

            gt, gq, gu, gv = (grad(which) for which in range(UP))
            production = (
                gu * gu + gv * gv, gt * gt, gq * gq, gt * gq, gu * gt, gv * gt, gu * gq, gu * gv,
            )
            for j in range(FLD):
                at = pl.ds(i * 64 + j, 8, stride=FLD)
                m = tile_ref[p, at, :]
                new = m + 0.5 * (jnp.tanh(production[j]) - (0.3 + 0.1 * j) * m)
                new_ref[p, at, :] = jnp.where(live, new, m)
        copies.append(
            pltpu.make_async_copy(
                new_ref.at[p], out_ref.at[:, pl.ds(p * LANES, LANES)], sem.at[p]
            )
        )
        copies[-1].start()
    for copy in copies:
        copy.wait()


SMEM = pl.BlockSpec(memory_space=pltpu.SMEM)
VMEM = pl.BlockSpec(memory_space=pltpu.VMEM)
ANY = pl.BlockSpec(memory_space=pl.ANY)
HBM = pl.BlockSpec(memory_space=pltpu.HBM)
PLANE = LEV * FLD
VMEM_LIMIT = 16 << 20


def here(shape, dtype=f32):
    return pltpu.VMEM(shape, dtype)


def far(shape):
    return jax.ShapeDtypeStruct(shape, f32)


def hold(x):
    return pltpu.with_memory_space_constraint(x, pltpu.VMEM)


def outside(x):
    return pltpu.with_memory_space_constraint(x, pltpu.HBM)


def call(kernel, ins, outs, out_specs, scratch, name):
    return pl.pallas_call(
        kernel,
        in_specs=ins,
        out_specs=out_specs,
        out_shape=outs,
        scratch_shapes=scratch,
        name=name,
        compiler_params=pltpu.CompilerParams(vmem_limit_bytes=VMEM_LIMIT),
    )


def pack(rows, owner_row, mom):
    return call(
        pack_kernel,
        [HBM] * 3,
        [here((ROWS1 * PEERS, LANES))],
        [VMEM],
        [
            pltpu.SMEM((4,), jnp.int32),
            pltpu.VMEM((1, COL), jnp.int32),
            pltpu.VMEM((ROWS1 * LANES, LANES), f32),
            pltpu.SemaphoreType.DMA((CAP, DOWN)),
            pltpu.SemaphoreType.DMA((2,)),
        ],
        "pack",
    )(outside(rows), outside(owner_row), outside(mom))[0]


def prepare(owner_row, regime_row, state, mom, weights):
    return call(
        prepare_kernel,
        [VMEM] * 2 + [HBM] * 3,
        [
            here((2, PLANE, LANES)),
            here((SLOTS, COL), bf16),
            here((2, PARTS, LEV, LANES)),
            here((CAP, PLANE, LANES)),
            here((2, 2 * LANES, 2 * LANES), bf16),
        ],
        [VMEM] * 5,
        [
            pltpu.VMEM((4, LANES, LANES), f32),
            pltpu.SemaphoreType.DMA((2,)),
            pltpu.SemaphoreType.DMA((CAP,)),
            pltpu.SemaphoreType.DMA,
        ],
        "prepare",
    )(owner_row, regime_row, outside(state), outside(mom), outside(weights))


def physics(device, cols, regime_row, got, tiles, hot, parts, weights):
    return call(
        physics_kernel,
        [SMEM] * 2 + [VMEM] * 6,
        [far((PLANE, COL)), here((ROWS2 * PEERS, LANES)), here((8, PEERS))],
        [ANY, VMEM, VMEM],
        [
            pltpu.VMEM((2, PLANE, LANES), f32),
            pltpu.VMEM((ROWS_UP * LANES, LANES), f32),
            pltpu.VMEM((DOWN * LEV + 8, COL), f32),
            pltpu.VMEM((2 * PAD_ROWS, LANES), f32),
            pltpu.VMEM((2 * PAD_ROWS, LANES), f32),
            pltpu.VMEM((2 * PAD_ROWS, LANES), f32),
            pltpu.VMEM((LEV, COL), f32),
            pltpu.VMEM((LEV, COL), f32),
            pltpu.VMEM((LEV, COL), f32),
            pltpu.SemaphoreType.DMA((2,)),
        ],
        "physics",
    )(device, cols, regime_row, *(hold(x) for x in (got, tiles, hot, parts, weights)))


def ocean(meta, back):
    return call(
        ocean_kernel, [VMEM, VMEM], [here((4, 4, LANES))] * 2, [VMEM] * 2, [], "ocean"
    )(hold(meta), hold(back))


def update(meta, back, tiles):
    return call(
        update_kernel,
        [VMEM] * 3,
        [far((PLANE, SLOTS))],
        [ANY],
        [
            pltpu.VMEM((ROWS_UP * LANES + 16, LANES), f32),
            pltpu.VMEM((CAP, PLANE, LANES), f32),
            pltpu.SemaphoreType.DMA((CAP,)),
        ],
        "update",
    )(hold(meta), hold(back), hold(tiles))[0]


def exchange(sent, rows):
    got = lax.all_to_all(
        sent.reshape(PEERS, 1, rows * LANES), ("node", "dev"), 0, 0, tiled=True
    )
    return got.reshape(PEERS * rows, LANES)


def local(state, span_owner, regime, moments, remap_weights, remap_rows, remap_cols):
    dev_count = lax.axis_size("dev")
    device = lax.axis_index(("node", "dev")).astype(jnp.int32).reshape(1)
    owner_row = span_owner.reshape(1, COL)
    regime_row = regime.reshape(1, COL)
    sent = pack(remap_rows, owner_row, moments)
    tiles, hot, parts, mom_tiles, weights = prepare(
        owner_row,
        regime_row,
        state.reshape(PLANE, COL),
        moments.reshape(PLANE, SLOTS),
        remap_weights,
    )
    got = exchange(sent, ROWS1)
    tend, sent, meta = physics(device, remap_cols, regime_row, got, tiles, hot, parts, weights)
    back = exchange(sent, ROWS2)
    keep, send = ocean(meta, back)
    other = lax.ppermute(send, "dev", [(i, i ^ 1) for i in range(dev_count)])
    new_mom = update(meta, back, mom_tiles)
    return tend.reshape(LEV, FLD, COL), new_mom.reshape(LEV, FLD, SLOTS), keep + other


def solution(mesh):
    return jax.shard_map(
        local,
        mesh=mesh,
        in_specs=(
            P(None, None, ("node", "dev")),
            P(("node", "dev"), None),
            P(("node", "dev")),
            P(None, None, ("node", "dev")),
            P(("node", "dev"), None, None),
            P(("node", "dev")),
            P(("node", "dev")),
        ),
        out_specs=(
            P(None, None, ("node", "dev")),
            P(None, None, ("node", "dev")),
            P(("node", "dev"), None, None),
        ),
        check_vma=False,
    )
```

```python
import jax
import jax.numpy as jnp
from jax import lax
from jax.experimental import pallas as pl
from jax.experimental.pallas import tpu as pltpu
from jax.sharding import PartitionSpec as P

LEV = 72
FLD = 8
PEERS = 128
LANES = 128
CAP = 4
COL = 256
SLOTS = CAP * PEERS
DOWN = 2
UP = 4
ROWS1 = 5
META = CAP * DOWN * LEV
ROWS_UP = CAP * UP * LEV // LANES
OCN_ROWS = 4
GROUP = 4
ROWS2 = ROWS_UP + OCN_ROWS
HALF = LEV // 2
PITCH = 9
PAD_ROWS = 664
PARTS = 9
f32 = jnp.float32
bf16 = jnp.bfloat16


def iota(shape, axis):
    return lax.broadcasted_iota(jnp.int32, shape, axis)


def split2(x):
    hi = x.astype(bf16)
    return hi, (x - hi.astype(f32)).astype(bf16)


def columns_down(owner_row):
    real = owner_row.astype(f32)
    parts = [
        jnp.broadcast_to(real[:, h * LANES : (h + 1) * LANES], (LANES, LANES)).T
        for h in range(COL // LANES)
    ]
    return jnp.concatenate(parts, axis=0)


def pack_kernel(
    rows_hbm, owner_hbm, mom_ref, out_ref, rows_ref, owner_ref, block_ref, sem, small_sem
):
    small = [
        pltpu.make_async_copy(owner_hbm, owner_ref, small_sem.at[0]),
        pltpu.make_async_copy(rows_hbm, rows_ref, small_sem.at[1]),
    ]
    copies = []
    for p in range(CAP):
        for at, moment in enumerate((0, 2)):
            copies.append(
                pltpu.make_async_copy(
                    mom_ref.at[:, moment, pl.ds(p * LANES, LANES)],
                    block_ref.at[pl.ds((p * DOWN + at) * LEV, LEV), :],
                    sem.at[p, at],
                )
            )
    for copy in small + copies:
        copy.start()
    for copy in small:
        copy.wait()
    owner_down = columns_down(owner_ref[...])
    peer = iota((COL, LANES), 1).astype(f32)
    count = jnp.sum((owner_down == peer).astype(f32), axis=0, keepdims=True)
    tail = ROWS1 * LANES - META
    which = iota((tail, LANES), 0)
    meta = jnp.where(which == 4, jnp.broadcast_to(count, (tail, LANES)), 0.0)
    for n in range(4):
        meta = jnp.where(which == n, rows_ref[n].astype(f32), meta)
    block_ref[META:, :] = meta
    for copy in copies:
        copy.wait()
    for t in range(ROWS1):
        out_ref[pl.ds(t, PEERS, stride=ROWS1), :] = block_ref[t * LANES : (t + 1) * LANES, :].T


def softplus(x):
    return jnp.maximum(x, 0.0) + jnp.log(1.0 + jnp.exp(-jnp.abs(x)))


def rain_fall(rain, above, top):
    rain_q = softplus(rain)
    falling = 0.5 * rain_q
    rolled = pltpu.roll(falling, 1, 0)
    return rain_q, rain + 0.5 * (jnp.where(top, above, rolled) - falling), rolled


def micro_free(x, rain_q, warm, mixed, icy):
    temper, vap, liq, rain, ice = x
    vapour = softplus(vap)
    liquid = softplus(liq)
    ice_q = softplus(ice)
    half_t = jnp.tanh(0.5 * temper)
    satur = 0.6 * jnp.exp(0.5 * half_t)
    excess = vapour - satur
    autoconv = 0.3 * liquid * liquid / (1.0 + liquid)
    evapor = 0.1 * rain_q * (0.5 - 0.5 * jnp.tanh(0.5 * excess))
    freeze = 0.3 * liquid * (0.5 - 0.5 * half_t)
    melting = 0.2 * ice_q * (0.5 + 0.5 * half_t)
    aggreg = 0.25 * ice_q * ice_q / (1.0 + ice_q)
    source = jnp.where(
        icy, 0.175 * jnp.tanh(vapour - 0.8 * satur), 0.2 * jnp.tanh(excess)
    )

    def pick(a, b, c):
        return jnp.where(warm, a, jnp.where(mixed, b, c))

    swap = freeze - melting
    kept = (
        temper + pick(-0.4 * evapor, 0.25 * swap, 0.25 * freeze),
        jnp.where(warm, vap + 0.5 * evapor, vap),
        liq - 0.5 * pick(autoconv, freeze + autoconv, freeze),
        rain + 0.5 * pick(autoconv - evapor, autoconv + melting, aggreg),
        jnp.where(warm, ice, ice + 0.5 * jnp.where(mixed, swap, freeze - aggreg)),
    )
    return kept, source, excess


def micro_bound(kept, source, excess, m2, icy):
    temper, vap, liq, rain, ice = kept
    gain = source * (1.0 + 0.5 * jnp.tanh(0.5 * (m2 + excess)))
    return (
        temper + jnp.where(icy, gain, 0.8 * gain),
        vap - gain,
        jnp.where(icy, liq, liq + gain),
        rain,
        jnp.where(icy, ice + gain, ice),
    )


def solve(a_ref, k_ref, c_ref, y_ref, g_ref):
    halves = range(COL // LANES)

    def row(ref, h, level):
        one = ref[level : level + 1, h * LANES : (h + 1) * LANES]
        return jnp.broadcast_to(one, (FLD, LANES))

    def rows(h, level):
        first = h * PAD_ROWS + level * PITCH
        return slice(first, first + FLD)

    def base(h, chain, step):
        return row(c_ref, h, LEV - 1 - step if chain else step)

    def link(h, chain, step):
        return row(k_ref, h, LEV - 1 - step if chain else step - 1)

    def finish(h, chain, step, r):
        k = LEV - 1 - step if chain else step
        d = a_ref[rows(h, k), :] * r
        if step > 0:
            d = d + (link(h, chain, step) * r) * last_d[h, chain]
        g = row(k_ref, h, k - 1 if chain else k) * r
        g_ref[rows(h, k), :] = g
        y_ref[rows(h, k), :] = d
        last_d[h, chain] = d
        last_g[h, chain] = g

    chains = [(h, chain) for h in halves for chain in range(2)]
    den, last_d, last_g = {}, {}, {}
    for at in chains:
        den[at] = base(*at, 0)
        finish(*at, 0, 1.0 / den[at])
    for step in range(1, HALF, 2):
        for at in chains:
            old = den[at]
            k = link(*at, step)
            r = 1.0 / (base(*at, step) * old - k * k)
            if step + 1 < HALF:
                k = link(*at, step + 1)
                den[at] = base(*at, step + 1) - (k * k * old) * r
            finish(*at, step, old * r)
            if step + 1 < HALF:
                finish(*at, step + 1, 1.0 / den[at])
    z = {}
    for h in halves:
        d_up, d_dn = last_d[h, 0], last_d[h, 1]
        g_up, g_dn = last_g[h, 0], last_g[h, 1]
        z[h, 0] = (d_up + g_up * d_dn) / (1.0 - g_up * g_dn)
        z[h, 1] = d_dn + g_dn * z[h, 0]
        y_ref[rows(h, HALF - 1), :] = z[h, 0]
        y_ref[rows(h, HALF), :] = z[h, 1]
    for step in range(1, HALF):
        for h in halves:
            for chain in range(2):
                k = HALF + step if chain else HALF - 1 - step
                z[h, chain] = y_ref[rows(h, k), :] + g_ref[rows(h, k), :] * z[h, chain]
                y_ref[rows(h, k), :] = z[h, chain]


def regimes(regime_ref, h):
    kind = jnp.broadcast_to(regime_ref[:, h * LANES : (h + 1) * LANES], (8, LANES))
    return kind == 0, kind == 1, kind == 2


def prepare_kernel(
    owner_ref, regime_ref, state_ref, mom_ref, weight_ref,
    tile_ref, hot_ref, part_ref, mom_tile_ref, weight_part_ref,
    weight_own, sem, mom_sem, weight_sem,
):
    copies = [
        pltpu.make_async_copy(
            state_ref.at[:, pl.ds(h * LANES, LANES)], tile_ref.at[h], sem.at[h]
        )
        for h in range(COL // LANES)
    ]
    weights = pltpu.make_async_copy(weight_ref, weight_own, weight_sem)
    moments = [
        pltpu.make_async_copy(
            mom_ref.at[:, pl.ds(p * LANES, LANES)], mom_tile_ref.at[p], mom_sem.at[p]
        )
        for p in range(CAP)
    ]
    for copy in copies + [weights] + moments:
        copy.start()
    owner_row = owner_ref[...]
    owner_down = columns_down(owner_row)
    owner_real = owner_row.astype(f32)
    before = jnp.zeros((1, COL), f32)
    for h in range(COL // LANES):
        same = (
            jnp.concatenate([owner_down[h * LANES : (h + 1) * LANES, :]] * 2, axis=1) == owner_real
        )
        earlier = iota((LANES, COL), 0) + h * LANES < iota((LANES, COL), 1)
        before = before + jnp.sum((same & earlier).astype(f32), axis=0, keepdims=True)
    slot = owner_row + PEERS * before.astype(jnp.int32)
    for p in range(CAP):
        hot_ref[p * PEERS : (p + 1) * PEERS, :] = (
            iota((PEERS, COL), 0) + p * PEERS == slot
        ).astype(bf16)
    top = iota((8, LANES), 0) == 0
    for h in range(COL // LANES):
        copies[h].wait()
        warm, mixed, icy = regimes(regime_ref, h)
        above = [jnp.zeros((8, LANES), f32)] * 2
        for i in range(LEV // 8):
            x = [tile_ref[h, pl.ds(i * 64 + f, 8, stride=FLD), :] for f in range(7)]
            rain_q, x[3], above[0] = rain_fall(x[3], above[0], top)
            kept, source, excess = micro_free(x[:5], rain_q, warm, mixed, icy)
            rain_q, rain, above[1] = rain_fall(kept[3], above[1], top)
            shear = None
            for f in (5, 6):
                if i < LEV // 8 - 1:
                    below = tile_ref[h, pl.ds(i * 64 + FLD + f, 8, stride=FLD), :]
                else:
                    below = pltpu.roll(x[f], 7, 0)
                square = (x[f] - below) * (x[f] - below)
                shear = square if shear is None else shear + square
            shear = 1.5 * shear / (1.0 + shear)
            values = kept[:3] + (rain, kept[4], source, excess, rain_q, shear)
            for f, value in enumerate(values):
                part_ref[h, f, i * 8 : i * 8 + 8, :] = value
    weights.wait()
    for n in range(4):
        down, across = (n % 2) * LANES, (n // 2) * LANES
        for at, part in enumerate(split2(weight_own[n])):
            weight_part_ref[at, down : down + LANES, across : across + LANES] = part
    for copy in moments:
        copy.wait()


def physics_kernel(
    device_ref,
    cols_ref,
    regime_ref,
    got_ref,
    tile_ref,
    hot_ref,
    part_ref,
    weight_ref,
    tend_out,
    out_ref,
    meta_ref,
    tend_ref,
    block_ref,
    mom_ref,
    a_ref,
    y_ref,
    g_ref,
    k_ref,
    c_ref,
    e_ref,
    tend_sem,
):
    for t in range(ROWS1):
        block_ref[t * LANES : (t + 1) * LANES, :] = got_ref[pl.ds(t, PEERS, stride=ROWS1), :].T
    device = device_ref[0]
    mine = device % GROUP
    picked = block_ref[META : META + 1, :]
    for n in range(1, 4):
        picked = jnp.where(mine == n, block_ref[META + n : META + n + 1, :], picked)
    meta_ref[0:1, :] = picked
    group = device - mine
    member = iota((16, PEERS), 0) // 4
    first_row = jnp.zeros((16, PEERS), f32)
    for flip in range(GROUP):
        partner = group + mine + flip - 2 * (mine & flip)
        first_row = jnp.where(member == flip, (partner * 4).astype(f32), first_row)
    meta_ref[8:24, :] = first_row + (iota((16, PEERS), 0) % 4).astype(f32)
    meta_ref[4:8, :] = block_ref[META + 4 : META + 8, :]
    slotted = jnp.concatenate(
        [block_ref[p * DOWN * LEV : (p + 1) * DOWN * LEV, :] for p in range(CAP)], axis=1
    )
    total = None
    for part in split2(slotted):
        got = jnp.dot(part, hot_ref[...], preferred_element_type=f32)
        total = got if total is None else total + got
    mom_ref[0 : DOWN * LEV, :] = total

    top = iota((8, LANES), 0) == 0
    for h in range(COL // LANES):
        lanes = slice(h * LANES, (h + 1) * LANES)
        warm, mixed, icy = regimes(regime_ref, h)
        base = h * PAD_ROWS
        for i in range(LEV // 8):
            m2 = mom_ref[LEV + i * 8 : LEV + i * 8 + 8, lanes]
            first = tuple(part_ref[h, f, i * 8 : i * 8 + 8, :] for f in range(8))
            x = micro_bound(first[:5], first[5], first[6], m2, icy)
            kept, source, excess = micro_free(x, first[7], warm, mixed, icy)
            x = micro_bound(kept, source, excess, m2, icy)
            for f, value in enumerate(x):
                a_ref[pl.ds(base + i * 8 * PITCH + f, 8, stride=PITCH), :] = value
            for f in range(5, FLD):
                a_ref[pl.ds(base + i * 8 * PITCH + f, 8, stride=PITCH), :] = tile_ref[
                    h, pl.ds(i * 64 + f, 8, stride=FLD), :
                ]
        for ref in (a_ref, y_ref):
            ref[base + LEV * PITCH : base + LEV * PITCH + FLD, :] = jnp.zeros((FLD, LANES), f32)
    last = iota((8, COL), 0) == 7
    for i in range(LEV // 8):
        m0 = mom_ref[i * 8 : i * 8 + 8, :]
        m0_next = mom_ref[i * 8 + 1 : i * 8 + 9, :]
        energy = 30.5 + 30.0 * jnp.tanh(m0 + m0_next)
        if i == LEV // 8 - 1:
            energy = jnp.where(last, 0.0, energy)
        e_ref[i * 8 : i * 8 + 8, :] = energy
    for turn in range(3):
        src = a_ref if turn == 0 else y_ref
        for h in range(COL // LANES):
            lanes = slice(h * LANES, (h + 1) * LANES)
            above = jnp.zeros((8, LANES), f32)
            for i in range(LEV // 8):

                def drop(f):
                    first = h * PAD_ROWS + i * 8 * PITCH + f
                    return (
                        src[pl.ds(first, 8, stride=PITCH), :]
                        - src[pl.ds(first + PITCH, 8, stride=PITCH), :]
                    )

                if turn == 0:
                    shear = part_ref[h, 8, i * 8 : i * 8 + 8, :]
                else:
                    du, dv = drop(5), drop(6)
                    shear = du * du + dv * dv
                    shear = 1.5 * shear / (1.0 + shear)
                mixing = 0.3 + shear * (0.5 - 0.5 * jnp.tanh(drop(0)))
                kappa = mixing * e_ref[i * 8 : i * 8 + 8, lanes]
                rolled = pltpu.roll(kappa, 1, 0)
                k_ref[i * 8 : i * 8 + 8, lanes] = kappa
                c_ref[i * 8 : i * 8 + 8, lanes] = 1.0 + kappa + jnp.where(top, above, rolled)
                above = rolled
        solve(a_ref, k_ref, c_ref, y_ref, g_ref)

    field = iota((FLD, LANES), 0)
    kept = (field >= 2) & (field <= 4)
    bottom = []
    for h in range(COL // LANES):
        level = slice((LEV - 1) * FLD, LEV * FLD)
        first = h * PAD_ROWS + (LEV - 1) * PITCH
        at = slice(first, first + FLD)
        old = tile_ref[h, level, :]
        bottom.append(old + (jnp.where(kept, a_ref[at, :], y_ref[at, :]) - old))
    b = jnp.concatenate(bottom, axis=1)
    b0, b3, b5, b6 = (b[f : f + 1, :] for f in (0, 3, 5, 6))
    wind = jnp.sqrt(1.0 + b5 * b5 + b6 * b6)
    flux = jnp.concatenate(
        [
            -0.5 * wind * b5,
            -0.5 * wind * b6,
            0.5 * softplus(b3),
            -0.3 * wind * b0,
            jnp.zeros((4, COL), f32),
        ],
        axis=0,
    )
    none = jnp.zeros((FLD, LANES), f32)
    used = []
    for n in range(4):
        mine = jnp.where(cols_ref[n] == 0, flux[:, :LANES], flux[:, LANES:])
        used.append(jnp.concatenate([none, mine] if n % 2 else [mine, none], axis=1))
    hi, low = split2(jnp.concatenate(used, axis=0))

    def weighted(parts, at):
        got = jnp.dot(
            jnp.concatenate(parts, axis=0), weight_ref[at], preferred_element_type=f32
        )
        total = got[0:32, :]
        for i in range(1, len(parts)):
            total = total + got[i * 32 : i * 32 + 32, :]
        return total

    products = weighted([hi], 1) + weighted([hi, low], 0)
    which = iota((PEERS, LANES), 0) % GROUP
    for e in range(4):
        value = jnp.broadcast_to(products[e : e + 1, 0:LANES], (PEERS, LANES))
        for n in range(1, 4):
            across = (n // 2) * LANES
            other = products[n * 8 + e : n * 8 + e + 1, across : across + LANES]
            value = jnp.where(which == n, other, value)
        out_ref[pl.ds(ROWS_UP + e, PEERS, stride=ROWS2), :] = value

    copies = []
    for h in range(COL // LANES):
        for k in range(LEV):
            rows = slice(k * FLD, (k + 1) * FLD)
            at = slice(h * PAD_ROWS + k * PITCH, h * PAD_ROWS + k * PITCH + FLD)
            mixed_state = jnp.where(kept, a_ref[at, :], y_ref[at, :])
            tend_ref[h, rows, :] = mixed_state - tile_ref[h, rows, :]
        copies.append(
            pltpu.make_async_copy(
                tend_ref.at[h], tend_out.at[:, pl.ds(h * LANES, LANES)], tend_sem.at[h]
            )
        )
        copies[-1].start()

    fields = jnp.concatenate(
        [
            jnp.concatenate(
                [y_ref[pl.ds(h * PAD_ROWS + f, LEV, stride=PITCH), :] for f in (0, 1, 5, 6)], axis=0
            )
            for h in range(COL // LANES)
        ],
        axis=1,
    )
    parts = split2(fields)
    sent = 0
    for pair in range(CAP // 2):
        hot = hot_ref[pair * 2 * PEERS : (pair + 1) * 2 * PEERS, :]
        total = None
        for part in parts:
            got = lax.dot_general(
                part, hot, (((1,), (1,)), ((), ())), preferred_element_type=f32
            )
            total = got if total is None else total + got
        for q in range(2):
            first = (pair * 2 + q) * UP * LEV
            block_ref[first : first + UP * LEV, :] = total[:, q * PEERS : (q + 1) * PEERS]
        ready = (pair + 1) * 2 * UP * LEV // LANES
        for t in range(sent, ready):
            out_ref[pl.ds(t, PEERS, stride=ROWS2), :] = block_ref[
                t * LANES : (t + 1) * LANES, :
            ].T
        sent = ready
    for copy in copies:
        copy.wait()


def ocean_kernel(meta_ref, got_ref, *sum_refs):
    chosen = (meta_ref[0:1, :] == meta_ref[8:24, :]).astype(bf16)
    values = jnp.concatenate(
        [got_ref[pl.ds(ROWS_UP + e, PEERS, stride=ROWS2), :] for e in range(4)], axis=1
    )
    total = None
    for part in split2(values):
        got = jnp.dot(chosen, part, preferred_element_type=f32)
        total = got if total is None else total + got
    for e in range(4):
        for flip in range(GROUP):
            sum_refs[flip][:, e, :] = total[
                flip * 4 : flip * 4 + 4, e * LANES : (e + 1) * LANES
            ]


def update_kernel(meta_ref, got_ref, tile_ref, out_ref, block_ref, new_ref, sem):
    count = meta_ref[4:5, :]
    unpacked = 0
    top = iota((8, LANES), 0) == 0
    last = iota((8, LANES), 0) == 7
    copies = []
    for p in range(CAP):
        needed = -(-(p + 1) * UP * LEV // LANES)
        for t in range(unpacked, needed):
            block_ref[8 + t * LANES : 8 + (t + 1) * LANES, :] = got_ref[
                pl.ds(t, PEERS, stride=ROWS2), :
            ].T
        unpacked = needed
        live = jnp.broadcast_to(count, (8, LANES)) > p + 0.5
        for i in range(LEV // 8):

            def grad(which):
                first = 8 + (p * UP + which) * LEV + i * 8
                prev = block_ref[first - 1 : first + 7, :]
                after = block_ref[first + 1 : first + 9, :]
                if i == 0:
                    prev = jnp.where(top, block_ref[first : first + 8, :], prev)
                if i == LEV // 8 - 1:
                    after = jnp.where(last, block_ref[first : first + 8, :], after)
                return prev - after

            gt, gq, gu, gv = (grad(which) for which in range(UP))
            production = (
                gu * gu + gv * gv, gt * gt, gq * gq, gt * gq, gu * gt, gv * gt, gu * gq, gu * gv,
            )
            for j in range(FLD):
                at = pl.ds(i * 64 + j, 8, stride=FLD)
                m = tile_ref[p, at, :]
                new = (0.85 - 0.05 * j) * m + 0.5 * jnp.tanh(production[j])
                new_ref[p, at, :] = jnp.where(live, new, m)
        copies.append(
            pltpu.make_async_copy(
                new_ref.at[p], out_ref.at[:, pl.ds(p * LANES, LANES)], sem.at[p]
            )
        )
        copies[-1].start()
    for copy in copies:
        copy.wait()


SMEM = pl.BlockSpec(memory_space=pltpu.SMEM)
VMEM = pl.BlockSpec(memory_space=pltpu.VMEM)
ANY = pl.BlockSpec(memory_space=pl.ANY)
HBM = pl.BlockSpec(memory_space=pltpu.HBM)
PLANE = LEV * FLD
VMEM_LIMIT = 16 << 20


def here(shape, dtype=f32):
    return pltpu.VMEM(shape, dtype)


def far(shape):
    return jax.ShapeDtypeStruct(shape, f32)


def hold(x):
    return pltpu.with_memory_space_constraint(x, pltpu.VMEM)


def outside(x):
    return pltpu.with_memory_space_constraint(x, pltpu.HBM)


def call(kernel, ins, outs, out_specs, scratch, name):
    return pl.pallas_call(
        kernel,
        in_specs=ins,
        out_specs=out_specs,
        out_shape=outs,
        scratch_shapes=scratch,
        name=name,
        compiler_params=pltpu.CompilerParams(vmem_limit_bytes=VMEM_LIMIT),
    )


def pack(rows, owner_row, mom):
    return call(
        pack_kernel,
        [HBM] * 3,
        [here((ROWS1 * PEERS, LANES))],
        [VMEM],
        [
            pltpu.SMEM((4,), jnp.int32),
            pltpu.VMEM((1, COL), jnp.int32),
            pltpu.VMEM((ROWS1 * LANES, LANES), f32),
            pltpu.SemaphoreType.DMA((CAP, DOWN)),
            pltpu.SemaphoreType.DMA((2,)),
        ],
        "pack",
    )(outside(rows), outside(owner_row), outside(mom))[0]


def prepare(owner_row, regime_row, state, mom, weights):
    return call(
        prepare_kernel,
        [VMEM] * 2 + [HBM] * 3,
        [
            here((2, PLANE, LANES)),
            here((SLOTS, COL), bf16),
            here((2, PARTS, LEV, LANES)),
            here((CAP, PLANE, LANES)),
            here((2, 2 * LANES, 2 * LANES), bf16),
        ],
        [VMEM] * 5,
        [
            pltpu.VMEM((4, LANES, LANES), f32),
            pltpu.SemaphoreType.DMA((2,)),
            pltpu.SemaphoreType.DMA((CAP,)),
            pltpu.SemaphoreType.DMA,
        ],
        "prepare",
    )(owner_row, regime_row, outside(state), outside(mom), outside(weights))


def physics(device, cols, regime_row, got, tiles, hot, parts, weights):
    return call(
        physics_kernel,
        [SMEM] * 2 + [VMEM] * 6,
        [far((PLANE, COL)), here((ROWS2 * PEERS, LANES)), here((24, PEERS))],
        [ANY, VMEM, VMEM],
        [
            pltpu.VMEM((2, PLANE, LANES), f32),
            pltpu.VMEM((ROWS_UP * LANES, LANES), f32),
            pltpu.VMEM((DOWN * LEV + 8, COL), f32),
            pltpu.VMEM((2 * PAD_ROWS, LANES), f32),
            pltpu.VMEM((2 * PAD_ROWS, LANES), f32),
            pltpu.VMEM((2 * PAD_ROWS, LANES), f32),
            pltpu.VMEM((LEV, COL), f32),
            pltpu.VMEM((LEV, COL), f32),
            pltpu.VMEM((LEV, COL), f32),
            pltpu.SemaphoreType.DMA((2,)),
        ],
        "physics",
    )(device, cols, regime_row, *(hold(x) for x in (got, tiles, hot, parts, weights)))


def ocean(meta, back):
    return call(
        ocean_kernel, [VMEM, VMEM], [here((4, 4, LANES))] * GROUP, [VMEM] * GROUP, [], "ocean"
    )(hold(meta), hold(back))


def update(meta, back, tiles):
    return call(
        update_kernel,
        [VMEM] * 3,
        [far((PLANE, SLOTS))],
        [ANY],
        [
            pltpu.VMEM((ROWS_UP * LANES + 16, LANES), f32),
            pltpu.VMEM((CAP, PLANE, LANES), f32),
            pltpu.SemaphoreType.DMA((CAP,)),
        ],
        "update",
    )(hold(meta), hold(back), hold(tiles))[0]


def exchange(sent, rows):
    got = lax.all_to_all(
        sent.reshape(PEERS, 1, rows * LANES), ("node", "dev"), 0, 0, tiled=True
    )
    return got.reshape(PEERS * rows, LANES)


def local(state, span_owner, regime, moments, remap_weights, remap_rows, remap_cols):
    dev_count = lax.axis_size("dev")
    device = lax.axis_index(("node", "dev")).astype(jnp.int32).reshape(1)
    owner_row = span_owner.reshape(1, COL)
    regime_row = regime.reshape(1, COL)
    sent = pack(remap_rows, owner_row, moments)
    tiles, hot, parts, mom_tiles, weights = prepare(
        owner_row,
        regime_row,
        state.reshape(PLANE, COL),
        moments.reshape(PLANE, SLOTS),
        remap_weights,
    )
    got = exchange(sent, ROWS1)
    tend, sent, meta = physics(device, remap_cols, regime_row, got, tiles, hot, parts, weights)
    back = exchange(sent, ROWS2)
    sums = ocean(meta, back)
    others = [
        lax.ppermute(sums[flip], "dev", [(i, i ^ flip) for i in range(dev_count)])
        for flip in (2, 3, 1)
    ]
    new_mom = update(meta, back, mom_tiles)
    flux = sums[0] + others[2] + others[0] + others[1]
    return tend.reshape(LEV, FLD, COL), new_mom.reshape(LEV, FLD, SLOTS), flux


def solution(mesh):
    return jax.shard_map(
        local,
        mesh=mesh,
        in_specs=(
            P(None, None, ("node", "dev")),
            P(("node", "dev"), None),
            P(("node", "dev")),
            P(None, None, ("node", "dev")),
            P(("node", "dev"), None, None),
            P(("node", "dev")),
            P(("node", "dev")),
        ),
        out_specs=(
            P(None, None, ("node", "dev")),
            P(None, None, ("node", "dev")),
            P(("node", "dev"), None, None),
        ),
        check_vma=False,
    )
```

```python
import jax
import jax.numpy as jnp
from jax import lax
from jax.experimental import pallas as pl
from jax.experimental.pallas import tpu as pltpu
from jax.sharding import PartitionSpec as P


LEV = 72
FLD = 8
PEERS = 128
LANES = 128
CAP = 4
COL = 256
SLOTS = CAP * PEERS
DOWN = 2
UP = 4
ROWS1 = 5
META = CAP * DOWN * LEV
ROWS_UP = CAP * UP * LEV // LANES
OCN_ROWS = 4
GROUP = 4
ROWS2 = ROWS_UP + OCN_ROWS
HALF = LEV // 2
PITCH = 9
PAD_ROWS = 664
PARTS = 9
f32 = jnp.float32
bf16 = jnp.bfloat16


def iota(shape, axis):
    return lax.broadcasted_iota(jnp.int32, shape, axis)


def split2(x):
    hi = x.astype(bf16)
    return hi, (x - hi.astype(f32)).astype(bf16)


def columns_down(owner_row):
    real = owner_row.astype(f32)
    parts = [
        jnp.broadcast_to(real[:, h * LANES : (h + 1) * LANES], (LANES, LANES)).T
        for h in range(COL // LANES)
    ]
    return jnp.concatenate(parts, axis=0)


def pack_kernel(
    rows_hbm, owner_hbm, mom_ref, out_ref, rows_ref, owner_ref, block_ref, sem, small_sem
):
    small = [
        pltpu.make_async_copy(owner_hbm, owner_ref, small_sem.at[0]),
        pltpu.make_async_copy(rows_hbm, rows_ref, small_sem.at[1]),
    ]
    copies = []
    for p in range(CAP):
        for at, moment in enumerate((0, 2)):
            copies.append(
                pltpu.make_async_copy(
                    mom_ref.at[:, moment, pl.ds(p * LANES, LANES)],
                    block_ref.at[pl.ds((p * DOWN + at) * LEV, LEV), :],
                    sem.at[p, at],
                )
            )
    for copy in small + copies:
        copy.start()
    for copy in small:
        copy.wait()
    owner_down = columns_down(owner_ref[...])
    peer = iota((COL, LANES), 1).astype(f32)
    count = jnp.sum((owner_down == peer).astype(f32), axis=0, keepdims=True)
    tail = ROWS1 * LANES - META
    which = iota((tail, LANES), 0)
    meta = jnp.where(which == 4, jnp.broadcast_to(count, (tail, LANES)), 0.0)
    for n in range(4):
        meta = jnp.where(which == n, rows_ref[n].astype(f32), meta)
    block_ref[META:, :] = meta
    for copy in copies:
        copy.wait()
    for t in range(ROWS1):
        out_ref[pl.ds(t, PEERS, stride=ROWS1), :] = block_ref[t * LANES : (t + 1) * LANES, :].T


def softplus(x):
    return jnp.maximum(x, 0.0) + jnp.log(1.0 + jnp.exp(-jnp.abs(x)))


def rain_fall(rain, above, top):
    rain_q = softplus(rain)
    falling = 0.5 * rain_q
    rolled = pltpu.roll(falling, 1, 0)
    return rain_q, rain + 0.5 * (jnp.where(top, above, rolled) - falling), rolled


def micro_free(x, rain_q, warm, mixed, icy):
    temper, vap, liq, rain, ice = x
    vapour = softplus(vap)
    liquid = softplus(liq)
    ice_q = softplus(ice)
    half_t = jnp.tanh(0.5 * temper)
    satur = 0.6 * jnp.exp(0.5 * half_t)
    excess = vapour - satur
    autoconv = 0.3 * liquid * liquid / (1.0 + liquid)
    evapor = 0.1 * rain_q * (0.5 - 0.5 * jnp.tanh(0.5 * excess))
    freeze = 0.3 * liquid * (0.5 - 0.5 * half_t)
    melting = 0.2 * ice_q * (0.5 + 0.5 * half_t)
    aggreg = 0.25 * ice_q * ice_q / (1.0 + ice_q)
    source = jnp.where(
        icy, 0.175 * jnp.tanh(vapour - 0.8 * satur), 0.2 * jnp.tanh(excess)
    )

    def pick(a, b, c):
        return jnp.where(warm, a, jnp.where(mixed, b, c))

    swap = freeze - melting
    kept = (
        temper + pick(-0.4 * evapor, 0.25 * swap, 0.25 * freeze),
        jnp.where(warm, vap + 0.5 * evapor, vap),
        liq - 0.5 * pick(autoconv, freeze + autoconv, freeze),
        rain + 0.5 * pick(autoconv - evapor, autoconv + melting, aggreg),
        jnp.where(warm, ice, ice + 0.5 * jnp.where(mixed, swap, freeze - aggreg)),
    )
    return kept, source, excess


def micro_bound(kept, source, excess, m2, icy):
    temper, vap, liq, rain, ice = kept
    gain = source * (1.0 + 0.5 * jnp.tanh(0.5 * (m2 + excess)))
    return (
        temper + jnp.where(icy, gain, 0.8 * gain),
        vap - gain,
        jnp.where(icy, liq, liq + gain),
        rain,
        jnp.where(icy, ice + gain, ice),
    )


def solve(a_ref, k_ref, c_ref, y_ref, g_ref):
    halves = range(COL // LANES)

    def row(ref, h, level):
        one = ref[level : level + 1, h * LANES : (h + 1) * LANES]
        return jnp.broadcast_to(one, (FLD, LANES))

    def rows(h, level):
        first = h * PAD_ROWS + level * PITCH
        return slice(first, first + FLD)

    def base(h, chain, step):
        return row(c_ref, h, LEV - 1 - step if chain else step)

    def link(h, chain, step):
        return row(k_ref, h, LEV - 1 - step if chain else step - 1)

    def finish(h, chain, step, r):
        k = LEV - 1 - step if chain else step
        d = a_ref[rows(h, k), :] * r
        if step > 0:
            d = d + (link(h, chain, step) * r) * last_d[h, chain]
        g = row(k_ref, h, k - 1 if chain else k) * r
        g_ref[rows(h, k), :] = g
        y_ref[rows(h, k), :] = d
        last_d[h, chain] = d
        last_g[h, chain] = g

    chains = [(h, chain) for h in halves for chain in range(2)]
    den, last_d, last_g = {}, {}, {}
    for at in chains:
        den[at] = base(*at, 0)
        finish(*at, 0, 1.0 / den[at])
    for step in range(1, HALF, 2):
        for at in chains:
            old = den[at]
            k = link(*at, step)
            r = 1.0 / (base(*at, step) * old - k * k)
            if step + 1 < HALF:
                k = link(*at, step + 1)
                den[at] = base(*at, step + 1) - (k * k * old) * r
            finish(*at, step, old * r)
            if step + 1 < HALF:
                finish(*at, step + 1, 1.0 / den[at])
    z = {}
    for h in halves:
        d_up, d_dn = last_d[h, 0], last_d[h, 1]
        g_up, g_dn = last_g[h, 0], last_g[h, 1]
        z[h, 0] = (d_up + g_up * d_dn) / (1.0 - g_up * g_dn)
        z[h, 1] = d_dn + g_dn * z[h, 0]
        y_ref[rows(h, HALF - 1), :] = z[h, 0]
        y_ref[rows(h, HALF), :] = z[h, 1]
    for step in range(1, HALF):
        for h in halves:
            for chain in range(2):
                k = HALF + step if chain else HALF - 1 - step
                z[h, chain] = y_ref[rows(h, k), :] + g_ref[rows(h, k), :] * z[h, chain]
                y_ref[rows(h, k), :] = z[h, chain]


def regimes(regime_ref, h):
    kind = jnp.broadcast_to(regime_ref[:, h * LANES : (h + 1) * LANES], (8, LANES))
    return kind == 0, kind == 1, kind == 2


def prepare_kernel(
    owner_ref, regime_ref, state_ref, mom_ref, weight_ref,
    tile_ref, hot_ref, part_ref, mom_tile_ref, weight_part_ref,
    weight_own, sem, mom_sem, weight_sem,
):
    copies = [
        pltpu.make_async_copy(
            state_ref.at[:, pl.ds(h * LANES, LANES)], tile_ref.at[h], sem.at[h]
        )
        for h in range(COL // LANES)
    ]
    weights = pltpu.make_async_copy(weight_ref, weight_own, weight_sem)
    moments = [
        pltpu.make_async_copy(
            mom_ref.at[:, pl.ds(p * LANES, LANES)], mom_tile_ref.at[p], mom_sem.at[p]
        )
        for p in range(CAP)
    ]
    for copy in copies + [weights] + moments:
        copy.start()
    owner_row = owner_ref[...]
    owner_down = columns_down(owner_row)
    owner_real = owner_row.astype(f32)
    before = jnp.zeros((1, COL), f32)
    for h in range(COL // LANES):
        same = (
            jnp.concatenate([owner_down[h * LANES : (h + 1) * LANES, :]] * 2, axis=1) == owner_real
        )
        earlier = iota((LANES, COL), 0) + h * LANES < iota((LANES, COL), 1)
        before = before + jnp.sum((same & earlier).astype(f32), axis=0, keepdims=True)
    slot = owner_row + PEERS * before.astype(jnp.int32)
    for p in range(CAP):
        hot_ref[p * PEERS : (p + 1) * PEERS, :] = (
            iota((PEERS, COL), 0) + p * PEERS == slot
        ).astype(bf16)
    top = iota((8, LANES), 0) == 0
    for h in range(COL // LANES):
        copies[h].wait()
        warm, mixed, icy = regimes(regime_ref, h)
        above = [jnp.zeros((8, LANES), f32)] * 2
        for i in range(LEV // 8):
            x = [tile_ref[h, pl.ds(i * 64 + f, 8, stride=FLD), :] for f in range(7)]
            rain_q, x[3], above[0] = rain_fall(x[3], above[0], top)
            kept, source, excess = micro_free(x[:5], rain_q, warm, mixed, icy)
            rain_q, rain, above[1] = rain_fall(kept[3], above[1], top)
            shear = None
            for f in (5, 6):
                if i < LEV // 8 - 1:
                    below = tile_ref[h, pl.ds(i * 64 + FLD + f, 8, stride=FLD), :]
                else:
                    below = pltpu.roll(x[f], 7, 0)
                square = (x[f] - below) * (x[f] - below)
                shear = square if shear is None else shear + square
            shear = 1.5 * shear / (1.0 + shear)
            values = kept[:3] + (rain, kept[4], source, excess, rain_q, shear)
            for f, value in enumerate(values):
                part_ref[h, f, i * 8 : i * 8 + 8, :] = value
    weights.wait()
    for n in range(4):
        down, across = (n % 2) * LANES, (n // 2) * LANES
        for at, part in enumerate(split2(weight_own[n])):
            weight_part_ref[at, down : down + LANES, across : across + LANES] = part
    for copy in moments:
        copy.wait()


def physics_kernel(
    device_ref,
    cols_ref,
    regime_ref,
    got_ref,
    tile_ref,
    hot_ref,
    part_ref,
    weight_ref,
    tend_out,
    out_ref,
    meta_ref,
    tend_ref,
    block_ref,
    mom_ref,
    a_ref,
    y_ref,
    g_ref,
    k_ref,
    c_ref,
    e_ref,
    tend_sem,
):
    for t in range(ROWS1):
        block_ref[t * LANES : (t + 1) * LANES, :] = got_ref[pl.ds(t, PEERS, stride=ROWS1), :].T
    device = device_ref[0]
    mine = device % GROUP
    picked = block_ref[META : META + 1, :]
    for n in range(1, 4):
        picked = jnp.where(mine == n, block_ref[META + n : META + n + 1, :], picked)
    meta_ref[0:1, :] = picked
    group = device - mine
    member = iota((16, PEERS), 0) // 4
    first_row = jnp.zeros((16, PEERS), f32)
    for flip in range(GROUP):
        partner = group + mine + flip - 2 * (mine & flip)
        first_row = jnp.where(member == flip, (partner * 4).astype(f32), first_row)
    meta_ref[8:24, :] = first_row + (iota((16, PEERS), 0) % 4).astype(f32)
    meta_ref[4:8, :] = block_ref[META + 4 : META + 8, :]
    slotted = jnp.concatenate(
        [block_ref[p * DOWN * LEV : (p + 1) * DOWN * LEV, :] for p in range(CAP)], axis=1
    )
    total = None
    for part in split2(slotted):
        got = jnp.dot(part, hot_ref[...], preferred_element_type=f32)
        total = got if total is None else total + got
    mom_ref[0 : DOWN * LEV, :] = total

    top = iota((8, LANES), 0) == 0
    for h in range(COL // LANES):
        lanes = slice(h * LANES, (h + 1) * LANES)
        warm, mixed, icy = regimes(regime_ref, h)
        base = h * PAD_ROWS
        for i in range(LEV // 8):
            m2 = mom_ref[LEV + i * 8 : LEV + i * 8 + 8, lanes]
            first = tuple(part_ref[h, f, i * 8 : i * 8 + 8, :] for f in range(8))
            x = micro_bound(first[:5], first[5], first[6], m2, icy)
            kept, source, excess = micro_free(x, first[7], warm, mixed, icy)
            x = micro_bound(kept, source, excess, m2, icy)
            for f, value in enumerate(x):
                a_ref[pl.ds(base + i * 8 * PITCH + f, 8, stride=PITCH), :] = value
            for f in range(5, FLD):
                a_ref[pl.ds(base + i * 8 * PITCH + f, 8, stride=PITCH), :] = tile_ref[
                    h, pl.ds(i * 64 + f, 8, stride=FLD), :
                ]
        for ref in (a_ref, y_ref):
            ref[base + LEV * PITCH : base + LEV * PITCH + FLD, :] = jnp.zeros((FLD, LANES), f32)
    last = iota((8, COL), 0) == 7
    for i in range(LEV // 8):
        m0 = mom_ref[i * 8 : i * 8 + 8, :]
        m0_next = mom_ref[i * 8 + 1 : i * 8 + 9, :]
        energy = 30.5 + 30.0 * jnp.tanh(m0 + m0_next)
        if i == LEV // 8 - 1:
            energy = jnp.where(last, 0.0, energy)
        e_ref[i * 8 : i * 8 + 8, :] = energy
    for turn in range(3):
        src = a_ref if turn == 0 else y_ref
        for h in range(COL // LANES):
            lanes = slice(h * LANES, (h + 1) * LANES)
            above = jnp.zeros((8, LANES), f32)
            for i in range(LEV // 8):

                def drop(f):
                    first = h * PAD_ROWS + i * 8 * PITCH + f
                    return (
                        src[pl.ds(first, 8, stride=PITCH), :]
                        - src[pl.ds(first + PITCH, 8, stride=PITCH), :]
                    )

                if turn == 0:
                    shear = part_ref[h, 8, i * 8 : i * 8 + 8, :]
                else:
                    du, dv = drop(5), drop(6)
                    shear = du * du + dv * dv
                    shear = 1.5 * shear / (1.0 + shear)
                mixing = 0.3 + shear * (0.5 - 0.5 * jnp.tanh(drop(0)))
                kappa = mixing * e_ref[i * 8 : i * 8 + 8, lanes]
                rolled = pltpu.roll(kappa, 1, 0)
                k_ref[i * 8 : i * 8 + 8, lanes] = kappa
                c_ref[i * 8 : i * 8 + 8, lanes] = 1.0 + kappa + jnp.where(top, above, rolled)
                above = rolled
        solve(a_ref, k_ref, c_ref, y_ref, g_ref)

    field = iota((FLD, LANES), 0)
    kept = (field >= 2) & (field <= 4)
    bottom = []
    for h in range(COL // LANES):
        level = slice((LEV - 1) * FLD, LEV * FLD)
        first = h * PAD_ROWS + (LEV - 1) * PITCH
        at = slice(first, first + FLD)
        old = tile_ref[h, level, :]
        bottom.append(old + (jnp.where(kept, a_ref[at, :], y_ref[at, :]) - old))
    b = jnp.concatenate(bottom, axis=1)
    b0, b3, b5, b6 = (b[f : f + 1, :] for f in (0, 3, 5, 6))
    wind = jnp.sqrt(1.0 + b5 * b5 + b6 * b6)
    flux = jnp.concatenate(
        [
            -0.5 * wind * b5,
            -0.5 * wind * b6,
            0.5 * softplus(b3),
            -0.3 * wind * b0,
            jnp.zeros((4, COL), f32),
        ],
        axis=0,
    )
    none = jnp.zeros((FLD, LANES), f32)
    used = []
    for n in range(4):
        mine = jnp.where(cols_ref[n] == 0, flux[:, :LANES], flux[:, LANES:])
        used.append(jnp.concatenate([none, mine] if n % 2 else [mine, none], axis=1))
    hi, low = split2(jnp.concatenate(used, axis=0))

    def weighted(parts, at):
        got = jnp.dot(
            jnp.concatenate(parts, axis=0), weight_ref[at], preferred_element_type=f32
        )
        total = got[0:32, :]
        for i in range(1, len(parts)):
            total = total + got[i * 32 : i * 32 + 32, :]
        return total

    products = weighted([hi], 1) + weighted([hi, low], 0)
    which = iota((PEERS, LANES), 0) % GROUP
    for e in range(4):
        value = jnp.broadcast_to(products[e : e + 1, 0:LANES], (PEERS, LANES))
        for n in range(1, 4):
            across = (n // 2) * LANES
            other = products[n * 8 + e : n * 8 + e + 1, across : across + LANES]
            value = jnp.where(which == n, other, value)
        out_ref[pl.ds(ROWS_UP + e, PEERS, stride=ROWS2), :] = value

    copies = []
    for h in range(COL // LANES):
        for k in range(LEV):
            rows = slice(k * FLD, (k + 1) * FLD)
            at = slice(h * PAD_ROWS + k * PITCH, h * PAD_ROWS + k * PITCH + FLD)
            mixed_state = jnp.where(kept, a_ref[at, :], y_ref[at, :])
            tend_ref[h, rows, :] = mixed_state - tile_ref[h, rows, :]
        copies.append(
            pltpu.make_async_copy(
                tend_ref.at[h], tend_out.at[:, pl.ds(h * LANES, LANES)], tend_sem.at[h]
            )
        )
        copies[-1].start()

    fields = jnp.concatenate(
        [
            jnp.concatenate(
                [y_ref[pl.ds(h * PAD_ROWS + f, LEV, stride=PITCH), :] for f in (0, 1, 5, 6)], axis=0
            )
            for h in range(COL // LANES)
        ],
        axis=1,
    )
    parts = split2(fields)
    sent = 0
    for pair in range(CAP // 2):
        hot = hot_ref[pair * 2 * PEERS : (pair + 1) * 2 * PEERS, :]
        total = None
        for part in parts:
            got = lax.dot_general(
                part, hot, (((1,), (1,)), ((), ())), preferred_element_type=f32
            )
            total = got if total is None else total + got
        for q in range(2):
            first = (pair * 2 + q) * UP * LEV
            block_ref[first : first + UP * LEV, :] = total[:, q * PEERS : (q + 1) * PEERS]
        ready = (pair + 1) * 2 * UP * LEV // LANES
        for t in range(sent, ready):
            out_ref[pl.ds(t, PEERS, stride=ROWS2), :] = block_ref[
                t * LANES : (t + 1) * LANES, :
            ].T
        sent = ready
    for copy in copies:
        copy.wait()


def ocean_kernel(meta_ref, got_ref, *sum_refs):
    chosen = (meta_ref[0:1, :] == meta_ref[8:24, :]).astype(bf16)
    values = jnp.concatenate(
        [got_ref[pl.ds(ROWS_UP + e, PEERS, stride=ROWS2), :] for e in range(4)], axis=1
    )
    total = None
    for part in split2(values):
        got = jnp.dot(chosen, part, preferred_element_type=f32)
        total = got if total is None else total + got
    for e in range(4):
        for flip in range(GROUP):
            sum_refs[flip][:, e, :] = total[
                flip * 4 : flip * 4 + 4, e * LANES : (e + 1) * LANES
            ]


def update_kernel(meta_ref, got_ref, tile_ref, out_ref, block_ref, new_ref, sem):
    count = meta_ref[4:5, :]
    unpacked = 0
    top = iota((8, LANES), 0) == 0
    last = iota((8, LANES), 0) == 7
    copies = []
    for p in range(CAP):
        needed = -(-(p + 1) * UP * LEV // LANES)
        for t in range(unpacked, needed):
            block_ref[8 + t * LANES : 8 + (t + 1) * LANES, :] = got_ref[
                pl.ds(t, PEERS, stride=ROWS2), :
            ].T
        unpacked = needed
        live = jnp.broadcast_to(count, (8, LANES)) > p + 0.5
        for i in range(LEV // 8):

            def grad(which):
                first = 8 + (p * UP + which) * LEV + i * 8
                prev = block_ref[first - 1 : first + 7, :]
                after = block_ref[first + 1 : first + 9, :]
                if i == 0:
                    prev = jnp.where(top, block_ref[first : first + 8, :], prev)
                if i == LEV // 8 - 1:
                    after = jnp.where(last, block_ref[first : first + 8, :], after)
                return prev - after

            gt, gq, gu, gv = (grad(which) for which in range(UP))
            production = (
                gu * gu + gv * gv, gt * gt, gq * gq, gt * gq, gu * gt, gv * gt, gu * gq, gu * gv,
            )
            for j in range(FLD):
                at = pl.ds(i * 64 + j, 8, stride=FLD)
                m = tile_ref[p, at, :]
                new = (0.85 - 0.05 * j) * m + 0.5 * jnp.tanh(production[j])
                new_ref[p, at, :] = jnp.where(live, new, m)
        copies.append(
            pltpu.make_async_copy(
                new_ref.at[p], out_ref.at[:, pl.ds(p * LANES, LANES)], sem.at[p]
            )
        )
        copies[-1].start()
    for copy in copies:
        copy.wait()


SMEM = pl.BlockSpec(memory_space=pltpu.SMEM)
VMEM = pl.BlockSpec(memory_space=pltpu.VMEM)
ANY = pl.BlockSpec(memory_space=pl.ANY)
HBM = pl.BlockSpec(memory_space=pltpu.HBM)
PLANE = LEV * FLD
VMEM_LIMIT = 16 << 20


def here(shape, dtype=f32):
    return pltpu.VMEM(shape, dtype)


def far(shape):
    return jax.ShapeDtypeStruct(shape, f32)


def hold(x):
    return pltpu.with_memory_space_constraint(x, pltpu.VMEM)


def outside(x):
    return pltpu.with_memory_space_constraint(x, pltpu.HBM)


def call(kernel, ins, outs, out_specs, scratch):
    return pl.pallas_call(
        kernel,
        in_specs=ins,
        out_specs=out_specs,
        out_shape=outs,
        scratch_shapes=scratch,
        compiler_params=pltpu.CompilerParams(vmem_limit_bytes=VMEM_LIMIT),
    )


def pack(rows, owner_row, mom):
    return call(
        pack_kernel,
        [HBM] * 3,
        [here((ROWS1 * PEERS, LANES))],
        [VMEM],
        [
            pltpu.SMEM((4,), jnp.int32),
            pltpu.VMEM((1, COL), jnp.int32),
            pltpu.VMEM((ROWS1 * LANES, LANES), f32),
            pltpu.SemaphoreType.DMA((CAP, DOWN)),
            pltpu.SemaphoreType.DMA((2,)),
        ],
    )(outside(rows), outside(owner_row), outside(mom))[0]


def prepare(owner_row, regime_row, state, mom, weights):
    return call(
        prepare_kernel,
        [VMEM] * 2 + [HBM] * 3,
        [
            here((2, PLANE, LANES)),
            here((SLOTS, COL), bf16),
            here((2, PARTS, LEV, LANES)),
            here((CAP, PLANE, LANES)),
            here((2, 2 * LANES, 2 * LANES), bf16),
        ],
        [VMEM] * 5,
        [
            pltpu.VMEM((4, LANES, LANES), f32),
            pltpu.SemaphoreType.DMA((2,)),
            pltpu.SemaphoreType.DMA((CAP,)),
            pltpu.SemaphoreType.DMA,
        ],
    )(owner_row, regime_row, outside(state), outside(mom), outside(weights))


def physics(device, cols, regime_row, got, tiles, hot, parts, weights):
    return call(
        physics_kernel,
        [SMEM] * 2 + [VMEM] * 6,
        [far((PLANE, COL)), here((ROWS2 * PEERS, LANES)), here((24, PEERS))],
        [ANY, VMEM, VMEM],
        [
            pltpu.VMEM((2, PLANE, LANES), f32),
            pltpu.VMEM((ROWS_UP * LANES, LANES), f32),
            pltpu.VMEM((DOWN * LEV + 8, COL), f32),
            pltpu.VMEM((2 * PAD_ROWS, LANES), f32),
            pltpu.VMEM((2 * PAD_ROWS, LANES), f32),
            pltpu.VMEM((2 * PAD_ROWS, LANES), f32),
            pltpu.VMEM((LEV, COL), f32),
            pltpu.VMEM((LEV, COL), f32),
            pltpu.VMEM((LEV, COL), f32),
            pltpu.SemaphoreType.DMA((2,)),
        ],
    )(device, cols, regime_row, *(hold(x) for x in (got, tiles, hot, parts, weights)))


def ocean(meta, back):
    return call(
        ocean_kernel, [VMEM, VMEM], [here((4, 4, LANES))] * GROUP, [VMEM] * GROUP, []
    )(hold(meta), hold(back))


def update(meta, back, tiles):
    return call(
        update_kernel,
        [VMEM] * 3,
        [far((PLANE, SLOTS))],
        [ANY],
        [
            pltpu.VMEM((ROWS_UP * LANES + 16, LANES), f32),
            pltpu.VMEM((CAP, PLANE, LANES), f32),
            pltpu.SemaphoreType.DMA((CAP,)),
        ],
    )(hold(meta), hold(back), hold(tiles))[0]


def exchange(sent, rows):
    got = lax.all_to_all(
        sent.reshape(PEERS, 1, rows * LANES), ("node", "dev"), 0, 0, tiled=True
    )
    return got.reshape(PEERS * rows, LANES)


def local(state, span_owner, regime, moments, remap_weights, remap_rows, remap_cols):
    dev_count = lax.axis_size("dev")
    device = lax.axis_index(("node", "dev")).astype(jnp.int32).reshape(1)
    owner_row = span_owner.reshape(1, COL)
    regime_row = regime.reshape(1, COL)
    sent = pack(remap_rows, owner_row, moments)
    tiles, hot, parts, mom_tiles, weights = prepare(
        owner_row,
        regime_row,
        state.reshape(PLANE, COL),
        moments.reshape(PLANE, SLOTS),
        remap_weights,
    )
    got = exchange(sent, ROWS1)
    tend, sent, meta = physics(device, remap_cols, regime_row, got, tiles, hot, parts, weights)
    back = exchange(sent, ROWS2)
    sums = ocean(meta, back)
    others = []
    for flip in (2, 3, 1):
        others.append(lax.ppermute(sums[flip], "dev", [(i, i ^ flip) for i in range(dev_count)]))
    new_mom = update(meta, back, mom_tiles)
    flux = sums[0] + others[2] + others[0] + others[1]
    return tend.reshape(LEV, FLD, COL), new_mom.reshape(LEV, FLD, SLOTS), flux


def solution(mesh):
    return jax.shard_map(
        local,
        mesh=mesh,
        in_specs=(
            P(None, None, ("node", "dev")),
            P(("node", "dev"), None),
            P(("node", "dev")),
            P(None, None, ("node", "dev")),
            P(("node", "dev"), None, None),
            P(("node", "dev")),
            P(("node", "dev")),
        ),
        out_specs=(
            P(None, None, ("node", "dev")),
            P(None, None, ("node", "dev")),
            P(("node", "dev"), None, None),
        ),
        check_vma=False,
    )
```

```python
import jax
import jax.numpy as jnp
from jax import lax
from jax.experimental import pallas as pl
from jax.experimental.pallas import tpu as pltpu
from jax.sharding import PartitionSpec as P


LEV = 72
FLD = 8
PEERS = 128
LANES = 128
CAP = 4
COL = 256
SLOTS = CAP * PEERS
DOWN = 2
UP = 4
ROWS1 = 5
META = CAP * DOWN * LEV
ROWS_UP = CAP * UP * LEV // LANES
OCN_ROWS = 4
GROUP = 4
ROWS2 = ROWS_UP + OCN_ROWS
HALF = LEV // 2
PITCH = 9
PAD_ROWS = 664
PARTS = 9
f32 = jnp.float32
bf16 = jnp.bfloat16


def iota(shape, axis):
    return lax.broadcasted_iota(jnp.int32, shape, axis)


def split2(x):
    hi = x.astype(bf16)
    return hi, (x - hi.astype(f32)).astype(bf16)


def columns_down(owner_row):
    real = owner_row.astype(f32)
    parts = [
        jnp.broadcast_to(real[:, h * LANES : (h + 1) * LANES], (LANES, LANES)).T
        for h in range(COL // LANES)
    ]
    return jnp.concatenate(parts, axis=0)


def pack_kernel(
    rows_hbm, owner_hbm, mom_ref, out_ref,
    rows_ref, owner_ref, block_ref, turned_ref, sem, small_sem, out_sem,
):
    small = [
        pltpu.make_async_copy(owner_hbm, owner_ref, small_sem.at[0]),
        pltpu.make_async_copy(rows_hbm, rows_ref, small_sem.at[1]),
    ]
    copies = []
    for p in range(CAP):
        for at, moment in enumerate((0, 2)):
            copies.append(
                pltpu.make_async_copy(
                    mom_ref.at[:, moment, pl.ds(p * LANES, LANES)],
                    block_ref.at[pl.ds((p * DOWN + at) * LEV, LEV), :],
                    sem.at[p, at],
                )
            )
    for copy in small + copies:
        copy.start()
    leaving = []

    def leave(t):
        turned_ref[t] = block_ref[t * LANES : (t + 1) * LANES, :].T
        leaving.append(
            pltpu.make_async_copy(
                turned_ref.at[t], out_ref.at[:, 0, pl.ds(t * LANES, LANES)], out_sem.at[t]
            )
        )
        leaving[-1].start()

    for copy in small:
        copy.wait()
    owner_down = columns_down(owner_ref[...])
    peer = iota((COL, LANES), 1).astype(f32)
    count = jnp.sum((owner_down == peer).astype(f32), axis=0, keepdims=True)
    tail = ROWS1 * LANES - META
    which = iota((tail, LANES), 0)
    meta = jnp.where(which == 4, jnp.broadcast_to(count, (tail, LANES)), 0.0)
    for n in range(4):
        meta = jnp.where(which == n, rows_ref[n].astype(f32), meta)
    block_ref[META:, :] = meta
    landed = 0
    for t in range(ROWS1):
        needed = min(-(-(t + 1) * LANES // LEV), CAP * DOWN)
        for copy in copies[landed:needed]:
            copy.wait()
        landed = needed
        leave(t)
    for copy in leaving:
        copy.wait()


def softplus(x):
    return jnp.maximum(x, 0.0) + jnp.log(1.0 + jnp.exp(-jnp.abs(x)))


def rain_fall(rain, above, top):
    rain_q = softplus(rain)
    falling = 0.5 * rain_q
    rolled = pltpu.roll(falling, 1, 0)
    return rain_q, rain + 0.5 * (jnp.where(top, above, rolled) - falling), rolled


def micro_free(x, rain_q, warm, mixed, icy):
    temper, vap, liq, rain, ice = x
    vapour = softplus(vap)
    liquid = softplus(liq)
    ice_q = softplus(ice)
    half_t = jnp.tanh(0.5 * temper)
    satur = 0.6 * jnp.exp(0.5 * half_t)
    excess = vapour - satur
    autoconv = 0.3 * liquid * liquid / (1.0 + liquid)
    evapor = 0.1 * rain_q * (0.5 - 0.5 * jnp.tanh(0.5 * excess))
    freeze = 0.3 * liquid * (0.5 - 0.5 * half_t)
    melting = 0.2 * ice_q * (0.5 + 0.5 * half_t)
    aggreg = 0.25 * ice_q * ice_q / (1.0 + ice_q)
    source = jnp.where(
        icy, 0.175 * jnp.tanh(vapour - 0.8 * satur), 0.2 * jnp.tanh(excess)
    )

    def pick(a, b, c):
        return jnp.where(warm, a, jnp.where(mixed, b, c))

    swap = freeze - melting
    kept = (
        temper + pick(-0.4 * evapor, 0.25 * swap, 0.25 * freeze),
        jnp.where(warm, vap + 0.5 * evapor, vap),
        liq - 0.5 * pick(autoconv, freeze + autoconv, freeze),
        rain + 0.5 * pick(autoconv - evapor, autoconv + melting, aggreg),
        jnp.where(warm, ice, ice + 0.5 * jnp.where(mixed, swap, freeze - aggreg)),
    )
    return kept, source, excess


def micro_bound(kept, source, excess, m2, icy):
    temper, vap, liq, rain, ice = kept
    gain = source * (1.0 + 0.5 * jnp.tanh(0.5 * (m2 + excess)))
    return (
        temper + jnp.where(icy, gain, 0.8 * gain),
        vap - gain,
        jnp.where(icy, liq, liq + gain),
        rain,
        jnp.where(icy, ice + gain, ice),
    )


def solve(a_ref, k_ref, c_ref, y_ref, g_ref):
    halves = range(COL // LANES)

    def row(ref, h, level):
        one = ref[level : level + 1, h * LANES : (h + 1) * LANES]
        return jnp.broadcast_to(one, (FLD, LANES))

    def rows(h, level):
        first = h * PAD_ROWS + level * PITCH
        return slice(first, first + FLD)

    def base(h, chain, step):
        return row(c_ref, h, LEV - 1 - step if chain else step)

    def link(h, chain, step):
        return row(k_ref, h, LEV - 1 - step if chain else step - 1)

    def finish(h, chain, step, r):
        k = LEV - 1 - step if chain else step
        d = a_ref[rows(h, k), :] * r
        if step > 0:
            d = d + (link(h, chain, step) * r) * last_d[h, chain]
        g = row(k_ref, h, k - 1 if chain else k) * r
        g_ref[rows(h, k), :] = g
        y_ref[rows(h, k), :] = d
        last_d[h, chain] = d
        last_g[h, chain] = g

    chains = [(h, chain) for h in halves for chain in range(2)]
    den, last_d, last_g = {}, {}, {}
    for at in chains:
        den[at] = base(*at, 0)
        finish(*at, 0, 1.0 / den[at])
    for step in range(1, HALF, 2):
        for at in chains:
            old = den[at]
            k = link(*at, step)
            r = 1.0 / (base(*at, step) * old - k * k)
            if step + 1 < HALF:
                k = link(*at, step + 1)
                den[at] = base(*at, step + 1) - (k * k * old) * r
            finish(*at, step, old * r)
            if step + 1 < HALF:
                finish(*at, step + 1, 1.0 / den[at])
    z = {}
    for h in halves:
        d_up, d_dn = last_d[h, 0], last_d[h, 1]
        g_up, g_dn = last_g[h, 0], last_g[h, 1]
        z[h, 0] = (d_up + g_up * d_dn) / (1.0 - g_up * g_dn)
        z[h, 1] = d_dn + g_dn * z[h, 0]
        y_ref[rows(h, HALF - 1), :] = z[h, 0]
        y_ref[rows(h, HALF), :] = z[h, 1]
    for step in range(1, HALF):
        for h in halves:
            for chain in range(2):
                k = HALF + step if chain else HALF - 1 - step
                z[h, chain] = y_ref[rows(h, k), :] + g_ref[rows(h, k), :] * z[h, chain]
                y_ref[rows(h, k), :] = z[h, chain]


def regimes(regime_ref, h):
    kind = jnp.broadcast_to(regime_ref[:, h * LANES : (h + 1) * LANES], (8, LANES))
    return kind == 0, kind == 1, kind == 2


def prepare_kernel(
    owner_ref, regime_ref, state_ref, mom_ref, weight_ref,
    tile_ref, hot_ref, part_ref, mom_tile_ref, weight_part_ref,
    weight_own, sem, mom_sem, weight_sem,
):
    copies = [
        pltpu.make_async_copy(
            state_ref.at[:, pl.ds(h * LANES, LANES)], tile_ref.at[h], sem.at[h]
        )
        for h in range(COL // LANES)
    ]
    weights = pltpu.make_async_copy(weight_ref, weight_own, weight_sem)
    moments = [
        pltpu.make_async_copy(
            mom_ref.at[:, pl.ds(p * LANES, LANES)], mom_tile_ref.at[p], mom_sem.at[p]
        )
        for p in range(CAP)
    ]
    for copy in copies + [weights] + moments:
        copy.start()
    owner_row = owner_ref[...]
    owner_down = columns_down(owner_row)
    owner_real = owner_row.astype(f32)
    before = jnp.zeros((1, COL), f32)
    for h in range(COL // LANES):
        same = (
            jnp.concatenate([owner_down[h * LANES : (h + 1) * LANES, :]] * 2, axis=1) == owner_real
        )
        earlier = iota((LANES, COL), 0) + h * LANES < iota((LANES, COL), 1)
        before = before + jnp.sum((same & earlier).astype(f32), axis=0, keepdims=True)
    slot = owner_row + PEERS * before.astype(jnp.int32)
    for p in range(CAP):
        hot_ref[p * PEERS : (p + 1) * PEERS, :] = (
            iota((PEERS, COL), 0) + p * PEERS == slot
        ).astype(bf16)
    top = iota((8, LANES), 0) == 0
    for h in range(COL // LANES):
        copies[h].wait()
        warm, mixed, icy = regimes(regime_ref, h)
        above = [jnp.zeros((8, LANES), f32)] * 2
        for i in range(LEV // 8):
            x = [tile_ref[h, pl.ds(i * 64 + f, 8, stride=FLD), :] for f in range(7)]
            rain_q, x[3], above[0] = rain_fall(x[3], above[0], top)
            kept, source, excess = micro_free(x[:5], rain_q, warm, mixed, icy)
            rain_q, rain, above[1] = rain_fall(kept[3], above[1], top)
            shear = None
            for f in (5, 6):
                if i < LEV // 8 - 1:
                    below = tile_ref[h, pl.ds(i * 64 + FLD + f, 8, stride=FLD), :]
                else:
                    below = pltpu.roll(x[f], 7, 0)
                square = (x[f] - below) * (x[f] - below)
                shear = square if shear is None else shear + square
            shear = 1.5 * shear / (1.0 + shear)
            values = kept[:3] + (rain, kept[4], source, excess, rain_q, shear)
            for f, value in enumerate(values):
                part_ref[h, f, i * 8 : i * 8 + 8, :] = value
    weights.wait()
    for n in range(4):
        down, across = (n % 2) * LANES, (n // 2) * LANES
        for at, part in enumerate(split2(weight_own[n])):
            weight_part_ref[at, down : down + LANES, across : across + LANES] = part
    for copy in moments:
        copy.wait()


def physics_kernel(
    device_ref,
    cols_ref,
    regime_ref,
    got_ref,
    tile_ref,
    hot_ref,
    part_ref,
    weight_ref,
    tend_out,
    out_ref,
    meta_ref,
    tend_ref,
    block_ref,
    mom_ref,
    a_ref,
    y_ref,
    g_ref,
    k_ref,
    c_ref,
    e_ref,
    tend_sem,
):
    for t in range(ROWS1):
        block_ref[t * LANES : (t + 1) * LANES, :] = got_ref[pl.ds(t, PEERS, stride=ROWS1), :].T
    device = device_ref[0]
    mine = device % GROUP
    picked = block_ref[META : META + 1, :]
    for n in range(1, 4):
        picked = jnp.where(mine == n, block_ref[META + n : META + n + 1, :], picked)
    meta_ref[0:1, :] = picked
    group = device - mine
    member = iota((16, PEERS), 0) // 4
    first_row = jnp.zeros((16, PEERS), f32)
    for flip in range(GROUP):
        partner = group + mine + flip - 2 * (mine & flip)
        first_row = jnp.where(member == flip, (partner * 4).astype(f32), first_row)
    meta_ref[8:24, :] = first_row + (iota((16, PEERS), 0) % 4).astype(f32)
    meta_ref[4:8, :] = block_ref[META + 4 : META + 8, :]
    slotted = jnp.concatenate(
        [block_ref[p * DOWN * LEV : (p + 1) * DOWN * LEV, :] for p in range(CAP)], axis=1
    )
    total = None
    for part in split2(slotted):
        got = jnp.dot(part, hot_ref[...], preferred_element_type=f32)
        total = got if total is None else total + got
    mom_ref[0 : DOWN * LEV, :] = total

    top = iota((8, LANES), 0) == 0
    for h in range(COL // LANES):
        lanes = slice(h * LANES, (h + 1) * LANES)
        warm, mixed, icy = regimes(regime_ref, h)
        base = h * PAD_ROWS
        for i in range(LEV // 8):
            m2 = mom_ref[LEV + i * 8 : LEV + i * 8 + 8, lanes]
            first = tuple(part_ref[h, f, i * 8 : i * 8 + 8, :] for f in range(8))
            x = micro_bound(first[:5], first[5], first[6], m2, icy)
            kept, source, excess = micro_free(x, first[7], warm, mixed, icy)
            x = micro_bound(kept, source, excess, m2, icy)
            for f, value in enumerate(x):
                a_ref[pl.ds(base + i * 8 * PITCH + f, 8, stride=PITCH), :] = value
            for f in range(5, FLD):
                a_ref[pl.ds(base + i * 8 * PITCH + f, 8, stride=PITCH), :] = tile_ref[
                    h, pl.ds(i * 64 + f, 8, stride=FLD), :
                ]
        for ref in (a_ref, y_ref):
            ref[base + LEV * PITCH : base + LEV * PITCH + FLD, :] = jnp.zeros((FLD, LANES), f32)
    last = iota((8, COL), 0) == 7
    for i in range(LEV // 8):
        m0 = mom_ref[i * 8 : i * 8 + 8, :]
        m0_next = mom_ref[i * 8 + 1 : i * 8 + 9, :]
        energy = 30.5 + 30.0 * jnp.tanh(m0 + m0_next)
        if i == LEV // 8 - 1:
            energy = jnp.where(last, 0.0, energy)
        e_ref[i * 8 : i * 8 + 8, :] = energy
    for turn in range(3):
        src = a_ref if turn == 0 else y_ref
        for h in range(COL // LANES):
            lanes = slice(h * LANES, (h + 1) * LANES)
            above = jnp.zeros((8, LANES), f32)
            for i in range(LEV // 8):

                def drop(f):
                    first = h * PAD_ROWS + i * 8 * PITCH + f
                    return (
                        src[pl.ds(first, 8, stride=PITCH), :]
                        - src[pl.ds(first + PITCH, 8, stride=PITCH), :]
                    )

                if turn == 0:
                    shear = part_ref[h, 8, i * 8 : i * 8 + 8, :]
                else:
                    du, dv = drop(5), drop(6)
                    shear = du * du + dv * dv
                    shear = 1.5 * shear / (1.0 + shear)
                mixing = 0.3 + shear * (0.5 - 0.5 * jnp.tanh(drop(0)))
                kappa = mixing * e_ref[i * 8 : i * 8 + 8, lanes]
                rolled = pltpu.roll(kappa, 1, 0)
                k_ref[i * 8 : i * 8 + 8, lanes] = kappa
                c_ref[i * 8 : i * 8 + 8, lanes] = 1.0 + kappa + jnp.where(top, above, rolled)
                above = rolled
        solve(a_ref, k_ref, c_ref, y_ref, g_ref)

    field = iota((FLD, LANES), 0)
    kept = (field >= 2) & (field <= 4)
    copies = []
    for h in range(COL // LANES):
        for k in range(LEV):
            rows = slice(k * FLD, (k + 1) * FLD)
            at = slice(h * PAD_ROWS + k * PITCH, h * PAD_ROWS + k * PITCH + FLD)
            mixed_state = jnp.where(kept, a_ref[at, :], y_ref[at, :])
            tend_ref[h, rows, :] = mixed_state - tile_ref[h, rows, :]
        copies.append(
            pltpu.make_async_copy(
                tend_ref.at[h], tend_out.at[:, pl.ds(h * LANES, LANES)], tend_sem.at[h]
            )
        )
        copies[-1].start()

    fields = jnp.concatenate(
        [
            jnp.concatenate(
                [y_ref[pl.ds(h * PAD_ROWS + f, LEV, stride=PITCH), :] for f in (0, 1, 5, 6)], axis=0
            )
            for h in range(COL // LANES)
        ],
        axis=1,
    )
    parts = split2(fields)
    sent = 0
    for pair in range(CAP // 2):
        hot = hot_ref[pair * 2 * PEERS : (pair + 1) * 2 * PEERS, :]
        total = None
        for part in parts:
            got = lax.dot_general(
                part, hot, (((1,), (1,)), ((), ())), preferred_element_type=f32
            )
            total = got if total is None else total + got
        for q in range(2):
            first = (pair * 2 + q) * UP * LEV
            block_ref[first : first + UP * LEV, :] = total[:, q * PEERS : (q + 1) * PEERS]
        ready = (pair + 1) * 2 * UP * LEV // LANES
        for t in range(sent, ready):
            out_ref[pl.ds(t, PEERS, stride=ROWS2), :] = block_ref[
                t * LANES : (t + 1) * LANES, :
            ].T
        sent = ready
    bottom = []
    for h in range(COL // LANES):
        level = slice((LEV - 1) * FLD, LEV * FLD)
        first = h * PAD_ROWS + (LEV - 1) * PITCH
        at = slice(first, first + FLD)
        old = tile_ref[h, level, :]
        bottom.append(old + (jnp.where(kept, a_ref[at, :], y_ref[at, :]) - old))
    b = jnp.concatenate(bottom, axis=1)
    b0, b3, b5, b6 = (b[f : f + 1, :] for f in (0, 3, 5, 6))
    wind = jnp.sqrt(1.0 + b5 * b5 + b6 * b6)
    flux = jnp.concatenate(
        [
            -0.5 * wind * b5,
            -0.5 * wind * b6,
            0.5 * softplus(b3),
            -0.3 * wind * b0,
            jnp.zeros((4, COL), f32),
        ],
        axis=0,
    )
    none = jnp.zeros((FLD, LANES), f32)
    used = []
    for n in range(4):
        mine = jnp.where(cols_ref[n] == 0, flux[:, :LANES], flux[:, LANES:])
        used.append(jnp.concatenate([none, mine] if n % 2 else [mine, none], axis=1))
    hi, low = split2(jnp.concatenate(used, axis=0))

    def weighted(parts, at):
        got = jnp.dot(
            jnp.concatenate(parts, axis=0), weight_ref[at], preferred_element_type=f32
        )
        total = got[0:32, :]
        for i in range(1, len(parts)):
            total = total + got[i * 32 : i * 32 + 32, :]
        return total

    products = weighted([hi], 1) + weighted([hi, low], 0)
    which = iota((PEERS, LANES), 0) % GROUP
    for e in range(4):
        value = jnp.broadcast_to(products[e : e + 1, 0:LANES], (PEERS, LANES))
        for n in range(1, 4):
            across = (n // 2) * LANES
            other = products[n * 8 + e : n * 8 + e + 1, across : across + LANES]
            value = jnp.where(which == n, other, value)
        out_ref[pl.ds(ROWS_UP + e, PEERS, stride=ROWS2), :] = value
    for copy in copies:
        copy.wait()


def ocean_kernel(meta_ref, got_ref, *sum_refs):
    chosen = (meta_ref[0:1, :] == meta_ref[8:24, :]).astype(bf16)
    values = jnp.concatenate(
        [got_ref[pl.ds(ROWS_UP + e, PEERS, stride=ROWS2), :] for e in range(4)], axis=1
    )
    total = None
    for part in split2(values):
        got = jnp.dot(chosen, part, preferred_element_type=f32)
        total = got if total is None else total + got
    for e in range(4):
        for flip in range(GROUP):
            sum_refs[flip][:, e, :] = total[
                flip * 4 : flip * 4 + 4, e * LANES : (e + 1) * LANES
            ]


def update_kernel(meta_ref, got_ref, tile_ref, out_ref, block_ref, new_ref, sem):
    count = meta_ref[4:5, :]
    unpacked = 0
    top = iota((8, LANES), 0) == 0
    last = iota((8, LANES), 0) == 7
    copies = []
    for p in range(CAP):
        needed = -(-(p + 1) * UP * LEV // LANES)
        for t in range(unpacked, needed):
            block_ref[8 + t * LANES : 8 + (t + 1) * LANES, :] = got_ref[
                pl.ds(t, PEERS, stride=ROWS2), :
            ].T
        unpacked = needed
        live = jnp.broadcast_to(count, (8, LANES)) > p + 0.5
        for i in range(LEV // 8):

            def grad(which):
                first = 8 + (p * UP + which) * LEV + i * 8
                prev = block_ref[first - 1 : first + 7, :]
                after = block_ref[first + 1 : first + 9, :]
                if i == 0:
                    prev = jnp.where(top, block_ref[first : first + 8, :], prev)
                if i == LEV // 8 - 1:
                    after = jnp.where(last, block_ref[first : first + 8, :], after)
                return prev - after

            gt, gq, gu, gv = (grad(which) for which in range(UP))
            production = (
                gu * gu + gv * gv, gt * gt, gq * gq, gt * gq, gu * gt, gv * gt, gu * gq, gu * gv,
            )
            for j in range(FLD):
                at = pl.ds(i * 64 + j, 8, stride=FLD)
                m = tile_ref[p, at, :]
                new = (0.85 - 0.05 * j) * m + 0.5 * jnp.tanh(production[j])
                new_ref[p, at, :] = jnp.where(live, new, m)
        copies.append(
            pltpu.make_async_copy(
                new_ref.at[p], out_ref.at[:, pl.ds(p * LANES, LANES)], sem.at[p]
            )
        )
        copies[-1].start()
    for copy in copies:
        copy.wait()


SMEM = pl.BlockSpec(memory_space=pltpu.SMEM)
VMEM = pl.BlockSpec(memory_space=pltpu.VMEM)
ANY = pl.BlockSpec(memory_space=pl.ANY)
HBM = pl.BlockSpec(memory_space=pltpu.HBM)
PLANE = LEV * FLD
VMEM_LIMIT = 16 << 20


def here(shape, dtype=f32):
    return pltpu.VMEM(shape, dtype)


def far(shape):
    return jax.ShapeDtypeStruct(shape, f32)


def hold(x):
    return pltpu.with_memory_space_constraint(x, pltpu.VMEM)


def outside(x):
    return pltpu.with_memory_space_constraint(x, pltpu.HBM)


def call(kernel, ins, outs, out_specs, scratch):
    return pl.pallas_call(
        kernel,
        in_specs=ins,
        out_specs=out_specs,
        out_shape=outs,
        scratch_shapes=scratch,
        compiler_params=pltpu.CompilerParams(vmem_limit_bytes=VMEM_LIMIT),
    )


def pack(rows, owner_row, mom):
    return call(
        pack_kernel,
        [HBM] * 3,
        [far((PEERS, 1, ROWS1 * LANES))],
        [ANY],
        [
            pltpu.SMEM((4,), jnp.int32),
            pltpu.VMEM((1, COL), jnp.int32),
            pltpu.VMEM((ROWS1 * LANES, LANES), f32),
            pltpu.VMEM((ROWS1, PEERS, LANES), f32),
            pltpu.SemaphoreType.DMA((CAP, DOWN)),
            pltpu.SemaphoreType.DMA((2,)),
            pltpu.SemaphoreType.DMA((ROWS1,)),
        ],
    )(outside(rows), outside(owner_row), outside(mom))[0]


def prepare(owner_row, regime_row, state, mom, weights):
    return call(
        prepare_kernel,
        [VMEM] * 2 + [HBM] * 3,
        [
            here((2, PLANE, LANES)),
            here((SLOTS, COL), bf16),
            here((2, PARTS, LEV, LANES)),
            here((CAP, PLANE, LANES)),
            here((2, 2 * LANES, 2 * LANES), bf16),
        ],
        [VMEM] * 5,
        [
            pltpu.VMEM((4, LANES, LANES), f32),
            pltpu.SemaphoreType.DMA((2,)),
            pltpu.SemaphoreType.DMA((CAP,)),
            pltpu.SemaphoreType.DMA,
        ],
    )(owner_row, regime_row, outside(state), outside(mom), outside(weights))


def physics(device, cols, regime_row, got, tiles, hot, parts, weights):
    return call(
        physics_kernel,
        [SMEM] * 2 + [VMEM] * 6,
        [far((PLANE, COL)), here((ROWS2 * PEERS, LANES)), here((24, PEERS))],
        [ANY, VMEM, VMEM],
        [
            pltpu.VMEM((2, PLANE, LANES), f32),
            pltpu.VMEM((ROWS_UP * LANES, LANES), f32),
            pltpu.VMEM((DOWN * LEV + 8, COL), f32),
            pltpu.VMEM((2 * PAD_ROWS, LANES), f32),
            pltpu.VMEM((2 * PAD_ROWS, LANES), f32),
            pltpu.VMEM((2 * PAD_ROWS, LANES), f32),
            pltpu.VMEM((LEV, COL), f32),
            pltpu.VMEM((LEV, COL), f32),
            pltpu.VMEM((LEV, COL), f32),
            pltpu.SemaphoreType.DMA((2,)),
        ],
    )(device, cols, regime_row, *(hold(x) for x in (got, tiles, hot, parts, weights)))


def ocean(meta, back):
    return call(
        ocean_kernel, [VMEM, VMEM], [here((4, 4, LANES))] * GROUP, [VMEM] * GROUP, []
    )(hold(meta), hold(back))


def update(meta, back, tiles):
    return call(
        update_kernel,
        [VMEM] * 3,
        [far((PLANE, SLOTS))],
        [ANY],
        [
            pltpu.VMEM((ROWS_UP * LANES + 16, LANES), f32),
            pltpu.VMEM((CAP, PLANE, LANES), f32),
            pltpu.SemaphoreType.DMA((CAP,)),
        ],
    )(hold(meta), hold(back), hold(tiles))[0]


def exchange(sent, rows):
    got = lax.all_to_all(
        sent.reshape(PEERS, 1, rows * LANES), ("node", "dev"), 0, 0, tiled=True
    )
    return got.reshape(PEERS * rows, LANES)


def local(state, span_owner, regime, moments, remap_weights, remap_rows, remap_cols):
    dev_count = lax.axis_size("dev")
    device = lax.axis_index(("node", "dev")).astype(jnp.int32).reshape(1)
    owner_row = span_owner.reshape(1, COL)
    regime_row = regime.reshape(1, COL)
    sent = pack(remap_rows, owner_row, moments)
    tiles, hot, parts, mom_tiles, weights = prepare(
        owner_row,
        regime_row,
        state.reshape(PLANE, COL),
        moments.reshape(PLANE, SLOTS),
        remap_weights,
    )
    got = exchange(sent, ROWS1)
    tend, sent, meta = physics(device, remap_cols, regime_row, got, tiles, hot, parts, weights)
    back = exchange(sent, ROWS2)
    sums = ocean(meta, back)
    others = []
    for flip in (2, 3, 1):
        others.append(lax.ppermute(sums[flip], "dev", [(i, i ^ flip) for i in range(dev_count)]))
    new_mom = update(meta, back, mom_tiles)
    flux = sums[0] + others[2] + others[0] + others[1]
    return tend.reshape(LEV, FLD, COL), new_mom.reshape(LEV, FLD, SLOTS), flux


def solution(mesh):
    return jax.shard_map(
        local,
        mesh=mesh,
        in_specs=(
            P(None, None, ("node", "dev")),
            P(("node", "dev"), None),
            P(("node", "dev")),
            P(None, None, ("node", "dev")),
            P(("node", "dev"), None, None),
            P(("node", "dev")),
            P(("node", "dev")),
        ),
        out_specs=(
            P(None, None, ("node", "dev")),
            P(None, None, ("node", "dev")),
            P(("node", "dev"), None, None),
        ),
        check_vma=False,
    )
```

```python
import jax
import jax.numpy as jnp
from jax import lax
from jax.experimental import pallas as pl
from jax.experimental.pallas import tpu as pltpu
from jax.sharding import PartitionSpec as P


LEV = 72
FLD = 8
PEERS = 128
LANES = 128
CAP = 4
COL = 256
SLOTS = CAP * PEERS
DOWN = 2
UP = 4
ROWS1 = 5
META = CAP * DOWN * LEV
ROWS_UP = CAP * UP * LEV // LANES
OCN_ROWS = 4
GROUP = 4
ROWS2 = ROWS_UP + OCN_ROWS
HALF = LEV // 2
PITCH = 9
PAD_ROWS = 664
PARTS = 9
f32 = jnp.float32
bf16 = jnp.bfloat16


def iota(shape, axis):
    return lax.broadcasted_iota(jnp.int32, shape, axis)


def split2(x):
    hi = x.astype(bf16)
    return hi, (x - hi.astype(f32)).astype(bf16)


def columns_down(owner_row):
    real = owner_row.astype(f32)
    parts = [
        jnp.broadcast_to(real[:, h * LANES : (h + 1) * LANES], (LANES, LANES)).T
        for h in range(COL // LANES)
    ]
    return jnp.concatenate(parts, axis=0)


def pack_kernel(
    rows_hbm, owner_hbm, mom_ref, out_ref, rows_ref, owner_ref, block_ref, sem, small_sem
):
    small = [
        pltpu.make_async_copy(owner_hbm, owner_ref, small_sem.at[0]),
        pltpu.make_async_copy(rows_hbm, rows_ref, small_sem.at[1]),
    ]
    copies = []
    for p in range(CAP):
        for at, moment in enumerate((0, 2)):
            copies.append(
                pltpu.make_async_copy(
                    mom_ref.at[:, moment, pl.ds(p * LANES, LANES)],
                    block_ref.at[pl.ds((p * DOWN + at) * LEV, LEV), :],
                    sem.at[p, at],
                )
            )
    for copy in small + copies:
        copy.start()
    for copy in small:
        copy.wait()
    owner_down = columns_down(owner_ref[...])
    peer = iota((COL, LANES), 1).astype(f32)
    count = jnp.sum((owner_down == peer).astype(f32), axis=0, keepdims=True)
    tail = ROWS1 * LANES - META
    which = iota((tail, LANES), 0)
    meta = jnp.where(which == 4, jnp.broadcast_to(count, (tail, LANES)), 0.0)
    for n in range(4):
        meta = jnp.where(which == n, rows_ref[n].astype(f32), meta)
    block_ref[META:, :] = meta
    for copy in copies:
        copy.wait()
    for t in range(ROWS1):
        out_ref[pl.ds(t, PEERS, stride=ROWS1), :] = block_ref[t * LANES : (t + 1) * LANES, :].T


def softplus(x):
    return jnp.maximum(x, 0.0) + jnp.log(1.0 + jnp.exp(-jnp.abs(x)))


def rain_fall(rain, above, top):
    rain_q = softplus(rain)
    falling = 0.5 * rain_q
    rolled = pltpu.roll(falling, 1, 0)
    return rain_q, rain + 0.5 * (jnp.where(top, above, rolled) - falling), rolled


def micro_free(x, rain_q, warm, mixed, icy):
    temper, vap, liq, rain, ice = x
    vapour = softplus(vap)
    liquid = softplus(liq)
    ice_q = softplus(ice)
    half_t = jnp.tanh(0.5 * temper)
    satur = 0.6 * jnp.exp(0.5 * half_t)
    excess = vapour - satur
    autoconv = 0.3 * liquid * liquid / (1.0 + liquid)
    evapor = 0.05 * rain_q * (1.0 - jnp.tanh(0.5 * excess))
    freeze = 0.15 * liquid * (1.0 - half_t)
    melting = 0.1 * ice_q * (1.0 + half_t)
    aggreg = 0.25 * ice_q * ice_q / (1.0 + ice_q)
    source = jnp.where(
        icy, 0.175 * jnp.tanh(vapour - 0.8 * satur), 0.2 * jnp.tanh(excess)
    )

    def pick(a, b, c):
        return jnp.where(warm, a, jnp.where(mixed, b, c))

    swap = freeze - melting
    kept = (
        temper + pick(-0.4 * evapor, 0.25 * swap, 0.25 * freeze),
        jnp.where(warm, vap + 0.5 * evapor, vap),
        liq - 0.5 * pick(autoconv, freeze + autoconv, freeze),
        rain + 0.5 * pick(autoconv - evapor, autoconv + melting, aggreg),
        jnp.where(warm, ice, ice + 0.5 * jnp.where(mixed, swap, freeze - aggreg)),
    )
    return kept, source, excess


def micro_bound(kept, source, excess, m2, icy):
    temper, vap, liq, rain, ice = kept
    gain = source * (1.0 + 0.5 * jnp.tanh(0.5 * (m2 + excess)))
    return (
        temper + jnp.where(icy, gain, 0.8 * gain),
        vap - gain,
        jnp.where(icy, liq, liq + gain),
        rain,
        jnp.where(icy, ice + gain, ice),
    )


def solve(a_ref, k_ref, c_ref, y_ref, g_ref):
    halves = range(COL // LANES)

    def row(ref, h, level):
        one = ref[level : level + 1, h * LANES : (h + 1) * LANES]
        return jnp.broadcast_to(one, (FLD, LANES))

    def rows(h, level):
        first = h * PAD_ROWS + level * PITCH
        return slice(first, first + FLD)

    def base(h, chain, step):
        return row(c_ref, h, LEV - 1 - step if chain else step)

    def link(h, chain, step):
        return row(k_ref, h, LEV - 1 - step if chain else step - 1)

    def finish(h, chain, step, r):
        k = LEV - 1 - step if chain else step
        d = a_ref[rows(h, k), :]
        if step > 0:
            d = d + link(h, chain, step) * last_d[h, chain]
        d = d * r
        g = row(k_ref, h, k - 1 if chain else k) * r
        g_ref[rows(h, k), :] = g
        y_ref[rows(h, k), :] = d
        last_d[h, chain] = d
        last_g[h, chain] = g

    chains = [(h, chain) for h in halves for chain in range(2)]
    den, last_d, last_g = {}, {}, {}
    for at in chains:
        den[at] = base(*at, 0)
        finish(*at, 0, 1.0 / den[at])
    for step in range(1, HALF, 2):
        for at in chains:
            old = den[at]
            k = link(*at, step)
            r = 1.0 / (base(*at, step) * old - k * k)
            if step + 1 < HALF:
                k = link(*at, step + 1)
                den[at] = base(*at, step + 1) - (k * k * old) * r
            finish(*at, step, old * r)
            if step + 1 < HALF:
                finish(*at, step + 1, 1.0 / den[at])
    z = {}
    for h in halves:
        d_up, d_dn = last_d[h, 0], last_d[h, 1]
        g_up, g_dn = last_g[h, 0], last_g[h, 1]
        z[h, 0] = (d_up + g_up * d_dn) / (1.0 - g_up * g_dn)
        z[h, 1] = d_dn + g_dn * z[h, 0]
        y_ref[rows(h, HALF - 1), :] = z[h, 0]
        y_ref[rows(h, HALF), :] = z[h, 1]
    for step in range(1, HALF):
        for h in halves:
            for chain in range(2):
                k = HALF + step if chain else HALF - 1 - step
                z[h, chain] = y_ref[rows(h, k), :] + g_ref[rows(h, k), :] * z[h, chain]
                y_ref[rows(h, k), :] = z[h, chain]


def regimes(regime_ref, h):
    kind = jnp.broadcast_to(regime_ref[:, h * LANES : (h + 1) * LANES], (8, LANES))
    return kind == 0, kind == 1, kind == 2


def prepare_kernel(
    owner_ref, regime_ref, state_ref, mom_ref, weight_ref,
    tile_ref, hot_ref, part_ref, mom_tile_ref, weight_part_ref,
    weight_own, sem, mom_sem, weight_sem,
):
    copies = [
        pltpu.make_async_copy(
            state_ref.at[:, pl.ds(h * LANES, LANES)], tile_ref.at[h], sem.at[h]
        )
        for h in range(COL // LANES)
    ]
    weights = pltpu.make_async_copy(weight_ref, weight_own, weight_sem)
    moments = [
        pltpu.make_async_copy(
            mom_ref.at[:, pl.ds(p * LANES, LANES)], mom_tile_ref.at[p], mom_sem.at[p]
        )
        for p in range(CAP)
    ]
    for copy in copies + [weights] + moments:
        copy.start()
    owner_row = owner_ref[...]
    owner_down = columns_down(owner_row)
    owner_real = owner_row.astype(f32)
    before = jnp.zeros((1, COL), f32)
    for h in range(COL // LANES):
        same = (
            jnp.concatenate([owner_down[h * LANES : (h + 1) * LANES, :]] * 2, axis=1) == owner_real
        )
        earlier = iota((LANES, COL), 0) + h * LANES < iota((LANES, COL), 1)
        before = before + jnp.sum((same & earlier).astype(f32), axis=0, keepdims=True)
    slot = owner_row + PEERS * before.astype(jnp.int32)
    for p in range(CAP):
        hot_ref[p * PEERS : (p + 1) * PEERS, :] = (
            iota((PEERS, COL), 0) + p * PEERS == slot
        ).astype(bf16)
    top = iota((8, LANES), 0) == 0
    for h in range(COL // LANES):
        copies[h].wait()
        warm, mixed, icy = regimes(regime_ref, h)
        above = [jnp.zeros((8, LANES), f32)] * 2
        for i in range(LEV // 8):
            x = [tile_ref[h, pl.ds(i * 64 + f, 8, stride=FLD), :] for f in range(7)]
            rain_q, x[3], above[0] = rain_fall(x[3], above[0], top)
            kept, source, excess = micro_free(x[:5], rain_q, warm, mixed, icy)
            rain_q, rain, above[1] = rain_fall(kept[3], above[1], top)
            shear = None
            for f in (5, 6):
                if i < LEV // 8 - 1:
                    below = tile_ref[h, pl.ds(i * 64 + FLD + f, 8, stride=FLD), :]
                else:
                    below = pltpu.roll(x[f], 7, 0)
                square = (x[f] - below) * (x[f] - below)
                shear = square if shear is None else shear + square
            shear = 0.75 * shear / (1.0 + shear)
            values = kept[:3] + (rain, kept[4], source, excess, rain_q, shear)
            for f, value in enumerate(values):
                part_ref[h, f, i * 8 : i * 8 + 8, :] = value
    weights.wait()
    for n in range(4):
        down, across = (n % 2) * LANES, (n // 2) * LANES
        for at, part in enumerate(split2(weight_own[n])):
            weight_part_ref[at, down : down + LANES, across : across + LANES] = part
    for copy in moments:
        copy.wait()


def physics_kernel(
    device_ref,
    cols_ref,
    regime_ref,
    got_ref,
    tile_ref,
    hot_ref,
    part_ref,
    weight_ref,
    tend_out,
    out_ref,
    meta_ref,
    tend_ref,
    block_ref,
    mom_ref,
    a_ref,
    y_ref,
    g_ref,
    k_ref,
    c_ref,
    e_ref,
    tend_sem,
):
    for t in range(ROWS1):
        block_ref[t * LANES : (t + 1) * LANES, :] = got_ref[pl.ds(t, PEERS, stride=ROWS1), :].T
    device = device_ref[0]
    mine = device % GROUP
    picked = block_ref[META : META + 1, :]
    for n in range(1, 4):
        picked = jnp.where(mine == n, block_ref[META + n : META + n + 1, :], picked)
    meta_ref[0:1, :] = picked
    group = device - mine
    member = iota((16, PEERS), 0) // 4
    first_row = jnp.zeros((16, PEERS), f32)
    for flip in range(GROUP):
        partner = group + mine + flip - 2 * (mine & flip)
        first_row = jnp.where(member == flip, (partner * 4).astype(f32), first_row)
    meta_ref[8:24, :] = first_row + (iota((16, PEERS), 0) % 4).astype(f32)
    meta_ref[4:8, :] = block_ref[META + 4 : META + 8, :]
    slotted = jnp.concatenate(
        [block_ref[p * DOWN * LEV : (p + 1) * DOWN * LEV, :] for p in range(CAP)], axis=1
    )
    total = None
    for part in split2(slotted):
        got = jnp.dot(part, hot_ref[...], preferred_element_type=f32)
        total = got if total is None else total + got
    mom_ref[0 : DOWN * LEV, :] = total

    top = iota((8, LANES), 0) == 0
    for h in range(COL // LANES):
        lanes = slice(h * LANES, (h + 1) * LANES)
        warm, mixed, icy = regimes(regime_ref, h)
        base = h * PAD_ROWS
        for i in range(LEV // 8):
            m2 = mom_ref[LEV + i * 8 : LEV + i * 8 + 8, lanes]
            first = tuple(part_ref[h, f, i * 8 : i * 8 + 8, :] for f in range(8))
            x = micro_bound(first[:5], first[5], first[6], m2, icy)
            kept, source, excess = micro_free(x, first[7], warm, mixed, icy)
            x = micro_bound(kept, source, excess, m2, icy)
            for f, value in enumerate(x):
                a_ref[pl.ds(base + i * 8 * PITCH + f, 8, stride=PITCH), :] = value
            for f in range(5, FLD):
                a_ref[pl.ds(base + i * 8 * PITCH + f, 8, stride=PITCH), :] = tile_ref[
                    h, pl.ds(i * 64 + f, 8, stride=FLD), :
                ]
        for ref in (a_ref, y_ref):
            ref[base + LEV * PITCH : base + LEV * PITCH + FLD, :] = jnp.zeros((FLD, LANES), f32)
    last = iota((8, COL), 0) == 7
    for i in range(LEV // 8):
        m0 = mom_ref[i * 8 : i * 8 + 8, :]
        m0_next = mom_ref[i * 8 + 1 : i * 8 + 9, :]
        energy = 30.5 + 30.0 * jnp.tanh(m0 + m0_next)
        if i == LEV // 8 - 1:
            energy = jnp.where(last, 0.0, energy)
        e_ref[i * 8 : i * 8 + 8, :] = energy
    for turn in range(3):
        src = a_ref if turn == 0 else y_ref
        for h in range(COL // LANES):
            lanes = slice(h * LANES, (h + 1) * LANES)
            above = jnp.zeros((8, LANES), f32)
            for i in range(LEV // 8):

                def drop(f):
                    first = h * PAD_ROWS + i * 8 * PITCH + f
                    return (
                        src[pl.ds(first, 8, stride=PITCH), :]
                        - src[pl.ds(first + PITCH, 8, stride=PITCH), :]
                    )

                if turn == 0:
                    shear = part_ref[h, 8, i * 8 : i * 8 + 8, :]
                else:
                    du, dv = drop(5), drop(6)
                    shear = du * du + dv * dv
                    shear = 0.75 * shear / (1.0 + shear)
                mixing = 0.3 + shear * (1.0 - jnp.tanh(drop(0)))
                kappa = mixing * e_ref[i * 8 : i * 8 + 8, lanes]
                rolled = pltpu.roll(kappa, 1, 0)
                k_ref[i * 8 : i * 8 + 8, lanes] = kappa
                c_ref[i * 8 : i * 8 + 8, lanes] = 1.0 + kappa + jnp.where(top, above, rolled)
                above = rolled
        solve(a_ref, k_ref, c_ref, y_ref, g_ref)

    field = iota((FLD, LANES), 0)
    kept = (field >= 2) & (field <= 4)
    bottom = []
    for h in range(COL // LANES):
        level = slice((LEV - 1) * FLD, LEV * FLD)
        first = h * PAD_ROWS + (LEV - 1) * PITCH
        at = slice(first, first + FLD)
        old = tile_ref[h, level, :]
        bottom.append(old + (jnp.where(kept, a_ref[at, :], y_ref[at, :]) - old))
    b = jnp.concatenate(bottom, axis=1)
    b0, b3, b5, b6 = (b[f : f + 1, :] for f in (0, 3, 5, 6))
    wind = jnp.sqrt(1.0 + b5 * b5 + b6 * b6)
    flux = jnp.concatenate(
        [
            -0.5 * wind * b5,
            -0.5 * wind * b6,
            0.5 * softplus(b3),
            -0.3 * wind * b0,
            jnp.zeros((4, COL), f32),
        ],
        axis=0,
    )
    none = jnp.zeros((FLD, LANES), f32)
    used = []
    for n in range(4):
        mine = jnp.where(cols_ref[n] == 0, flux[:, :LANES], flux[:, LANES:])
        used.append(jnp.concatenate([none, mine] if n % 2 else [mine, none], axis=1))
    hi, low = split2(jnp.concatenate(used, axis=0))

    def weighted(parts, at):
        got = jnp.dot(
            jnp.concatenate(parts, axis=0), weight_ref[at], preferred_element_type=f32
        )
        total = got[0:32, :]
        for i in range(1, len(parts)):
            total = total + got[i * 32 : i * 32 + 32, :]
        return total

    products = weighted([hi], 1) + weighted([hi, low], 0)
    which = iota((PEERS, LANES), 0) % GROUP
    for e in range(4):
        value = jnp.broadcast_to(products[e : e + 1, 0:LANES], (PEERS, LANES))
        for n in range(1, 4):
            across = (n // 2) * LANES
            other = products[n * 8 + e : n * 8 + e + 1, across : across + LANES]
            value = jnp.where(which == n, other, value)
        out_ref[pl.ds(ROWS_UP + e, PEERS, stride=ROWS2), :] = value

    copies = []
    for h in range(COL // LANES):
        for k in range(LEV):
            rows = slice(k * FLD, (k + 1) * FLD)
            at = slice(h * PAD_ROWS + k * PITCH, h * PAD_ROWS + k * PITCH + FLD)
            mixed_state = jnp.where(kept, a_ref[at, :], y_ref[at, :])
            tend_ref[h, rows, :] = mixed_state - tile_ref[h, rows, :]
        copies.append(
            pltpu.make_async_copy(
                tend_ref.at[h], tend_out.at[:, pl.ds(h * LANES, LANES)], tend_sem.at[h]
            )
        )
        copies[-1].start()

    fields = jnp.concatenate(
        [
            jnp.concatenate(
                [y_ref[pl.ds(h * PAD_ROWS + f, LEV, stride=PITCH), :] for f in (0, 1, 5, 6)], axis=0
            )
            for h in range(COL // LANES)
        ],
        axis=1,
    )
    parts = split2(fields)
    sent = 0
    for pair in range(CAP // 2):
        hot = hot_ref[pair * 2 * PEERS : (pair + 1) * 2 * PEERS, :]
        total = None
        for part in parts:
            got = lax.dot_general(
                part, hot, (((1,), (1,)), ((), ())), preferred_element_type=f32
            )
            total = got if total is None else total + got
        for q in range(2):
            first = (pair * 2 + q) * UP * LEV
            block_ref[first : first + UP * LEV, :] = total[:, q * PEERS : (q + 1) * PEERS]
        ready = (pair + 1) * 2 * UP * LEV // LANES
        for t in range(sent, ready):
            out_ref[pl.ds(t, PEERS, stride=ROWS2), :] = block_ref[
                t * LANES : (t + 1) * LANES, :
            ].T
        sent = ready
    for copy in copies:
        copy.wait()


def ocean_kernel(meta_ref, got_ref, *sum_refs):
    chosen = (meta_ref[0:1, :] == meta_ref[8:24, :]).astype(bf16)
    values = jnp.concatenate(
        [got_ref[pl.ds(ROWS_UP + e, PEERS, stride=ROWS2), :] for e in range(4)], axis=1
    )
    total = None
    for part in split2(values):
        got = jnp.dot(chosen, part, preferred_element_type=f32)
        total = got if total is None else total + got
    for e in range(4):
        for flip in range(GROUP):
            sum_refs[flip][:, e, :] = total[
                flip * 4 : flip * 4 + 4, e * LANES : (e + 1) * LANES
            ]


def update_kernel(meta_ref, got_ref, tile_ref, out_ref, block_ref, new_ref, sem):
    count = meta_ref[4:5, :]
    unpacked = 0
    top = iota((8, LANES), 0) == 0
    last = iota((8, LANES), 0) == 7
    copies = []
    for p in range(CAP):
        needed = -(-(p + 1) * UP * LEV // LANES)
        for t in range(unpacked, needed):
            block_ref[8 + t * LANES : 8 + (t + 1) * LANES, :] = got_ref[
                pl.ds(t, PEERS, stride=ROWS2), :
            ].T
        unpacked = needed
        live = jnp.broadcast_to(count, (8, LANES)) > p + 0.5
        for i in range(LEV // 8):

            def grad(which):
                first = 8 + (p * UP + which) * LEV + i * 8
                prev = block_ref[first - 1 : first + 7, :]
                after = block_ref[first + 1 : first + 9, :]
                if i == 0:
                    prev = jnp.where(top, block_ref[first : first + 8, :], prev)
                if i == LEV // 8 - 1:
                    after = jnp.where(last, block_ref[first : first + 8, :], after)
                return prev - after

            gt, gq, gu, gv = (grad(which) for which in range(UP))
            production = (
                gu * gu + gv * gv, gt * gt, gq * gq, gt * gq, gu * gt, gv * gt, gu * gq, gu * gv,
            )
            for j in range(FLD):
                at = pl.ds(i * 64 + j, 8, stride=FLD)
                m = tile_ref[p, at, :]
                new = (0.85 - 0.05 * j) * m + 0.5 * jnp.tanh(production[j])
                new_ref[p, at, :] = jnp.where(live, new, m)
        copies.append(
            pltpu.make_async_copy(
                new_ref.at[p], out_ref.at[:, pl.ds(p * LANES, LANES)], sem.at[p]
            )
        )
        copies[-1].start()
    for copy in copies:
        copy.wait()


SMEM = pl.BlockSpec(memory_space=pltpu.SMEM)
VMEM = pl.BlockSpec(memory_space=pltpu.VMEM)
ANY = pl.BlockSpec(memory_space=pl.ANY)
HBM = pl.BlockSpec(memory_space=pltpu.HBM)
PLANE = LEV * FLD
VMEM_LIMIT = 16 << 20


def here(shape, dtype=f32):
    return pltpu.VMEM(shape, dtype)


def far(shape):
    return jax.ShapeDtypeStruct(shape, f32)


def hold(x):
    return pltpu.with_memory_space_constraint(x, pltpu.VMEM)


def outside(x):
    return pltpu.with_memory_space_constraint(x, pltpu.HBM)


def call(kernel, ins, outs, out_specs, scratch):
    return pl.pallas_call(
        kernel,
        in_specs=ins,
        out_specs=out_specs,
        out_shape=outs,
        scratch_shapes=scratch,
        compiler_params=pltpu.CompilerParams(vmem_limit_bytes=VMEM_LIMIT),
    )


def pack(rows, owner_row, mom):
    return call(
        pack_kernel,
        [HBM] * 3,
        [here((ROWS1 * PEERS, LANES))],
        [VMEM],
        [
            pltpu.SMEM((4,), jnp.int32),
            pltpu.VMEM((1, COL), jnp.int32),
            pltpu.VMEM((ROWS1 * LANES, LANES), f32),
            pltpu.SemaphoreType.DMA((CAP, DOWN)),
            pltpu.SemaphoreType.DMA((2,)),
        ],
    )(outside(rows), outside(owner_row), outside(mom))[0]


def prepare(owner_row, regime_row, state, mom, weights):
    return call(
        prepare_kernel,
        [VMEM] * 2 + [HBM] * 3,
        [
            here((2, PLANE, LANES)),
            here((SLOTS, COL), bf16),
            here((2, PARTS, LEV, LANES)),
            here((CAP, PLANE, LANES)),
            here((2, 2 * LANES, 2 * LANES), bf16),
        ],
        [VMEM] * 5,
        [
            pltpu.VMEM((4, LANES, LANES), f32),
            pltpu.SemaphoreType.DMA((2,)),
            pltpu.SemaphoreType.DMA((CAP,)),
            pltpu.SemaphoreType.DMA,
        ],
    )(owner_row, regime_row, outside(state), outside(mom), outside(weights))


def physics(device, cols, regime_row, got, tiles, hot, parts, weights):
    return call(
        physics_kernel,
        [SMEM] * 2 + [VMEM] * 6,
        [far((PLANE, COL)), here((ROWS2 * PEERS, LANES)), here((24, PEERS))],
        [ANY, VMEM, VMEM],
        [
            pltpu.VMEM((2, PLANE, LANES), f32),
            pltpu.VMEM((ROWS_UP * LANES, LANES), f32),
            pltpu.VMEM((DOWN * LEV + 8, COL), f32),
            pltpu.VMEM((2 * PAD_ROWS, LANES), f32),
            pltpu.VMEM((2 * PAD_ROWS, LANES), f32),
            pltpu.VMEM((2 * PAD_ROWS, LANES), f32),
            pltpu.VMEM((LEV, COL), f32),
            pltpu.VMEM((LEV, COL), f32),
            pltpu.VMEM((LEV, COL), f32),
            pltpu.SemaphoreType.DMA((2,)),
        ],
    )(device, cols, regime_row, *(hold(x) for x in (got, tiles, hot, parts, weights)))


def ocean(meta, back):
    return call(
        ocean_kernel, [VMEM, VMEM], [here((4, 4, LANES))] * GROUP, [VMEM] * GROUP, []
    )(hold(meta), hold(back))


def update(meta, back, tiles):
    return call(
        update_kernel,
        [VMEM] * 3,
        [far((PLANE, SLOTS))],
        [ANY],
        [
            pltpu.VMEM((ROWS_UP * LANES + 16, LANES), f32),
            pltpu.VMEM((CAP, PLANE, LANES), f32),
            pltpu.SemaphoreType.DMA((CAP,)),
        ],
    )(hold(meta), hold(back), hold(tiles))[0]


def exchange(sent, rows):
    got = lax.all_to_all(
        sent.reshape(PEERS, 1, rows * LANES), ("node", "dev"), 0, 0, tiled=True
    )
    return got.reshape(PEERS * rows, LANES)


def local(state, span_owner, regime, moments, remap_weights, remap_rows, remap_cols):
    dev_count = lax.axis_size("dev")
    device = lax.axis_index(("node", "dev")).astype(jnp.int32).reshape(1)
    owner_row = span_owner.reshape(1, COL)
    regime_row = regime.reshape(1, COL)
    sent = pack(remap_rows, owner_row, moments)
    tiles, hot, parts, mom_tiles, weights = prepare(
        owner_row,
        regime_row,
        state.reshape(PLANE, COL),
        moments.reshape(PLANE, SLOTS),
        remap_weights,
    )
    got = exchange(sent, ROWS1)
    tend, sent, meta = physics(device, remap_cols, regime_row, got, tiles, hot, parts, weights)
    back = exchange(sent, ROWS2)
    sums = ocean(meta, back)
    others = []
    for flip in (2, 3, 1):
        others.append(lax.ppermute(sums[flip], "dev", [(i, i ^ flip) for i in range(dev_count)]))
    new_mom = update(meta, back, mom_tiles)
    flux = sums[0] + others[2] + others[0] + others[1]
    return tend.reshape(LEV, FLD, COL), new_mom.reshape(LEV, FLD, SLOTS), flux


def solution(mesh):
    return jax.shard_map(
        local,
        mesh=mesh,
        in_specs=(
            P(None, None, ("node", "dev")),
            P(("node", "dev"), None),
            P(("node", "dev")),
            P(None, None, ("node", "dev")),
            P(("node", "dev"), None, None),
            P(("node", "dev")),
            P(("node", "dev")),
        ),
        out_specs=(
            P(None, None, ("node", "dev")),
            P(None, None, ("node", "dev")),
            P(("node", "dev"), None, None),
        ),
        check_vma=False,
    )
```

```python
import jax
import jax.numpy as jnp
from jax import lax
from jax.experimental import pallas as pl
from jax.experimental.pallas import tpu as pltpu
from jax.sharding import PartitionSpec as P


LEV = 72
FLD = 8
PEERS = 128
LANES = 128
CAP = 4
COL = 256
SLOTS = CAP * PEERS
DOWN = 2
UP = 4
ROWS1 = 5
META = CAP * DOWN * LEV
ROWS_UP = CAP * UP * LEV // LANES
OCN_ROWS = 4
GROUP = 4
ROWS2 = ROWS_UP + OCN_ROWS
HALF = LEV // 2
PITCH = 9
PAD_ROWS = 664
PARTS = 9
f32 = jnp.float32
bf16 = jnp.bfloat16


def iota(shape, axis):
    return lax.broadcasted_iota(jnp.int32, shape, axis)


def split2(x):
    hi = x.astype(bf16)
    return hi, (x - hi.astype(f32)).astype(bf16)


def columns_down(owner_row):
    real = owner_row.astype(f32)
    parts = [
        jnp.broadcast_to(real[:, h * LANES : (h + 1) * LANES], (LANES, LANES)).T
        for h in range(COL // LANES)
    ]
    return jnp.concatenate(parts, axis=0)


def pack_kernel(
    rows_hbm, owner_hbm, mom_ref, out_ref, rows_ref, owner_ref, block_ref, sem, small_sem
):
    small = [
        pltpu.make_async_copy(owner_hbm, owner_ref, small_sem.at[0]),
        pltpu.make_async_copy(rows_hbm, rows_ref, small_sem.at[1]),
    ]
    copies = []
    for p in range(CAP):
        for at, moment in enumerate((0, 2)):
            copies.append(
                pltpu.make_async_copy(
                    mom_ref.at[:, moment, pl.ds(p * LANES, LANES)],
                    block_ref.at[pl.ds((p * DOWN + at) * LEV, LEV), :],
                    sem.at[p, at],
                )
            )
    for copy in copies + small:
        copy.start()
    for copy in small:
        copy.wait()
    owner_down = columns_down(owner_ref[...])
    peer = iota((COL, LANES), 1).astype(f32)
    count = jnp.sum((owner_down == peer).astype(f32), axis=0, keepdims=True)
    tail = ROWS1 * LANES - META
    which = iota((tail, LANES), 0)
    meta = jnp.where(which == 4, jnp.broadcast_to(count, (tail, LANES)), 0.0)
    for n in range(4):
        meta = jnp.where(which == n, rows_ref[n].astype(f32), meta)
    block_ref[META:, :] = meta
    for copy in copies:
        copy.wait()
    for t in range(ROWS1):
        out_ref[pl.ds(t, PEERS, stride=ROWS1), :] = block_ref[t * LANES : (t + 1) * LANES, :].T


def softplus(x):
    return jnp.maximum(x, 0.0) + jnp.log(1.0 + jnp.exp(-jnp.abs(x)))


def rain_fall(rain, above, top):
    rain_q = softplus(rain)
    falling = 0.5 * rain_q
    rolled = pltpu.roll(falling, 1, 0)
    return rain_q, rain + 0.5 * (jnp.where(top, above, rolled) - falling), rolled


def micro_free(x, rain_q, warm, mixed, icy):
    temper, vap, liq, rain, ice = x
    vapour = softplus(vap)
    liquid = softplus(liq)
    ice_q = softplus(ice)
    half_t = jnp.tanh(0.5 * temper)
    satur = 0.6 * jnp.exp(0.5 * half_t)
    excess = vapour - satur
    autoconv = 0.3 * liquid * liquid / (1.0 + liquid)
    evapor = 0.1 * rain_q * (0.5 - 0.5 * jnp.tanh(0.5 * excess))
    freeze = 0.3 * liquid * (0.5 - 0.5 * half_t)
    melting = 0.2 * ice_q * (0.5 + 0.5 * half_t)
    aggreg = 0.25 * ice_q * ice_q / (1.0 + ice_q)
    source = jnp.where(
        icy, 0.175 * jnp.tanh(vapour - 0.8 * satur), 0.2 * jnp.tanh(excess)
    )

    def pick(a, b, c):
        return jnp.where(warm, a, jnp.where(mixed, b, c))

    swap = freeze - melting
    kept = (
        temper + pick(-0.4 * evapor, 0.25 * swap, 0.25 * freeze),
        jnp.where(warm, vap + 0.5 * evapor, vap),
        liq - 0.5 * pick(autoconv, freeze + autoconv, freeze),
        rain + 0.5 * pick(autoconv - evapor, autoconv + melting, aggreg),
        jnp.where(warm, ice, ice + 0.5 * jnp.where(mixed, swap, freeze - aggreg)),
    )
    return kept, source, excess


def micro_bound(kept, source, excess, m2, icy):
    temper, vap, liq, rain, ice = kept
    gain = source * (1.0 + 0.5 * jnp.tanh(0.5 * (m2 + excess)))
    return (
        temper + jnp.where(icy, gain, 0.8 * gain),
        vap - gain,
        jnp.where(icy, liq, liq + gain),
        rain,
        jnp.where(icy, ice + gain, ice),
    )


def solve(a_ref, k_ref, c_ref, y_ref, g_ref):
    halves = range(COL // LANES)

    def row(ref, h, level):
        one = ref[level : level + 1, h * LANES : (h + 1) * LANES]
        return jnp.broadcast_to(one, (FLD, LANES))

    def rows(h, level):
        first = h * PAD_ROWS + level * PITCH
        return slice(first, first + FLD)

    def base(h, chain, step):
        return row(c_ref, h, LEV - 1 - step if chain else step)

    def link(h, chain, step):
        return row(k_ref, h, LEV - 1 - step if chain else step - 1)

    def finish(h, chain, step, r):
        k = LEV - 1 - step if chain else step
        d = a_ref[rows(h, k), :]
        if step > 0:
            d = d + link(h, chain, step) * last_d[h, chain]
        d = d * r
        g = row(k_ref, h, k - 1 if chain else k) * r
        g_ref[rows(h, k), :] = g
        y_ref[rows(h, k), :] = d
        last_d[h, chain] = d
        last_g[h, chain] = g

    chains = [(h, chain) for h in halves for chain in range(2)]
    den, last_d, last_g = {}, {}, {}
    for at in chains:
        den[at] = base(*at, 0)
        finish(*at, 0, 1.0 / den[at])
    for step in range(1, HALF, 2):
        for at in chains:
            old = den[at]
            k = link(*at, step)
            r = 1.0 / (base(*at, step) * old - k * k)
            if step + 1 < HALF:
                k = link(*at, step + 1)
                den[at] = base(*at, step + 1) - (k * k * old) * r
            finish(*at, step, old * r)
            if step + 1 < HALF:
                finish(*at, step + 1, 1.0 / den[at])
    z = {}
    for h in halves:
        d_up, d_dn = last_d[h, 0], last_d[h, 1]
        g_up, g_dn = last_g[h, 0], last_g[h, 1]
        z[h, 0] = (d_up + g_up * d_dn) / (1.0 - g_up * g_dn)
        z[h, 1] = d_dn + g_dn * z[h, 0]
        y_ref[rows(h, HALF - 1), :] = z[h, 0]
        y_ref[rows(h, HALF), :] = z[h, 1]
    for step in range(1, HALF):
        for h in halves:
            for chain in range(2):
                k = HALF + step if chain else HALF - 1 - step
                z[h, chain] = y_ref[rows(h, k), :] + g_ref[rows(h, k), :] * z[h, chain]
                y_ref[rows(h, k), :] = z[h, chain]


def regimes(regime_ref, h):
    kind = jnp.broadcast_to(regime_ref[:, h * LANES : (h + 1) * LANES], (8, LANES))
    return kind == 0, kind == 1, kind == 2


def prepare_kernel(
    owner_ref, regime_ref, state_ref, mom_ref, weight_ref,
    tile_ref, hot_ref, part_ref, mom_tile_ref, weight_part_ref,
    weight_own, sem, mom_sem, weight_sem,
):
    copies = [
        pltpu.make_async_copy(
            state_ref.at[:, pl.ds(h * LANES, LANES)], tile_ref.at[h], sem.at[h]
        )
        for h in range(COL // LANES)
    ]
    weights = pltpu.make_async_copy(weight_ref, weight_own, weight_sem)
    moments = [
        pltpu.make_async_copy(
            mom_ref.at[:, pl.ds(p * LANES, LANES)], mom_tile_ref.at[p], mom_sem.at[p]
        )
        for p in range(CAP)
    ]
    for copy in copies + [weights] + moments:
        copy.start()
    owner_row = owner_ref[...]
    owner_down = columns_down(owner_row)
    owner_real = owner_row.astype(f32)
    before = jnp.zeros((1, COL), f32)
    for h in range(COL // LANES):
        same = (
            jnp.concatenate([owner_down[h * LANES : (h + 1) * LANES, :]] * 2, axis=1) == owner_real
        )
        earlier = iota((LANES, COL), 0) + h * LANES < iota((LANES, COL), 1)
        before = before + jnp.sum((same & earlier).astype(f32), axis=0, keepdims=True)
    slot = owner_row + PEERS * before.astype(jnp.int32)
    for p in range(CAP):
        hot_ref[p * PEERS : (p + 1) * PEERS, :] = (
            iota((PEERS, COL), 0) + p * PEERS == slot
        ).astype(bf16)
    top = iota((8, LANES), 0) == 0
    for h in range(COL // LANES):
        copies[h].wait()
        warm, mixed, icy = regimes(regime_ref, h)
        above = [jnp.zeros((8, LANES), f32)] * 2
        for i in range(LEV // 8):
            x = [tile_ref[h, pl.ds(i * 64 + f, 8, stride=FLD), :] for f in range(7)]
            rain_q, x[3], above[0] = rain_fall(x[3], above[0], top)
            kept, source, excess = micro_free(x[:5], rain_q, warm, mixed, icy)
            rain_q, rain, above[1] = rain_fall(kept[3], above[1], top)
            shear = None
            for f in (5, 6):
                if i < LEV // 8 - 1:
                    below = tile_ref[h, pl.ds(i * 64 + FLD + f, 8, stride=FLD), :]
                else:
                    below = pltpu.roll(x[f], 7, 0)
                square = (x[f] - below) * (x[f] - below)
                shear = square if shear is None else shear + square
            shear = 1.5 * shear / (1.0 + shear)
            values = kept[:3] + (rain, kept[4], source, excess, rain_q, shear)
            for f, value in enumerate(values):
                part_ref[h, f, i * 8 : i * 8 + 8, :] = value
    weights.wait()
    for n in range(4):
        down, across = (n % 2) * LANES, (n // 2) * LANES
        for at, part in enumerate(split2(weight_own[n])):
            weight_part_ref[at, down : down + LANES, across : across + LANES] = part
    for copy in moments:
        copy.wait()


def physics_kernel(
    device_ref,
    cols_ref,
    regime_ref,
    got_ref,
    tile_ref,
    hot_ref,
    part_ref,
    weight_ref,
    tend_out,
    out_ref,
    meta_ref,
    tend_ref,
    block_ref,
    mom_ref,
    a_ref,
    y_ref,
    g_ref,
    k_ref,
    c_ref,
    e_ref,
    tend_sem,
):
    for t in range(ROWS1):
        block_ref[t * LANES : (t + 1) * LANES, :] = got_ref[pl.ds(t, PEERS, stride=ROWS1), :].T
    device = device_ref[0]
    mine = device % GROUP
    picked = block_ref[META : META + 1, :]
    for n in range(1, 4):
        picked = jnp.where(mine == n, block_ref[META + n : META + n + 1, :], picked)
    meta_ref[0:1, :] = picked
    group = device - mine
    member = iota((16, PEERS), 0) // 4
    first_row = jnp.zeros((16, PEERS), f32)
    for flip in range(GROUP):
        partner = group + mine + flip - 2 * (mine & flip)
        first_row = jnp.where(member == flip, (partner * 4).astype(f32), first_row)
    meta_ref[8:24, :] = first_row + (iota((16, PEERS), 0) % 4).astype(f32)
    meta_ref[4:8, :] = block_ref[META + 4 : META + 8, :]
    slotted = jnp.concatenate(
        [block_ref[p * DOWN * LEV : (p + 1) * DOWN * LEV, :] for p in range(CAP)], axis=1
    )
    total = None
    for part in split2(slotted):
        got = jnp.dot(part, hot_ref[...], preferred_element_type=f32)
        total = got if total is None else total + got
    mom_ref[0 : DOWN * LEV, :] = total

    top = iota((8, LANES), 0) == 0
    for h in range(COL // LANES):
        lanes = slice(h * LANES, (h + 1) * LANES)
        warm, mixed, icy = regimes(regime_ref, h)
        base = h * PAD_ROWS
        for i in range(LEV // 8):
            m2 = mom_ref[LEV + i * 8 : LEV + i * 8 + 8, lanes]
            first = tuple(part_ref[h, f, i * 8 : i * 8 + 8, :] for f in range(8))
            x = micro_bound(first[:5], first[5], first[6], m2, icy)
            kept, source, excess = micro_free(x, first[7], warm, mixed, icy)
            x = micro_bound(kept, source, excess, m2, icy)
            for f, value in enumerate(x):
                a_ref[pl.ds(base + i * 8 * PITCH + f, 8, stride=PITCH), :] = value
            for f in range(5, FLD):
                a_ref[pl.ds(base + i * 8 * PITCH + f, 8, stride=PITCH), :] = tile_ref[
                    h, pl.ds(i * 64 + f, 8, stride=FLD), :
                ]
        for ref in (a_ref, y_ref):
            ref[base + LEV * PITCH : base + LEV * PITCH + FLD, :] = jnp.zeros((FLD, LANES), f32)
    last = iota((8, COL), 0) == 7
    for i in range(LEV // 8):
        m0 = mom_ref[i * 8 : i * 8 + 8, :]
        m0_next = mom_ref[i * 8 + 1 : i * 8 + 9, :]
        energy = 30.5 + 30.0 * jnp.tanh(m0 + m0_next)
        if i == LEV // 8 - 1:
            energy = jnp.where(last, 0.0, energy)
        e_ref[i * 8 : i * 8 + 8, :] = energy
    for turn in range(3):
        src = a_ref if turn == 0 else y_ref
        for h in range(COL // LANES):
            lanes = slice(h * LANES, (h + 1) * LANES)
            above = jnp.zeros((8, LANES), f32)
            for i in range(LEV // 8):

                def drop(f):
                    first = h * PAD_ROWS + i * 8 * PITCH + f
                    return (
                        src[pl.ds(first, 8, stride=PITCH), :]
                        - src[pl.ds(first + PITCH, 8, stride=PITCH), :]
                    )

                if turn == 0:
                    shear = part_ref[h, 8, i * 8 : i * 8 + 8, :]
                else:
                    du, dv = drop(5), drop(6)
                    shear = du * du + dv * dv
                    shear = 1.5 * shear / (1.0 + shear)
                mixing = 0.3 + shear * (0.5 - 0.5 * jnp.tanh(drop(0)))
                kappa = mixing * e_ref[i * 8 : i * 8 + 8, lanes]
                rolled = pltpu.roll(kappa, 1, 0)
                k_ref[i * 8 : i * 8 + 8, lanes] = kappa
                c_ref[i * 8 : i * 8 + 8, lanes] = 1.0 + kappa + jnp.where(top, above, rolled)
                above = rolled
        solve(a_ref, k_ref, c_ref, y_ref, g_ref)

    field = iota((FLD, LANES), 0)
    kept = (field >= 2) & (field <= 4)
    bottom = []
    for h in range(COL // LANES):
        level = slice((LEV - 1) * FLD, LEV * FLD)
        first = h * PAD_ROWS + (LEV - 1) * PITCH
        at = slice(first, first + FLD)
        old = tile_ref[h, level, :]
        bottom.append(old + (jnp.where(kept, a_ref[at, :], y_ref[at, :]) - old))
    b = jnp.concatenate(bottom, axis=1)
    b0, b3, b5, b6 = (b[f : f + 1, :] for f in (0, 3, 5, 6))
    wind = jnp.sqrt(1.0 + b5 * b5 + b6 * b6)
    flux = jnp.concatenate(
        [
            -0.5 * wind * b5,
            -0.5 * wind * b6,
            0.5 * softplus(b3),
            -0.3 * wind * b0,
            jnp.zeros((4, COL), f32),
        ],
        axis=0,
    )
    none = jnp.zeros((FLD, LANES), f32)
    used = []
    for n in range(4):
        mine = jnp.where(cols_ref[n] == 0, flux[:, :LANES], flux[:, LANES:])
        used.append(jnp.concatenate([none, mine] if n % 2 else [mine, none], axis=1))
    hi, low = split2(jnp.concatenate(used, axis=0))

    def weighted(parts, at):
        got = jnp.dot(
            jnp.concatenate(parts, axis=0), weight_ref[at], preferred_element_type=f32
        )
        total = got[0:32, :]
        for i in range(1, len(parts)):
            total = total + got[i * 32 : i * 32 + 32, :]
        return total

    products = weighted([hi], 1) + weighted([hi, low], 0)
    which = iota((PEERS, LANES), 0) % GROUP
    for e in range(4):
        value = jnp.broadcast_to(products[e : e + 1, 0:LANES], (PEERS, LANES))
        for n in range(1, 4):
            across = (n // 2) * LANES
            other = products[n * 8 + e : n * 8 + e + 1, across : across + LANES]
            value = jnp.where(which == n, other, value)
        out_ref[pl.ds(ROWS_UP + e, PEERS, stride=ROWS2), :] = value

    copies = []
    for h in range(COL // LANES):
        for k in range(LEV):
            rows = slice(k * FLD, (k + 1) * FLD)
            at = slice(h * PAD_ROWS + k * PITCH, h * PAD_ROWS + k * PITCH + FLD)
            mixed_state = jnp.where(kept, a_ref[at, :], y_ref[at, :])
            tend_ref[h, rows, :] = mixed_state - tile_ref[h, rows, :]
        copies.append(
            pltpu.make_async_copy(
                tend_ref.at[h], tend_out.at[:, pl.ds(h * LANES, LANES)], tend_sem.at[h]
            )
        )
        copies[-1].start()

    fields = jnp.concatenate(
        [
            jnp.concatenate(
                [y_ref[pl.ds(h * PAD_ROWS + f, LEV, stride=PITCH), :] for f in (0, 1, 5, 6)], axis=0
            )
            for h in range(COL // LANES)
        ],
        axis=1,
    )
    parts = split2(fields)
    sent = 0
    for pair in range(CAP // 2):
        hot = hot_ref[pair * 2 * PEERS : (pair + 1) * 2 * PEERS, :]
        total = None
        for part in parts:
            got = lax.dot_general(
                part, hot, (((1,), (1,)), ((), ())), preferred_element_type=f32
            )
            total = got if total is None else total + got
        for q in range(2):
            first = (pair * 2 + q) * UP * LEV
            block_ref[first : first + UP * LEV, :] = total[:, q * PEERS : (q + 1) * PEERS]
        ready = (pair + 1) * 2 * UP * LEV // LANES
        for t in range(sent, ready):
            out_ref[pl.ds(t, PEERS, stride=ROWS2), :] = block_ref[
                t * LANES : (t + 1) * LANES, :
            ].T
        sent = ready
    for copy in copies:
        copy.wait()


def ocean_kernel(meta_ref, got_ref, *sum_refs):
    chosen = (meta_ref[0:1, :] == meta_ref[8:24, :]).astype(bf16)
    values = jnp.concatenate(
        [got_ref[pl.ds(ROWS_UP + e, PEERS, stride=ROWS2), :] for e in range(4)], axis=1
    )
    total = None
    for part in split2(values):
        got = jnp.dot(chosen, part, preferred_element_type=f32)
        total = got if total is None else total + got
    for e in range(4):
        for flip in range(GROUP):
            sum_refs[flip][:, e, :] = total[
                flip * 4 : flip * 4 + 4, e * LANES : (e + 1) * LANES
            ]


def update_kernel(meta_ref, got_ref, tile_ref, out_ref, block_ref, new_ref, sem):
    count = meta_ref[4:5, :]
    unpacked = 0
    top = iota((8, LANES), 0) == 0
    last = iota((8, LANES), 0) == 7
    copies = []
    for p in range(CAP):
        needed = -(-(p + 1) * UP * LEV // LANES)
        for t in range(unpacked, needed):
            block_ref[8 + t * LANES : 8 + (t + 1) * LANES, :] = got_ref[
                pl.ds(t, PEERS, stride=ROWS2), :
            ].T
        unpacked = needed
        live = jnp.broadcast_to(count, (8, LANES)) > p + 0.5
        for i in range(LEV // 8):

            def grad(which):
                first = 8 + (p * UP + which) * LEV + i * 8
                prev = block_ref[first - 1 : first + 7, :]
                after = block_ref[first + 1 : first + 9, :]
                if i == 0:
                    prev = jnp.where(top, block_ref[first : first + 8, :], prev)
                if i == LEV // 8 - 1:
                    after = jnp.where(last, block_ref[first : first + 8, :], after)
                return prev - after

            gt, gq, gu, gv = (grad(which) for which in range(UP))
            production = (
                gu * gu + gv * gv, gt * gt, gq * gq, gt * gq, gu * gt, gv * gt, gu * gq, gu * gv,
            )
            for j in range(FLD):
                at = pl.ds(i * 64 + j, 8, stride=FLD)
                m = tile_ref[p, at, :]
                new = (0.85 - 0.05 * j) * m + 0.5 * jnp.tanh(production[j])
                new_ref[p, at, :] = jnp.where(live, new, m)
        copies.append(
            pltpu.make_async_copy(
                new_ref.at[p], out_ref.at[:, pl.ds(p * LANES, LANES)], sem.at[p]
            )
        )
        copies[-1].start()
    for copy in copies:
        copy.wait()


SMEM = pl.BlockSpec(memory_space=pltpu.SMEM)
VMEM = pl.BlockSpec(memory_space=pltpu.VMEM)
ANY = pl.BlockSpec(memory_space=pl.ANY)
HBM = pl.BlockSpec(memory_space=pltpu.HBM)
PLANE = LEV * FLD
VMEM_LIMIT = 16 << 20


def here(shape, dtype=f32):
    return pltpu.VMEM(shape, dtype)


def far(shape):
    return jax.ShapeDtypeStruct(shape, f32)


def hold(x):
    return pltpu.with_memory_space_constraint(x, pltpu.VMEM)


def outside(x):
    return pltpu.with_memory_space_constraint(x, pltpu.HBM)


def call(kernel, ins, outs, out_specs, scratch):
    return pl.pallas_call(
        kernel,
        in_specs=ins,
        out_specs=out_specs,
        out_shape=outs,
        scratch_shapes=scratch,
        compiler_params=pltpu.CompilerParams(vmem_limit_bytes=VMEM_LIMIT),
    )


def pack(rows, owner_row, mom):
    return call(
        pack_kernel,
        [HBM] * 3,
        [here((ROWS1 * PEERS, LANES))],
        [VMEM],
        [
            pltpu.SMEM((4,), jnp.int32),
            pltpu.VMEM((1, COL), jnp.int32),
            pltpu.VMEM((ROWS1 * LANES, LANES), f32),
            pltpu.SemaphoreType.DMA((CAP, DOWN)),
            pltpu.SemaphoreType.DMA((2,)),
        ],
    )(outside(rows), outside(owner_row), outside(mom))[0]


def prepare(owner_row, regime_row, state, mom, weights):
    return call(
        prepare_kernel,
        [VMEM] * 2 + [HBM] * 3,
        [
            here((2, PLANE, LANES)),
            here((SLOTS, COL), bf16),
            here((2, PARTS, LEV, LANES)),
            here((CAP, PLANE, LANES)),
            here((2, 2 * LANES, 2 * LANES), bf16),
        ],
        [VMEM] * 5,
        [
            pltpu.VMEM((4, LANES, LANES), f32),
            pltpu.SemaphoreType.DMA((2,)),
            pltpu.SemaphoreType.DMA((CAP,)),
            pltpu.SemaphoreType.DMA,
        ],
    )(owner_row, regime_row, outside(state), outside(mom), outside(weights))


def physics(device, cols, regime_row, got, tiles, hot, parts, weights):
    return call(
        physics_kernel,
        [SMEM] * 2 + [VMEM] * 6,
        [far((PLANE, COL)), here((ROWS2 * PEERS, LANES)), here((24, PEERS))],
        [ANY, VMEM, VMEM],
        [
            pltpu.VMEM((2, PLANE, LANES), f32),
            pltpu.VMEM((ROWS_UP * LANES, LANES), f32),
            pltpu.VMEM((DOWN * LEV + 8, COL), f32),
            pltpu.VMEM((2 * PAD_ROWS, LANES), f32),
            pltpu.VMEM((2 * PAD_ROWS, LANES), f32),
            pltpu.VMEM((2 * PAD_ROWS, LANES), f32),
            pltpu.VMEM((LEV, COL), f32),
            pltpu.VMEM((LEV, COL), f32),
            pltpu.VMEM((LEV, COL), f32),
            pltpu.SemaphoreType.DMA((2,)),
        ],
    )(device, cols, regime_row, *(hold(x) for x in (got, tiles, hot, parts, weights)))


def ocean(meta, back):
    return call(
        ocean_kernel, [VMEM, VMEM], [here((4, 4, LANES))] * GROUP, [VMEM] * GROUP, []
    )(hold(meta), hold(back))


def update(meta, back, tiles):
    return call(
        update_kernel,
        [VMEM] * 3,
        [far((PLANE, SLOTS))],
        [ANY],
        [
            pltpu.VMEM((ROWS_UP * LANES + 16, LANES), f32),
            pltpu.VMEM((CAP, PLANE, LANES), f32),
            pltpu.SemaphoreType.DMA((CAP,)),
        ],
    )(hold(meta), hold(back), hold(tiles))[0]


def exchange(sent, rows):
    got = lax.all_to_all(
        sent.reshape(PEERS, 1, rows * LANES), ("node", "dev"), 0, 0, tiled=True
    )
    return got.reshape(PEERS * rows, LANES)


def local(state, span_owner, regime, moments, remap_weights, remap_rows, remap_cols):
    dev_count = lax.axis_size("dev")
    device = lax.axis_index(("node", "dev")).astype(jnp.int32).reshape(1)
    owner_row = span_owner.reshape(1, COL)
    regime_row = regime.reshape(1, COL)
    sent = pack(remap_rows, owner_row, moments)
    tiles, hot, parts, mom_tiles, weights = prepare(
        owner_row,
        regime_row,
        state.reshape(PLANE, COL),
        moments.reshape(PLANE, SLOTS),
        remap_weights,
    )
    got = exchange(sent, ROWS1)
    tend, sent, meta = physics(device, remap_cols, regime_row, got, tiles, hot, parts, weights)
    back = exchange(sent, ROWS2)
    sums = ocean(meta, back)
    others = []
    for flip in (2, 3, 1):
        others.append(lax.ppermute(sums[flip], "dev", [(i, i ^ flip) for i in range(dev_count)]))
    new_mom = update(meta, back, mom_tiles)
    flux = sums[0] + others[2] + others[0] + others[1]
    return tend.reshape(LEV, FLD, COL), new_mom.reshape(LEV, FLD, SLOTS), flux


def solution(mesh):
    return jax.shard_map(
        local,
        mesh=mesh,
        in_specs=(
            P(None, None, ("node", "dev")),
            P(("node", "dev"), None),
            P(("node", "dev")),
            P(None, None, ("node", "dev")),
            P(("node", "dev"), None, None),
            P(("node", "dev")),
            P(("node", "dev")),
        ),
        out_specs=(
            P(None, None, ("node", "dev")),
            P(None, None, ("node", "dev")),
            P(("node", "dev"), None, None),
        ),
        check_vma=False,
    )
```
